256 devices in a mesh: blk: 16 (over x, y_lo, core), grp: 16 (over z, y_hi).
Axes of the slice: x: 4, y: 4 (y_hi: 2, y_lo: 2; y = y_hi * 2 + y_lo), z: 8, core: 2. Of those that a mesh axis runs over, the one named last changes fastest.
Arguments:
- phase_space: float32 [6, 32768], P(None, 'blk'), may hold values from -3.5 to 3.5
- force_rates: float32 [6, 32768], P(None, 'blk'), may hold values from -4 to 4
- irregular: float32 [6, 32768], P(None, 'blk'), may hold values from -3 to 3
- stellar_masses: float32 [32768], P('blk'), may hold values from 9.155274e-06 to 9.1552734e-05
- levels: int32 [256], P('blk'), may hold values from 0 to 3, as said below
- active: int32 [4, 256], P(None, 'blk'), may hold values from 0 to 1, as said below
- partner: int32 [256], P('blk'), may hold values from 0 to 255, as said below
Outputs:
- kinematics: float32 [6, 32768], P(None, 'blk')
- combined_force: float32 [6, 32768], P(None, 'blk')
- irregular_force: float32 [6, 32768], P(None, 'blk')
The draws below stay inside these ranges and needn't reach their ends.
Inputs may be any that keep to these rules, and one draw needn't show every extreme that they name: levels of 0 to 3; in every shard 2 to 4 blocks have level 0, at most 6 level 1 or less and at most 8 level 2 or less, and some shard has exactly 4, 6 and 8. active[n, b] is 1 exactly when n + 1 is a multiple of 2 ** levels[b]. partner is mutual (the partner of partner[b] is b) and has the same place within its shard; the blocks of one shard have exactly 1 partner on each shard, their own shard included, where the one block is its own partner.
All inputs are finite; a program needn't handle non-finite values.
Results may differ from the reference program's by a relative error of at most 0.0003.
Values sent between devices are 32-bit elements; how exact they have to be, the bound alone decides.
No kernel may reach another device: no remote copies, remote signals or barrier semaphores. Data moves between devices by JAX's collectives and lax.ppermute only.
A program may use at most 64 MiB of HBM per device.

```python
import math
import jax
import jax.numpy as jnp
from jax import lax

BS = 128
STEPS = 4
NBS = 16
NBALL = 256
NSTARS = 32768
CAP0 = 4
CAP1 = 6
CAP2 = 8
N_BLK = 16


def level_table(base_key):
    stream = jax.random.split(jax.random.fold_in(base_key, 11), 5)
    shard_ids = jnp.arange(N_BLK)
    level_zero = jax.random.randint(stream[0], (N_BLK,), max(1, CAP0 // 2), CAP0 + 1)
    level_one = level_zero + jax.random.randint(stream[1], (N_BLK,), 0, CAP1 - CAP0 + 1)
    level_two = level_one + jax.random.randint(stream[2], (N_BLK,), 0, CAP2 - CAP1 + 1)
    forced = jax.random.randint(stream[3], (), 0, N_BLK)
    is_forced = shard_ids == forced
    level_zero = jnp.where(is_forced, CAP0, level_zero)
    level_one = jnp.where(is_forced, CAP1, level_one)
    level_two = jnp.where(is_forced, CAP2, level_two)
    ranking = jax.vmap(lambda subkey: jax.random.permutation(subkey, NBS))(jax.random.split(stream[4], N_BLK))
    graded = (ranking >= level_zero[:, None]).astype(jnp.int32)
    graded = graded + (ranking >= level_one[:, None]).astype(jnp.int32)
    graded = graded + (ranking >= level_two[:, None]).astype(jnp.int32)
    return graded.reshape(-1).astype(jnp.int32)


def partner_table(base_key):
    stream = jax.random.split(jax.random.fold_in(base_key, 29), 2)
    layer_mask = jax.random.permutation(stream[0], NBS)
    labels = jax.random.permutation(stream[1], N_BLK)
    inverse_labels = jnp.argsort(labels)
    partner_shard = inverse_labels[jnp.bitwise_xor(labels[:, None], layer_mask[None, :])]
    return (partner_shard * NBS + jnp.arange(NBS)[None, :]).reshape(-1).astype(jnp.int32)


def draw_levels(key, part):
    return level_table(key)


def draw_active(key, part):
    graded = level_table(key)
    periods = jnp.power(2, graded)
    numbers = jnp.arange(STEPS) + 1
    return (numbers[:, None] % periods[None, :] == 0).astype(jnp.int32)


def draw_partner(key, part):
    return partner_table(key)


def draw_phase_space(key, part):
    paired = partner_table(key)
    grouping = jnp.minimum(jnp.arange(NBALL), paired)
    stream = jax.random.split(jax.random.fold_in(key, 41), 4)
    centres = jnp.clip(0.7 * jax.random.normal(stream[0], (3, NBALL)), -2.5, 2.5)
    drifts = jnp.clip(0.3 * jax.random.normal(stream[1], (3, NBALL)), -1.0, 1.0)
    spread = jnp.clip(0.3 * jax.random.normal(stream[2], (3, NSTARS)), -1.0, 1.0)
    stirred = jnp.clip(0.3 * jax.random.normal(stream[3], (3, NSTARS)), -1.0, 1.0)
    position = jnp.repeat(centres[:, grouping], BS, axis=1) + spread
    velocity = jnp.repeat(drifts[:, grouping], BS, axis=1) + stirred
    return jnp.concatenate([position, velocity], axis=0).astype(jnp.float32)


def block_levels(key, extent, pieces, low, top_value):
    level, own = 1.0, jax.random.fold_in(key, 6)
    for dim, blocks in pieces:
        heights = jnp.exp(jax.random.uniform(jax.random.fold_in(own, dim), (blocks,), jnp.float32, low / len(pieces), top_value / len(pieces)))
        level = level * jnp.repeat(heights, extent[dim] // blocks).reshape([-1 if axis == dim else 1 for axis in range(len(extent))])
    return level


def scatter_about(stream_key, extent, scale, most, cuts=(), held_as=jnp.bfloat16):
    result = jax.random.normal(stream_key, extent, jnp.float32) * scale
    if len(cuts) > 0:
        result = block_levels(stream_key, extent, cuts, -0.22, 0.18) * result
    return jnp.clip(result, min=-most, max=most).astype(held_as)


def setup_inputs(seed: int = 0) -> dict:
    key_of = jax.random.split(jax.random.key(seed), 8)
    return {
        "phase_space": draw_phase_space(jax.random.fold_in(key_of[7], 71), 0),
        "force_rates": scatter_about(key_of[1], (6, NSTARS), 1.0, 4.0, ((1, 16),), jnp.float32),
        "irregular": scatter_about(key_of[2], (6, NSTARS), 0.5, 3.0, ((1, 16),), jnp.float32),
        "stellar_masses": jnp.clip(jnp.exp(math.log(9.1552734375e-05) - 2.3025851 * jax.random.uniform(key_of[3], (NSTARS,), jnp.float32) ** block_levels(key_of[3], (NSTARS,), ((0, 16),), -0.2, 0.2)), 9.15527380129788e-06, 9.1552734375e-05),
        "levels": draw_levels(jax.random.fold_in(key_of[7], 71), 0),
        "active": draw_active(jax.random.fold_in(key_of[7], 71), 0),
        "partner": draw_partner(jax.random.fold_in(key_of[7], 71), 0),
    }


soft_wide = 0.04
soft_close = 0.0001
time_tick = 0.125

def pair_terms(targets, sources, soften):
    offset = sources[0:3][..., None, :] - targets[0:3][..., :, None]
    motion = sources[3:6][..., None, :] - targets[3:6][..., :, None]
    distance = lax.optimization_barrier(jnp.sum(offset * offset, axis=0)) + soften
    inverse = lax.rsqrt(distance)
    weight = sources[6][..., None, :] * inverse * inverse * inverse
    radial = lax.optimization_barrier(jnp.sum(offset * motion, axis=0)) / distance
    acceleration = lax.optimization_barrier(jnp.sum(weight * offset, axis=-1))
    jerk_term = lax.optimization_barrier(jnp.sum(weight * (motion - 3.0 * radial * offset), axis=-1))
    return jnp.concatenate([acceleration, jerk_term], axis=0)

def predict_orbits(kinematic, slopes, interval):
    half_square = interval * interval * 0.5
    cube_sixth = interval * interval * interval / 6.0
    position = kinematic[0:3] + kinematic[3:6] * interval + slopes[0:3] * half_square + slopes[3:6] * cube_sixth
    velocity = kinematic[3:6] + slopes[0:3] * interval + slopes[3:6] * half_square
    return jnp.concatenate([position, velocity], axis=0)

def correct(kinematic, slopes, renewed, interval):
    velocity = kinematic[3:6] + (slopes[0:3] + renewed[0:3]) * (interval * 0.5) + (slopes[3:6] - renewed[3:6]) * (interval * interval / 12.0)
    position = kinematic[0:3] + (kinematic[3:6] + velocity) * (interval * 0.5) + (slopes[0:3] - renewed[0:3]) * (interval * interval / 12.0)
    return jnp.concatenate([position, velocity], axis=0)

def write_back(current, renewed, packed_layout, live_flag, block_members):
    layout = current.reshape(current.shape[0], -1, block_members)
    previous = layout[:, packed_layout, :]
    update = jnp.where(live_flag[None, :, None] > 0, renewed, previous)
    return layout.at[:, packed_layout, :].set(update).reshape(current.shape[0], -1)

def regular_sum(incoming_stars, star_registry):
    shards = star_registry.reshape(7, N_BLK, -1).transpose(1, 0, 2)

    def one_block(targets):

        def absorb(running, portion):
            return (running + pair_terms(targets, portion, soft_wide), None)
        return lax.scan(absorb, jnp.zeros_like(targets), shards)[0]
    return lax.map(one_block, incoming_stars.transpose(1, 0, 2)).transpose(1, 0, 2)

def reference(phase_space, force_rates, irregular, stellar_masses, levels, active, partner):
    all_blocks = levels.shape[0]
    block_members = phase_space.shape[1] // all_blocks
    block_list = all_blocks // N_BLK
    limits = [block_list // 4, 3 * block_list // 8, block_list // 2, block_list]
    kinematics, combined_force, irregular_force = (phase_space, force_rates, irregular)
    for moment in range(STEPS):
        number = moment + 1
        capacity = limits[min((number & -number).bit_length() - 1, 3)]
        period = jnp.power(2, levels)
        updated = moment // period * period
        block_interval = (number - updated).astype(jnp.float32) * time_tick
        extrapolated_state = predict_orbits(kinematics, combined_force, jnp.repeat(block_interval, block_members))
        star_registry = jnp.concatenate([extrapolated_state, stellar_masses[None, :]], axis=0)
        catalog_grid = star_registry.reshape(7, all_blocks, block_members)
        live_grid = active[moment].reshape(N_BLK, block_list)
        packed_layout = jnp.argsort(1 - live_grid, axis=1, stable=True)[:, :capacity].astype(jnp.int32)
        packed_layout = (packed_layout + block_list * jnp.arange(N_BLK, dtype=jnp.int32)[:, None]).reshape(-1)
        live_flag = active[moment][packed_layout]
        incoming_stars = catalog_grid[:6, packed_layout, :]
        regular_part = regular_sum(incoming_stars, star_registry)
        partner_block = partner[packed_layout]
        partner_rows = catalog_grid[:, partner_block, :]
        keep_mass = jnp.where((partner_block != packed_layout)[:, None], partner_rows[6], jnp.float32(0.0))
        partner_rows = jnp.concatenate([partner_rows[0:6], keep_mass[None]], axis=0)
        nearby = jnp.concatenate([catalog_grid[:, packed_layout, :], partner_rows], axis=2)
        close_part = pair_terms(incoming_stars, nearby, soft_close) - pair_terms(incoming_stars, nearby, soft_wide)
        combined = regular_part + close_part
        previous_state = kinematics.reshape(6, all_blocks, block_members)[:, packed_layout, :]
        previous_slope = combined_force.reshape(6, all_blocks, block_members)[:, packed_layout, :]
        interval_packed = block_interval[packed_layout][None, :, None]
        renewed = correct(previous_state, previous_slope, combined, interval_packed)
        kinematics = write_back(kinematics, renewed, packed_layout, live_flag, block_members)
        combined_force = write_back(combined_force, combined, packed_layout, live_flag, block_members)
        irregular_force = write_back(irregular_force, close_part, packed_layout, live_flag, block_members)
    return (kinematics, combined_force, irregular_force)
```

```python
import functools
import jax
import jax.numpy as jnp
from jax import lax
from jax.experimental import pallas as pl
from jax.experimental.pallas import tpu as pltpu
from jax.sharding import PartitionSpec as P

WIDE = 0.04
CLOSE = 0.0001
TICK = 0.125
NB = 16
BS = 128
W = NB * BS
F32 = jnp.float32
CAPS = (4, 6, 4, 8)
TOP = (0, 1, 0, 2)
SENT = (-1, 0, 1, 1)
SLOTS = (0, 4, 8, 8)

VMEM = pl.BlockSpec(memory_space=pltpu.VMEM)
SMEM = pl.BlockSpec(memory_space=pltpu.SMEM)


def pair(target, source, mass, soften, acc):
    r = [source[c] - target[c] for c in range(3)]
    w = [source[c] - target[c] for c in range(3, 6)]
    d = (r[0] * r[0] + soften) + r[1] * r[1] + r[2] * r[2]
    s = lax.rsqrt(d)
    s2 = s * s
    weight = (mass * s) * s2
    q = (r[0] * w[0] + r[1] * w[1] + r[2] * w[2]) * (s2 * 3.0)
    acc = list(acc)
    for c in range(3):
        acc[c] = acc[c] + weight * r[c]
        acc[3 + c] = acc[3 + c] + weight * (w[c] - q * r[c])
    return tuple(acc)


def pair_split(target, source, mass, acc):
    r = [source[c] - target[c] for c in range(3)]
    w = [source[c] - target[c] for c in range(3, 6)]
    dd = r[0] * r[0] + r[1] * r[1] + r[2] * r[2]
    rw = (r[0] * w[0] + r[1] * w[1] + r[2] * w[2]) * 3.0
    acc = list(acc)
    for soften, sign in ((CLOSE, 1.0), (WIDE, -1.0)):
        s = lax.rsqrt(dd + soften)
        s2 = s * s
        weight = (mass * s) * (s2 * sign)
        q = rw * s2
        for c in range(3):
            acc[c] = acc[c] + weight * r[c]
            acc[3 + c] = acc[3 + c] + weight * (w[c] - q * r[c])
    return tuple(acc)


def zeros():
    return tuple(jnp.zeros((8, 128), F32) for _ in range(6))


def fill_slots(lev, top, slots):
    for s in range(24):
        slots[0, s] = 0
        slots[1, s] = -1000
        slots[2, s] = 0
    count = jnp.int32(0)
    ones = [jnp.int32(0), jnp.int32(4)]
    for k in range(NB):
        level = lev[k]
        live = level <= top
        place = jnp.where(level == 0, ones[0], jnp.where(level == 1, ones[1], -1000))
        slots[0, count] = k
        slots[1, count] = jnp.where(live, place, -1000)
        slots[2, count] = jnp.where(live, level, 0)
        count = count + live.astype(jnp.int32)
        ones[0] = ones[0] + (level == 0).astype(jnp.int32)
        ones[1] = ones[1] + (level == 1).astype(jnp.int32)
    return count


def span_of(level):
    return jnp.where(level == 0, TICK, jnp.where(level == 1, 2 * TICK, 4 * TICK)).astype(F32)


XS, MS, VS, AS, JS = (0, 1, 2), 3, (4, 5, 6), (8, 9, 10), (12, 13, 14)


def columns(tile):
    return tuple(
        [tile[:, c : c + 1] for c in group] for group in (XS, VS, AS, JS)
    )


def forecast(x, v, a, j, t):
    t2 = t * t * 0.5
    t3 = t * t * t * (1.0 / 6.0)
    xp = [x[c] + v[c] * t + a[c] * t2 + j[c] * t3 for c in range(3)]
    vp = [v[c] + a[c] * t + j[c] * t2 for c in range(3)]
    return xp + vp


def fill_sources(table, predicted, t, sent):
    row = lax.broadcasted_iota(jnp.int32, (8, 128), 0)
    t2 = t * t * 0.5
    t3 = t * t * t / 6.0
    low = row < 3
    high = (row > 3) & (row < 7)
    zero = jnp.zeros((8, 128), F32)
    c1 = jnp.where(low, t, zero)
    c2 = jnp.where(low | high, t2, zero)
    c3 = jnp.where(low, t3, jnp.where(high, t, zero))

    def shard(b, _):
        for k in range(NB):
            at = pl.ds(k * BS, BS)
            first = table[b, 0:8, at]
            second = table[b, 8:16, at]
            other = pltpu.roll(first, 4, 0)
            value = first + c1 * other + c2 * second + c3 * pltpu.roll(second, 4, 0)
            value = jnp.where(row == 7, other, value)
            if sent >= 0:
                value = jnp.where((row == 3) & (other < sent + 0.5), 0.0, value)
            predicted[b, :, at] = value
        return 0

    lax.fori_loop(0, table.shape[0], shard, 0)


def fill_targets(state, slots, cap, targets):
    for s in range(cap):
        x, v, a, j = columns(state[slots[0, s]])
        t = span_of(slots[2, s])
        for c, value in enumerate(forecast(x, v, a, j, t)):
            targets[s, c] = jnp.broadcast_to(value, (8, 128))


def broad(row):
    return jnp.broadcast_to(row, (8, 128))


def table_tile(predicted, b, k):
    at = pl.ds(k * BS, BS)
    rows = [broad(predicted[b, r : r + 1, at]) for r in (0, 1, 2, 4, 5, 6)]
    return rows, broad(predicted[b, 3:4, at])


def sweep_table(predicted, targets, cap, regular):
    shards = predicted.shape[0]

    def two(p, _):
        goal = [[targets[2 * p + e, c] for c in range(6)] for e in range(2)]

        def shard(b, acc):
            for k in range(NB):
                rows, mass = table_tile(predicted, b, k)
                acc = tuple(pair(goal[e], rows, mass, WIDE, acc[e]) for e in range(2))
            return acc

        acc = lax.fori_loop(0, shards, shard, (zeros(), zeros()))
        for e in range(2):
            for c in range(6):
                regular[2 * p + e, c] = acc[e][c]
        return 0

    lax.fori_loop(0, cap // 2, two, 0)


def close_table(predicted, targets, slots, cap, own, levall, partner, sent, irregular):
    for s in range(cap):
        k = slots[0, s]
        q = partner[k] // NB
        goal = [targets[s, c] for c in range(6)]
        acc = zeros()
        for b, wanted in ((own, None), (q, q != own)):
            here = jnp.bool_(True) if wanted is None else wanted
            if sent >= 0:
                level = slots[2, s] if wanted is None else levall[q * NB + k]
                here = here & (level > sent)
            at = pl.ds(pl.multiple_of(k * BS, BS), BS)
            rows = [broad(predicted[b, r : r + 1, at]) for r in (0, 1, 2, 4, 5, 6)]
            mass = broad(predicted[b, 7:8, at]) * jnp.where(here, 1.0, 0.0).astype(F32)
            acc = pair_split(goal, rows, mass, acc)
        for c in range(6):
            irregular[s, c] = acc[c]


def fill_received(got, turned):
    senders, _, lanes = got.shape
    for t in range(lanes // 128):
        for half in range(senders // 128):
            part = got[pl.ds(half * 128, 128), 0, pl.ds(t * 128, 128)]
            turned[pl.ds(t * 16, 16), :, pl.ds(half * 128, 128)] = part.T.reshape(16, 8, 128)


def sweep_received(turned, mass, slots_in, targets, cap, regular):
    halves = turned.shape[2] // 128

    def two(p, _):
        goal = [[targets[2 * p + e, c] for c in range(6)] for e in range(2)]

        def slot(s, acc):
            for i in range(8):
                for half in range(halves):
                    at = pl.ds(half * 128, 128)
                    rows = [broad(turned[f * slots_in + s, i : i + 1, at]) for f in range(6)]
                    m = broad(mass[s, i : i + 1, at])
                    acc = tuple(pair(goal[e], rows, m, WIDE, acc[e]) for e in range(2))
            return acc

        start = tuple(tuple(regular[2 * p + e, c] for c in range(6)) for e in range(2))
        acc = lax.fori_loop(0, slots_in, slot, start)
        for e in range(2):
            for c in range(6):
                regular[2 * p + e, c] = acc[e][c]
        return 0

    lax.fori_loop(0, cap // 2, two, 0)


def close_received(turned, mass, slots_in, targets, slots, cap, own, levall, partner, sent, irregular):
    lane = lax.broadcasted_iota(jnp.int32, (8, 128), 1)
    row = lax.broadcasted_iota(jnp.int32, (8, 128), 0)
    keep = lane // 16 == row
    for s in range(cap):
        k = slots[0, s]
        q = partner[k] // NB
        goal = [targets[s, c] for c in range(6)]
        acc = tuple(irregular[s, c] for c in range(6))
        for b, wanted in ((own, None), (q, q != own)):
            if wanted is None:
                here = slots[2, s] <= sent
                place = slots[1, s]
            else:
                level = levall[q * NB + k]
                here = wanted & (level <= sent)
                place = jnp.where(level == 0, 0, 4)
                for e in range(NB):
                    same = (levall[q * NB + e] == level) & (e < k)
                    place = place + same.astype(jnp.int32)
            place = jnp.clip(jnp.where(here, place, 0), 0, slots_in - 1)
            at = pl.ds(pl.multiple_of((b // 8) * 128, 128), 128)
            shift = lax.rem(128 - lax.rem(b, 8) * 16, 128)

            def gather(tile):
                tile = pltpu.roll(pltpu.roll(tile, shift, 1), 0, 1, stride=16, stride_axis=0)
                return broad(jnp.sum(jnp.where(keep, tile, 0.0), axis=0, keepdims=True))

            rows = [gather(turned[f * slots_in + place, :, at]) for f in range(6)]
            m = gather(mass[place, :, at]) * jnp.where(here, 1.0, 0.0).astype(F32)
            acc = pair_split(goal, rows, m, acc)
        for c in range(6):
            irregular[s, c] = acc[c]


def place_tiles(parts, count, width):
    per = 128 // width
    tiles = [jnp.zeros((8, 128), F32) for _ in range(count // per)]
    lane = lax.broadcasted_iota(jnp.int32, (8, 128), 1)
    for f, slot, column in parts:
        t = f // per
        tiles[t] = jnp.where(lane == (f % per) * width + slot * 8, column, tiles[t])
    out = []
    for tile in tiles:
        tile = pltpu.roll(tile, 0, 1, stride=1, stride_axis=0)
        out.append(jnp.sum(tile, axis=0, keepdims=True))
    return out


def send(tiles, pay):
    for t, tile in enumerate(tiles):
        full = jnp.broadcast_to(tile[None], (pay.shape[0], 1, 128))
        pay[:, :, pl.ds(t * 128, 128)] = full


def finish(step, state, slots, count, cap, regular, irregular, pay, lev):
    lane = lax.broadcasted_iota(jnp.int32, (8, 128), 1)
    parts = []
    for s in range(cap):
        k = slots[0, s]
        level = slots[2, s]
        place = slots[1, s]
        t = span_of(level)
        tile = state[k]
        x, v, a, j = columns(tile)
        close = [jnp.sum(irregular[s, c], axis=1, keepdims=True) for c in range(6)]
        total = [jnp.sum(regular[s, c], axis=1, keepdims=True) + close[c] for c in range(6)]
        half = t * 0.5
        twelfth = t * t * (1.0 / 12.0)
        v1 = [v[c] + (a[c] + total[c]) * half + (j[c] - total[3 + c]) * twelfth for c in range(3)]
        x1 = [x[c] + (v[c] + v1[c]) * half + (a[c] - total[c]) * twelfth for c in range(3)]
        if step == 3:
            mark = jnp.where(s < count, s, -1000)
            for f, column in enumerate(x1 + v1 + total + close):
                parts.append((f, s, column))
            continue
        fresh = tile
        for at, column in zip(XS + VS + AS + JS, x1 + v1 + total):
            fresh = jnp.where(lane == at, column, fresh)

        @pl.when(s < count)
        def _(k=k, fresh=fresh):
            state[k] = fresh

        ahead = forecast(x1, v1, total[:3], total[3:], TICK)
        for f, column in enumerate(ahead):
            parts.append((f, place, column))
        if step == 0:
            parts.append((6, place, tile[:, MS : MS + 1]))
    if step == 0:
        seen = jnp.int32(0)
        for k in range(NB):
            one = lev[k] == 1
            parts.append((7, jnp.where(one, seen, -1000), state[k][:, MS : MS + 1]))
            seen = seen + one.astype(jnp.int32)
        send(place_tiles(parts, 8, 32), pay)
    elif step == 1:
        send(place_tiles(parts, 6, 64), pay)
    elif step == 2:
        seen = jnp.int32(4)
        for k in range(NB):
            one = lev[k] == 1
            mark = jnp.where(one, seen, -1000)
            x, v, a, j = columns(state[k])
            for f, column in enumerate(forecast(x, v, a, j, 2 * TICK)):
                parts.append((f, mark, column))
            seen = seen + one.astype(jnp.int32)
        send(place_tiles(parts, 6, 64), pay)
    else:
        send(place_tiles(parts, 18, 64), pay)


def pack_kernel(ps, fr, mass, lev, out):
    out[0:3, :] = ps[0:3, :]
    out[3:4, :] = mass[...]
    out[4:7, :] = ps[3:6, :]
    for k in range(NB):
        out[7:8, pl.ds(k * BS, BS)] = jnp.full((1, BS), lev[k].astype(F32))
    out[8:11, :] = fr[0:3, :]
    out[11:12, :] = jnp.zeros((1, W), F32)
    out[12:15, :] = fr[3:6, :]
    out[15:16, :] = jnp.zeros((1, W), F32)


def first_kernel(own, table, lev, partner, state, pay, predicted, targets, regular, irregular, turned, slots):
    me = own[0]
    col = own[1]
    count = fill_slots(lev, TOP[0], slots)
    for k in range(NB):
        turned[:, 0:16] = table[me, :, pl.ds(k * BS, BS)].T
        state[k] = jnp.zeros((8, 128), F32)
        state[k, :, 0:16] = turned[pl.ds(pl.multiple_of(col * 8, 8), 8), 0:16]
    fill_sources(table, predicted, TICK, -1)
    fill_targets(state, slots, CAPS[0], targets)
    sweep_table(predicted, targets, CAPS[0], regular)
    close_table(predicted, targets, slots, CAPS[0], me, None, partner, -1, irregular)
    finish(0, state, slots, count, CAPS[0], regular, irregular, pay, lev)


def ahead_kernel(step, own, table, lev, levall, partner, state, regular, irregular, predicted, targets, slots):
    fill_slots(lev, TOP[step], slots)
    fill_sources(table, predicted, (step + 1) * TICK, SENT[step])
    fill_targets(state, slots, CAPS[step], targets)
    sweep_table(predicted, targets, CAPS[step], regular)
    close_table(predicted, targets, slots, CAPS[step], own[0], levall, partner, SENT[step], irregular)


def after_kernel(step, own, got, lev, levall, partner, state_in, reg_in, irr_in, *rest):
    if step == 1:
        state, pay, masses, regular, irregular, targets, turned, slots = rest
    elif step == 2:
        masses, state, pay, regular, irregular, targets, turned, slots = rest
    else:
        masses, pay, regular, irregular, targets, turned, slots = rest
        state = state_in
    count = fill_slots(lev, TOP[step], slots)
    cap = CAPS[step]
    if step < 3:
        state[...] = state_in[...]
    regular[...] = reg_in[...]
    irregular[...] = irr_in[...]
    fill_received(got, turned)
    if step == 1:
        masses[0:4] = turned[24:28]
        masses[4:8] = turned[28:32]
    fill_targets(state, slots, cap, targets)
    sweep_received(turned, masses, SLOTS[step], targets, cap, regular)
    close_received(turned, masses, SLOTS[step], targets, slots, cap, own[0], levall, partner, SENT[step], irregular)
    finish(step, state, slots, count, cap, regular, irregular, pay, lev)


def last_kernel(got, ps, fr, irr, lev, kin, comb, close, slots):
    count = fill_slots(lev, TOP[3], slots)
    kin[...] = ps[...]
    comb[...] = fr[...]
    close[...] = irr[...]
    senders = got.shape[0]
    lane = lax.broadcasted_iota(jnp.int32, (senders, 128), 1)
    row = lax.broadcasted_iota(jnp.int32, (senders, 128), 0)
    keep = lane // 8 == row
    for t in range(9):
        tile = got[:, 0, pl.ds(t * 128, 128)]
        for e in range(2):
            f = 2 * t + e
            out = (kin, comb, close)[f // 6]
            for s in range(CAPS[3]):
                shift = (128 - (e * 64 + s * 8)) % 128
                moved = pltpu.roll(pltpu.roll(tile, shift, 1), 0, 1, stride=8, stride_axis=0)
                value = jnp.sum(jnp.where(keep, moved, 0.0), axis=0, keepdims=True)
                at = pl.ds(pl.multiple_of(slots[0, s] * BS, BS), BS)

                @pl.when(s < count)
                def _(out=out, f=f, at=at, value=value):
                    out[f % 6 : f % 6 + 1, at] = value


def body(phase_space, force_rates, irregular, stellar_masses, levels, active, partner):
    shards = lax.axis_size("blk")
    columns_ = lax.axis_size("grp")
    everyone = shards * columns_
    own = jnp.stack([lax.axis_index("blk"), lax.axis_index("grp")]).astype(jnp.int32)
    packed = pl.pallas_call(
        pack_kernel,
        out_shape=jax.ShapeDtypeStruct((16, W), F32),
        in_specs=[VMEM, VMEM, VMEM, SMEM],
        out_specs=VMEM,
        name="pack",
    )(phase_space, force_rates, stellar_masses[None, :], levels)
    table = lax.all_gather(packed, "blk", axis=0, tiled=False)
    levall = table[:, 7, ::BS].astype(jnp.int32).reshape(shards * NB)

    def exchange(pay, axis):
        return lax.all_to_all(pay, axis, split_axis=0, concat_axis=0, tiled=True)

    sums = lambda cap: pltpu.VMEM((cap, 6, 8, 128), F32)
    slots = pltpu.SMEM((3, 24), jnp.int32)
    state_shape = jax.ShapeDtypeStruct((NB, 8, 128), F32)
    predicted = pltpu.VMEM((shards, 8, W), F32)
    state, pay = pl.pallas_call(
        first_kernel,
        out_shape=(state_shape, jax.ShapeDtypeStruct((everyone, 1, 256), F32)),
        in_specs=[SMEM, VMEM, SMEM, SMEM],
        out_specs=(VMEM, VMEM),
        scratch_shapes=[
            predicted, sums(4), sums(4), sums(4), pltpu.VMEM((128, 128), F32), slots,
        ],
        name="first",
    )(own, table, levels, partner)
    masses = None
    for step in (1, 2, 3):
        cap = CAPS[step]
        lanes = (0, 256, 384, 384)[step]
        got = exchange(pay, ("blk", "grp"))
        sum_shape = jax.ShapeDtypeStruct((cap, 6, 8, 128), F32)
        reg, irr = pl.pallas_call(
            functools.partial(ahead_kernel, step),
            out_shape=(sum_shape, sum_shape),
            in_specs=[SMEM, VMEM, SMEM, SMEM, SMEM, VMEM],
            out_specs=(VMEM, VMEM),
            scratch_shapes=[predicted, sums(cap), slots],
            name=f"ahead{step}",
        )(own, table, levels, levall, partner, state)
        mass_shape = jax.ShapeDtypeStruct((8, 8, everyone), F32)
        wide = (0, 384, 384, 1152)[step]
        pay_shape = jax.ShapeDtypeStruct((everyone if step < 3 else columns_, 1, wide), F32)
        out_shape = {1: (state_shape, pay_shape, mass_shape), 2: (state_shape, pay_shape), 3: (pay_shape,)}[step]
        ins = (own, got, levels, levall, partner, state, reg, irr) + (() if step == 1 else (masses,))
        outs = pl.pallas_call(
            functools.partial(after_kernel, step),
            out_shape=out_shape,
            in_specs=[SMEM, VMEM, SMEM, SMEM, SMEM] + [VMEM] * (len(ins) - 5),
            out_specs=tuple(VMEM for _ in out_shape),
            scratch_shapes=[
                sums(cap), sums(cap), sums(cap), pltpu.VMEM((lanes // 8, 8, everyone), F32), slots,
            ],
            name=f"after{step}",
        )(*ins)
        if step == 1:
            state, pay, masses = outs
        elif step == 2:
            state, pay = outs
        else:
            (pay,) = outs
    got = exchange(pay, "grp")
    shape = jax.ShapeDtypeStruct((6, W), F32)
    return tuple(
        pl.pallas_call(
            last_kernel,
            out_shape=(shape, shape, shape),
            in_specs=[VMEM, VMEM, VMEM, VMEM, SMEM],
            out_specs=(VMEM, VMEM, VMEM),
            scratch_shapes=[slots],
            name="last",
        )(got, phase_space, force_rates, irregular, levels)
    )


def solution(mesh):
    in_specs = (
        P(None, "blk"), P(None, "blk"), P(None, "blk"), P("blk"), P("blk"), P(None, "blk"), P("blk"),
    )
    out_specs = (P(None, "blk"), P(None, "blk"), P(None, "blk"))
    return jax.shard_map(body, mesh=mesh, in_specs=in_specs, out_specs=out_specs, check_vma=False)
```

```python
import functools
import jax
import jax.numpy as jnp
from jax import lax
from jax.experimental import pallas as pl
from jax.experimental.pallas import tpu as pltpu
from jax.sharding import PartitionSpec as P

WIDE = 0.04
CLOSE = 0.0001
TICK = 0.125
NB = 16
BS = 128
W = NB * BS
F32 = jnp.float32
CAPS = (4, 6, 4, 8)
TOP = (0, 1, 0, 2)
SENT = (-1, 0, 1, 1)
SLOTS = (0, 4, 8, 8)

VMEM = pl.BlockSpec(memory_space=pltpu.VMEM)
SMEM = pl.BlockSpec(memory_space=pltpu.SMEM)


def pair(target, source, mass, soften, acc):
    r = [source[c] - target[c] for c in range(3)]
    w = [source[c] - target[c] for c in range(3, 6)]
    d = (r[0] * r[0] + soften) + r[1] * r[1] + r[2] * r[2]
    s = lax.rsqrt(d)
    s2 = s * s
    weight = (mass * s) * s2
    q = (r[0] * w[0] + r[1] * w[1] + r[2] * w[2]) * (s2 * 3.0)
    acc = list(acc)
    for c in range(3):
        acc[c] = acc[c] + weight * r[c]
        acc[3 + c] = acc[3 + c] + weight * (w[c] - q * r[c])
    return tuple(acc)


def pair_split(target, source, mass, acc):
    r = [source[c] - target[c] for c in range(3)]
    w = [source[c] - target[c] for c in range(3, 6)]
    dd = r[0] * r[0] + r[1] * r[1] + r[2] * r[2]
    rw = (r[0] * w[0] + r[1] * w[1] + r[2] * w[2]) * 3.0
    acc = list(acc)
    for soften, sign in ((CLOSE, 1.0), (WIDE, -1.0)):
        s = lax.rsqrt(dd + soften)
        s2 = s * s
        weight = (mass * s) * (s2 * sign)
        q = rw * s2
        for c in range(3):
            acc[c] = acc[c] + weight * r[c]
            acc[3 + c] = acc[3 + c] + weight * (w[c] - q * r[c])
    return tuple(acc)


def zeros():
    return tuple(jnp.zeros((8, 128), F32) for _ in range(6))


def fill_slots(lev, top, slots):
    for s in range(24):
        slots[0, s] = 0
        slots[1, s] = -1000
        slots[2, s] = 0
    count = jnp.int32(0)
    ones = [jnp.int32(0), jnp.int32(4)]
    for k in range(NB):
        level = lev[k]
        live = level <= top
        place = jnp.where(level == 0, ones[0], jnp.where(level == 1, ones[1], -1000))
        slots[0, count] = k
        slots[1, count] = jnp.where(live, place, -1000)
        slots[2, count] = jnp.where(live, level, 0)
        count = count + live.astype(jnp.int32)
        ones[0] = ones[0] + (level == 0).astype(jnp.int32)
        ones[1] = ones[1] + (level == 1).astype(jnp.int32)
    return count


def span_of(level):
    return jnp.where(level == 0, TICK, jnp.where(level == 1, 2 * TICK, 4 * TICK)).astype(F32)


XS, MS, VS, AS, JS = (0, 1, 2), 3, (4, 5, 6), (8, 9, 10), (11, 12, 13)


def columns(tile):
    return tuple(
        [tile[:, c : c + 1] for c in group] for group in (XS, VS, AS, JS)
    )


def forecast(x, v, a, j, t):
    t2 = t * t * 0.5
    t3 = t * t * t * (1.0 / 6.0)
    xp = [x[c] + v[c] * t + a[c] * t2 + j[c] * t3 for c in range(3)]
    vp = [v[c] + a[c] * t + j[c] * t2 for c in range(3)]
    return xp + vp


ROWS = 14 * NB
RATES = 8 * (NB // 2)


def first_row(k):
    return k * 8 + (6 * NB if k >= NB // 2 else 0)


class Forecast:
    def __init__(self, t):
        row = lax.broadcasted_iota(jnp.int32, (8, 128), 0)
        zero = jnp.zeros((8, 128), F32)
        low = row < 3
        high = (row > 3) & (row < 7)
        self.low = lambda value: jnp.where(low, value, zero)
        self.high = lambda value: jnp.where(high, value, zero)
        t2 = t * t * 0.5
        t3 = t * t * t / 6.0
        self.c = (self.low(t), self.low(t2), self.low(t3), self.high(t), self.high(t2))

    def __call__(self, table, b, at, rates):
        first = table[b, at, :]
        second = [table[b, pl.ds(rates + o, 8), :] for o in (0, 3, -4, -1)]
        value = first + self.c[0] * pltpu.roll(first, 4, 0)
        for c, part in zip(self.c[1:], second):
            value = value + c * part
        return value


def fill_sources(table, predicted, ahead, levall, sent):
    def shard(b, count):
        for k in range(NB):
            tile = ahead(table, b, pl.ds(first_row(k), 8), RATES + 6 * k)
            predicted[count] = tile
            if sent >= 0:
                count = count + (levall[b * NB + k] > sent).astype(jnp.int32)
            else:
                count = count + 1
        return count

    count = lax.fori_loop(0, table.shape[0], shard, jnp.int32(0))
    if sent >= 0:
        for e in range(NB):
            predicted[count + e] = jnp.zeros((8, 128), F32)
    return count


def fill_targets(state, slots, cap, targets):
    for s in range(cap):
        x, v, a, j = columns(state[slots[0, s]])
        t = span_of(slots[2, s])
        for c, value in enumerate(forecast(x, v, a, j, t)):
            targets[s, c] = jnp.broadcast_to(value, (8, 128))


def broad(row):
    return jnp.broadcast_to(row, (8, 128))


def tile_rows(tiles, at):
    rows = [broad(tiles[at, r : r + 1, :]) for r in (0, 1, 2, 4, 5, 6)]
    return rows, broad(tiles[at, 3:4, :])


def sweep_table(predicted, count, targets, cap, regular):
    def two(p, _):
        goal = [[targets[2 * p + e, c] for c in range(6)] for e in range(2)]

        def group(b, acc):
            for k in range(NB):
                rows, mass = tile_rows(predicted, b * NB + k)
                acc = tuple(pair(goal[e], rows, mass, WIDE, acc[e]) for e in range(2))
            return acc

        acc = lax.fori_loop(0, (count + NB - 1) // NB, group, (zeros(), zeros()))
        for e in range(2):
            for c in range(6):
                regular[2 * p + e, c] = acc[e][c]
        return 0

    lax.fori_loop(0, cap // 2, two, 0)


def close_table(table, ahead, near, targets, slots, cap, own, levall, partner, sent, irregular):
    for s in range(cap):
        k = slots[0, s]
        at = pl.ds(pl.multiple_of(k * 8 + jnp.where(k >= NB // 2, 6 * NB, 0), 8), 8)
        for e, b in enumerate((own, partner[k] // NB)):
            near[2 * s + e] = ahead(table, b, at, RATES + 6 * k)
    for s in range(cap):
        k = slots[0, s]
        q = partner[k] // NB
        goal = [targets[s, c] for c in range(6)]
        acc = zeros()
        for e, wanted in enumerate((None, q != own)):
            here = jnp.bool_(True) if wanted is None else wanted
            if sent >= 0:
                level = slots[2, s] if wanted is None else levall[q * NB + k]
                here = here & (level > sent)
            rows, mass = tile_rows(near, 2 * s + e)
            acc = pair_split(goal, rows, mass * jnp.where(here, 1.0, 0.0).astype(F32), acc)
        for c in range(6):
            irregular[s, c] = acc[c]


def sum_up(regular, irregular, cap, sums):
    lane = lax.broadcasted_iota(jnp.int32, (8, 128), 1)
    for s in range(cap):
        tile = jnp.zeros((8, 128), F32)
        for at, part in ((0, regular), (8, irregular)):
            for c in range(6):
                tile = jnp.where(lane == at + c, jnp.sum(part[s, c], axis=1, keepdims=True), tile)
        sums[s] = tile


def fill_received(got, turned):
    senders, _, lanes = got.shape
    for t in range(lanes // 128):
        for half in range(senders // 128):
            part = got[pl.ds(half * 128, 128), 0, pl.ds(t * 128, 128)]
            turned[pl.ds(t * 16, 16), :, pl.ds(half * 128, 128)] = part.T.reshape(16, 8, 128)


def sweep_received(turned, mass, slots_in, used, targets, cap, regular):
    halves = turned.shape[2] // 128

    def two(p, _):
        goal = [[targets[2 * p + e, c] for c in range(6)] for e in range(2)]

        def slot(s, acc):
            for i in range(8):
                for half in range(halves):
                    at = pl.ds(half * 128, 128)
                    rows = [broad(turned[f * slots_in + s, i : i + 1, at]) for f in range(6)]
                    m = broad(mass[s, i : i + 1, at])
                    acc = tuple(pair(goal[e], rows, m, WIDE, acc[e]) for e in range(2))
            return acc

        acc = lax.fori_loop(0, used, slot, (zeros(), zeros()))
        for e in range(2):
            for c in range(6):
                regular[2 * p + e, c] = acc[e][c]
        return 0

    lax.fori_loop(0, cap // 2, two, 0)


def close_received(turned, mass, slots_in, targets, slots, cap, own, levall, partner, sent, irregular):
    lane = lax.broadcasted_iota(jnp.int32, (8, 128), 1)
    row = lax.broadcasted_iota(jnp.int32, (8, 128), 0)
    keep = lane // 16 == row
    for s in range(cap):
        k = slots[0, s]
        q = partner[k] // NB
        goal = [targets[s, c] for c in range(6)]
        acc = zeros()
        for b, wanted in ((own, None), (q, q != own)):
            if wanted is None:
                here = slots[2, s] <= sent
                place = slots[1, s]
            else:
                level = levall[q * NB + k]
                here = wanted & (level <= sent)
                place = jnp.where(level == 0, 0, 4)
                for e in range(NB):
                    same = (levall[q * NB + e] == level) & (e < k)
                    place = place + same.astype(jnp.int32)
            place = jnp.clip(jnp.where(here, place, 0), 0, slots_in - 1)
            at = pl.ds(pl.multiple_of((b // 8) * 128, 128), 128)
            shift = lax.rem(128 - lax.rem(b, 8) * 16, 128)

            def gather(tile):
                tile = pltpu.roll(pltpu.roll(tile, shift, 1), 0, 1, stride=16, stride_axis=0)
                return broad(jnp.sum(jnp.where(keep, tile, 0.0), axis=0, keepdims=True))

            rows = [gather(turned[f * slots_in + place, :, at]) for f in range(6)]
            m = gather(mass[place, :, at]) * jnp.where(here, 1.0, 0.0).astype(F32)
            acc = pair_split(goal, rows, m, acc)
        for c in range(6):
            irregular[s, c] = acc[c]


def place_tiles(parts, count, width):
    per = 128 // width
    tiles = [jnp.zeros((8, 128), F32) for _ in range(count // per)]
    lane = lax.broadcasted_iota(jnp.int32, (8, 128), 1)
    for f, slot, column in parts:
        t = f // per
        tiles[t] = jnp.where(lane == (f % per) * width + slot * 8, column, tiles[t])
    out = []
    for tile in tiles:
        tile = pltpu.roll(tile, 0, 1, stride=1, stride_axis=0)
        out.append(jnp.sum(tile, axis=0, keepdims=True))
    return out


def send(tiles, pay):
    for t, tile in enumerate(tiles):
        full = jnp.broadcast_to(tile[None], (pay.shape[0], 1, 128))
        pay[:, :, pl.ds(t * 128, 128)] = full


def finish(step, state, slots, count, cap, regular, irregular, sums, pay, lev):
    lane = lax.broadcasted_iota(jnp.int32, (8, 128), 1)
    parts = []
    for s in range(cap):
        k = slots[0, s]
        level = slots[2, s]
        place = slots[1, s]
        t = span_of(level)
        tile = state[k]
        x, v, a, j = columns(tile)
        close = [jnp.sum(irregular[s, c], axis=1, keepdims=True) for c in range(6)]
        total = [jnp.sum(regular[s, c], axis=1, keepdims=True) for c in range(6)]
        if sums is not None:
            before = sums[s]
            close = [close[c] + before[:, 8 + c : 9 + c] for c in range(6)]
            total = [total[c] + before[:, c : c + 1] for c in range(6)]
        total = [total[c] + close[c] for c in range(6)]
        half = t * 0.5
        twelfth = t * t * (1.0 / 12.0)
        v1 = [v[c] + (a[c] + total[c]) * half + (j[c] - total[3 + c]) * twelfth for c in range(3)]
        x1 = [x[c] + (v[c] + v1[c]) * half + (a[c] - total[c]) * twelfth for c in range(3)]
        if step == 3:
            mark = jnp.where(s < count, s, -1000)
            for f, column in enumerate(x1 + v1 + total + close):
                parts.append((f, s, column))
            continue
        fresh = tile
        for at, column in zip(XS + VS + AS + JS, x1 + v1 + total):
            fresh = jnp.where(lane == at, column, fresh)

        @pl.when(s < count)
        def _(k=k, fresh=fresh):
            state[k] = fresh

        ahead = forecast(x1, v1, total[:3], total[3:], TICK)
        for f, column in enumerate(ahead):
            parts.append((f, place, column))
        if step == 0:
            parts.append((6, place, tile[:, MS : MS + 1]))
    if step == 0:
        seen = jnp.int32(0)
        for k in range(NB):
            one = lev[k] == 1
            parts.append((7, jnp.where(one, seen, -1000), state[k][:, MS : MS + 1]))
            seen = seen + one.astype(jnp.int32)
        send(place_tiles(parts, 8, 32), pay)
    elif step == 1:
        send(place_tiles(parts, 6, 64), pay)
    elif step == 2:
        seen = jnp.int32(4)
        for k in range(NB):
            one = lev[k] == 1
            mark = jnp.where(one, seen, -1000)
            x, v, a, j = columns(state[k])
            for f, column in enumerate(forecast(x, v, a, j, 2 * TICK)):
                parts.append((f, mark, column))
            seen = seen + one.astype(jnp.int32)
        send(place_tiles(parts, 6, 64), pay)
    else:
        send(place_tiles(parts, 18, 64), pay)


def pack_kernel(ps, fr, mass, lev, out):
    lane = lax.broadcasted_iota(jnp.int32, (1, BS), 1)
    levels = jnp.zeros((1, BS), F32)
    for k in range(NB):
        levels = jnp.where(lane == k, lev[k].astype(F32), levels)
    for k in range(NB):
        at = pl.ds(k * BS, BS)
        first = first_row(k)
        out[first : first + 3, :] = ps[0:3, at]
        out[first + 3 : first + 4, :] = mass[:, at]
        out[first + 4 : first + 7, :] = ps[3:6, at]
        out[first + 7 : first + 8, :] = levels
        out[RATES + 6 * k : RATES + 6 * k + 6, :] = fr[:, at]


def first_kernel(own, table, lev, partner, state, pay, predicted, near, targets, regular, irregular, turned, slots):
    me = own[0]
    col = pl.multiple_of(own[1] * 8, 8)
    count = fill_slots(lev, TOP[0], slots)
    for k in range(NB):
        turned[k, :, 0:8] = table[me, pl.ds(first_row(k), 8), :].T
        turned[k, :, 8:16] = table[me, pl.ds(RATES + 6 * k, 8), :].T
    for k in range(NB):
        state[k] = turned[k, pl.ds(col, 8), :]
    ahead = Forecast(TICK)
    used = fill_sources(table, predicted, ahead, None, -1)
    fill_targets(state, slots, CAPS[0], targets)
    sweep_table(predicted, used, targets, CAPS[0], regular)
    close_table(table, ahead, near, targets, slots, CAPS[0], me, None, partner, -1, irregular)
    finish(0, state, slots, count, CAPS[0], regular, irregular, None, pay, lev)


def ahead_kernel(step, own, table, lev, levall, partner, state, sums, *rest):
    if step == 1:
        ones, predicted, near, targets, regular, irregular, slots = rest
    else:
        predicted, near, targets, regular, irregular, slots = rest
    cap = CAPS[step]
    fill_slots(lev, TOP[step], slots)
    ahead = Forecast((step + 1) * TICK)
    used = fill_sources(table, predicted, ahead, levall, SENT[step])
    fill_targets(state, slots, cap, targets)
    sweep_table(predicted, used, targets, cap, regular)
    close_table(table, ahead, near, targets, slots, cap, own[0], levall, partner, SENT[step], irregular)
    sum_up(regular, irregular, cap, sums)
    if step == 1:

        def shard(b, most):
            here = jnp.int32(0)
            for k in range(NB):
                here = here + (levall[b * NB + k] == 1).astype(jnp.int32)
            return jnp.maximum(most, here)

        ones[0] = lax.fori_loop(0, table.shape[0], shard, jnp.int32(0))


def after_kernel(step, own, got, lev, levall, partner, state_in, sums, *rest):
    if step == 1:
        state, pay, masses, regular, irregular, targets, turned, slots = rest
        used = SLOTS[step]
    else:
        masses, ones, *rest = rest
        used = jnp.minimum(4 + ones[0], SLOTS[step])
        if step == 2:
            state, pay, regular, irregular, targets, turned, slots = rest
        else:
            pay, regular, irregular, targets, turned, slots = rest
            state = state_in
    count = fill_slots(lev, TOP[step], slots)
    cap = CAPS[step]
    if step < 3:
        state[...] = state_in[...]
    fill_received(got, turned)
    if step == 1:
        masses[0:4] = turned[24:28]
        masses[4:8] = turned[28:32]
    fill_targets(state, slots, cap, targets)
    sweep_received(turned, masses, SLOTS[step], used, targets, cap, regular)
    close_received(turned, masses, SLOTS[step], targets, slots, cap, own[0], levall, partner, SENT[step], irregular)
    finish(step, state, slots, count, cap, regular, irregular, sums, pay, lev)


def last_kernel(got, ps, fr, irr, lev, kin, comb, close, slots):
    count = fill_slots(lev, TOP[3], slots)
    kin[...] = ps[...]
    comb[...] = fr[...]
    close[...] = irr[...]
    senders = got.shape[0]
    lane = lax.broadcasted_iota(jnp.int32, (senders, 128), 1)
    row = lax.broadcasted_iota(jnp.int32, (senders, 128), 0)
    spread = [pltpu.roll(got[:, 0, pl.ds(t * 128, 128)], 0, 1, stride=8, stride_axis=0) for t in range(9)]
    for s in range(CAPS[3]):
        rows = []
        for f in range(18):
            t, e = divmod(f, 2)
            start = e * 64 + s * 8
            keep = (lane + (128 - start)) % 128 // 8 == row
            value = jnp.sum(jnp.where(keep, spread[t], 0.0), axis=0, keepdims=True)
            rows.append(pltpu.roll(value, (128 - start) % 128, 1))
        at = pl.ds(pl.multiple_of(slots[0, s] * BS, BS), BS)

        @pl.when(s < count)
        def _(at=at, rows=rows):
            for f, value in enumerate(rows):
                out = (kin, comb, close)[f // 6]
                out[f % 6 : f % 6 + 1, at] = value


def body(phase_space, force_rates, irregular, stellar_masses, levels, active, partner):
    shards = lax.axis_size("blk")
    columns_ = lax.axis_size("grp")
    everyone = shards * columns_
    own = jnp.stack([lax.axis_index("blk"), lax.axis_index("grp")]).astype(jnp.int32)
    packed = pl.pallas_call(
        pack_kernel,
        out_shape=jax.ShapeDtypeStruct((ROWS, BS), F32),
        in_specs=[VMEM, VMEM, VMEM, SMEM],
        out_specs=VMEM,
        name="pack",
    )(phase_space, force_rates, stellar_masses[None, :], levels)
    table = lax.all_gather(packed, "blk", axis=0, tiled=False)
    levall = table[:, 7, :NB].astype(jnp.int32).reshape(shards * NB)

    def exchange(pay, axis):
        return lax.all_to_all(pay, axis, split_axis=0, concat_axis=0, tiled=True)

    parts = lambda cap: pltpu.VMEM((cap, 6, 8, 128), F32)
    tiles = lambda count: pltpu.VMEM((count, 8, 128), F32)
    slots = pltpu.SMEM((3, 24), jnp.int32)
    state_shape = jax.ShapeDtypeStruct((NB, 8, 128), F32)
    predicted = tiles(shards * NB + NB)
    state, pay = pl.pallas_call(
        first_kernel,
        out_shape=(state_shape, jax.ShapeDtypeStruct((everyone, 1, 256), F32)),
        in_specs=[SMEM, VMEM, SMEM, SMEM],
        out_specs=(VMEM, VMEM),
        scratch_shapes=[
            predicted, tiles(8), parts(4), parts(4), parts(4), pltpu.VMEM((NB, 128, 128), F32), slots,
        ],
        name="first",
    )(own, table, levels, partner)
    masses = ones = None
    for step in (1, 2, 3):
        cap = CAPS[step]
        lanes = (0, 256, 384, 384)[step]
        got = exchange(pay, ("blk", "grp"))
        sums_shape = jax.ShapeDtypeStruct((cap, 8, 128), F32)
        outs = pl.pallas_call(
            functools.partial(ahead_kernel, step),
            out_shape=(sums_shape, jax.ShapeDtypeStruct((1,), jnp.int32)) if step == 1 else sums_shape,
            in_specs=[SMEM, VMEM, SMEM, SMEM, SMEM, VMEM],
            out_specs=(VMEM, SMEM) if step == 1 else VMEM,
            scratch_shapes=[predicted, tiles(2 * cap), parts(cap), parts(cap), parts(cap), slots],
            name=f"ahead{step}",
        )(own, table, levels, levall, partner, state)
        if step == 1:
            sums, ones = outs
        else:
            sums = outs
        mass_shape = jax.ShapeDtypeStruct((8, 8, everyone), F32)
        wide = (0, 384, 384, 1152)[step]
        pay_shape = jax.ShapeDtypeStruct((everyone if step < 3 else columns_, 1, wide), F32)
        out_shape = {1: (state_shape, pay_shape, mass_shape), 2: (state_shape, pay_shape), 3: (pay_shape,)}[step]
        ins = (own, got, levels, levall, partner, state, sums)
        specs = [SMEM, VMEM, SMEM, SMEM, SMEM, VMEM, VMEM]
        if step > 1:
            ins += (masses, ones)
            specs += [VMEM, SMEM]
        outs = pl.pallas_call(
            functools.partial(after_kernel, step),
            out_shape=out_shape,
            in_specs=specs,
            out_specs=tuple(VMEM for _ in out_shape),
            scratch_shapes=[
                parts(cap), parts(cap), parts(cap), pltpu.VMEM((lanes // 8, 8, everyone), F32), slots,
            ],
            name=f"after{step}",
        )(*ins)
        if step == 1:
            state, pay, masses = outs
        elif step == 2:
            state, pay = outs
        else:
            (pay,) = outs
    got = exchange(pay, "grp")
    shape = jax.ShapeDtypeStruct((6, W), F32)
    return tuple(
        pl.pallas_call(
            last_kernel,
            out_shape=(shape, shape, shape),
            in_specs=[VMEM, VMEM, VMEM, VMEM, SMEM],
            out_specs=(VMEM, VMEM, VMEM),
            scratch_shapes=[slots],
            name="last",
        )(got, phase_space, force_rates, irregular, levels)
    )


def solution(mesh):
    in_specs = (
        P(None, "blk"), P(None, "blk"), P(None, "blk"), P("blk"), P("blk"), P(None, "blk"), P("blk"),
    )
    out_specs = (P(None, "blk"), P(None, "blk"), P(None, "blk"))
    return jax.shard_map(body, mesh=mesh, in_specs=in_specs, out_specs=out_specs, check_vma=False)
```

```python
import functools
import jax
import jax.numpy as jnp
from jax import lax
from jax.experimental import pallas as pl
from jax.experimental.pallas import tpu as pltpu
from jax.sharding import PartitionSpec as P

WIDE = 0.04
CLOSE = 0.0001
TICK = 0.125
NB = 16
BS = 128
W = NB * BS
F32 = jnp.float32
CAPS = (4, 6, 4, 8)
TOP = (0, 1, 0, 2)
SENT = (-1, 0, 1, 1)
SLOTS = (0, 4, 8, 8)

VMEM = pl.BlockSpec(memory_space=pltpu.VMEM)
SMEM = pl.BlockSpec(memory_space=pltpu.SMEM)


def pair(target, source, mass, soften, acc):
    r = [source[c] - target[c] for c in range(3)]
    w = [source[c] - target[c] for c in range(3, 6)]
    d = (r[0] * r[0] + soften) + r[1] * r[1] + r[2] * r[2]
    s = lax.rsqrt(d)
    s2 = s * s
    weight = (mass * s) * s2
    q = (r[0] * w[0] + r[1] * w[1] + r[2] * w[2]) * (s2 * 3.0)
    acc = list(acc)
    for c in range(3):
        acc[c] = acc[c] + weight * r[c]
        acc[3 + c] = acc[3 + c] + weight * (w[c] - q * r[c])
    return tuple(acc)


def pair_split(target, source, mass, acc):
    r = [source[c] - target[c] for c in range(3)]
    w = [source[c] - target[c] for c in range(3, 6)]
    dd = r[0] * r[0] + r[1] * r[1] + r[2] * r[2]
    rw = (r[0] * w[0] + r[1] * w[1] + r[2] * w[2]) * 3.0
    acc = list(acc)
    for soften, sign in ((CLOSE, 1.0), (WIDE, -1.0)):
        s = lax.rsqrt(dd + soften)
        s2 = s * s
        weight = (mass * s) * (s2 * sign)
        q = rw * s2
        for c in range(3):
            acc[c] = acc[c] + weight * r[c]
            acc[3 + c] = acc[3 + c] + weight * (w[c] - q * r[c])
    return tuple(acc)


def zeros():
    return tuple(jnp.zeros((8, 128), F32) for _ in range(6))


BLOCK, PLACE, LEVEL, SHARD, ROW, HERE, COUNT = range(7)


def fill_slots(lev, top, cap, plan):
    for s in range(cap):
        plan[BLOCK, s] = 0
        plan[PLACE, s] = -1000
        plan[LEVEL, s] = 0
    count = jnp.int32(0)
    ones = [jnp.int32(0), jnp.int32(4)]
    for k in range(NB):
        level = lev[k]
        live = level <= top
        place = jnp.where(level == 0, ones[0], jnp.where(level == 1, ones[1], -1000))
        plan[BLOCK, count] = k
        plan[PLACE, count] = jnp.where(live, place, -1000)
        plan[LEVEL, count] = jnp.where(live, level, 0)
        count = count + live.astype(jnp.int32)
        ones[0] = ones[0] + (level == 0).astype(jnp.int32)
        ones[1] = ones[1] + (level == 1).astype(jnp.int32)
    plan[COUNT, 0] = count


def fill_near(plan, cap, own, levall, partner, sent):
    for s in range(cap):
        k = plan[BLOCK, s]
        q = partner[k] // NB
        level = levall[q * NB + k]
        place = jnp.where(level == 0, 0, 4)
        for e in range(NB):
            same = (levall[q * NB + e] == level) & (e < k)
            place = place + same.astype(jnp.int32)
        ours = plan[LEVEL, s] <= sent
        theirs = (q != own) & (level <= sent)
        for e, (b, row, here) in enumerate(((own, plan[PLACE, s], ours), (q, place, theirs))):
            plan[SHARD, 2 * s + e] = b
            plan[ROW, 2 * s + e] = jnp.clip(jnp.where(here, row, 0), 0, 3 if sent == 0 else 7)
            plan[HERE, 2 * s + e] = here.astype(jnp.int32)


def span_of(level):
    return jnp.where(level == 0, TICK, jnp.where(level == 1, 2 * TICK, 4 * TICK)).astype(F32)


XS, MS, VS, AS, JS = (0, 1, 2), 3, (4, 5, 6), (8, 9, 10), (11, 12, 13)


def columns(tile):
    return tuple(
        [tile[:, c : c + 1] for c in group] for group in (XS, VS, AS, JS)
    )


def forecast(x, v, a, j, t):
    t2 = t * t * 0.5
    t3 = t * t * t * (1.0 / 6.0)
    xp = [x[c] + v[c] * t + a[c] * t2 + j[c] * t3 for c in range(3)]
    vp = [v[c] + a[c] * t + j[c] * t2 for c in range(3)]
    return xp + vp


class Forecast:
    def __init__(self, t):
        row = lax.broadcasted_iota(jnp.int32, (8, 128), 0)
        zero = jnp.zeros((8, 128), F32)
        low = row < 3
        high = (row > 3) & (row < 7)
        self.low = lambda value: jnp.where(low, value, zero)
        self.high = lambda value: jnp.where(high, value, zero)
        t2 = t * t * 0.5
        t3 = t * t * t / 6.0
        self.c = (self.low(t), self.low(t2), self.low(t3), self.high(t), self.high(t2))

    def __call__(self, table, rates, b, k):
        first = table[b, pl.ds(7 * k, 8), :]
        value = first + self.c[0] * pltpu.roll(first, 4, 0)
        for c, o in zip(self.c[1:], (4, 7, 0, 3)):
            value = value + c * rates[b, pl.ds(6 * k + o, 8), :]
        return value


def fill_sources(table, rates, predicted, ahead, levall, sent):
    def shard(b, count):
        for k in range(NB):
            predicted[count] = ahead(table, rates, b, k)
            count = count + (levall[b * NB + k] > sent).astype(jnp.int32)
        return count

    count = lax.fori_loop(0, table.shape[0], shard, jnp.int32(0))
    for e in range(NB):
        predicted[count + e] = jnp.zeros((8, 128), F32)
    return count


def fill_targets(state, plan, cap, targets):
    for s in range(cap):
        x, v, a, j = columns(state[plan[BLOCK, s]])
        t = span_of(plan[LEVEL, s])
        for c, value in enumerate(forecast(x, v, a, j, t)):
            targets[s, c] = jnp.broadcast_to(value, (8, 128))


def broad(row):
    return jnp.broadcast_to(row, (8, 128))


def tile_rows(tiles, at, start=0):
    rows = [broad(tiles[at, pl.ds(start + r, 1), :]) for r in (0, 1, 2, 4, 5, 6)]
    return rows, broad(tiles[at, pl.ds(start + 3, 1), :])


def sweep_table(groups, load, targets, cap, regular):
    def two(p, _):
        goal = [[targets[2 * p + e, c] for c in range(6)] for e in range(2)]

        def group(b, acc):
            for k in range(NB):
                rows, mass = load(b, k)
                acc = tuple(pair(goal[e], rows, mass, WIDE, acc[e]) for e in range(2))
            return acc

        acc = lax.fori_loop(0, groups, group, (zeros(), zeros()))
        for e in range(2):
            for c in range(6):
                regular[2 * p + e, c] = acc[e][c]
        return 0

    lax.fori_loop(0, cap // 2, two, 0)


def close_pairs(load, wanted, targets, cap, irregular):
    for s in range(cap):
        goal = [targets[s, c] for c in range(6)]
        acc = zeros()
        for e in range(2):
            rows, mass = load(s, e)
            acc = pair_split(goal, rows, mass * jnp.where(wanted(s, e), 1.0, 0.0).astype(F32), acc)
        for c in range(6):
            irregular[s, c] = acc[c]


def sum_up(regular, irregular, cap, sums):
    lane = lax.broadcasted_iota(jnp.int32, (8, 128), 1)
    for s in range(cap):
        tile = jnp.zeros((8, 128), F32)
        for at, part in ((0, regular), (8, irregular)):
            for c in range(6):
                tile = jnp.where(lane == at + c, jnp.sum(part[s, c], axis=1, keepdims=True), tile)
        sums[s] = tile


def fill_received(got, turned):
    senders, _, lanes = got.shape
    for t in range(lanes // 128):
        for half in range(senders // 128):
            part = got[pl.ds(half * 128, 128), 0, pl.ds(t * 128, 128)]
            turned[pl.ds(t * 16, 16), :, pl.ds(half * 128, 128)] = part.T.reshape(16, 8, 128)


def sweep_received(turned, mass, slots_in, used, targets, plan, near, cap, regular):
    halves = turned.shape[2] // 128
    lane = lax.broadcasted_iota(jnp.int32, (8, 128), 1)
    row = lax.broadcasted_iota(jnp.int32, (8, 128), 0)
    keep = lane // 16 == row

    def two(p, _):
        goal = [[targets[2 * p + e, c] for c in range(6)] for e in range(2)]

        def slot(s, acc):
            item = 4 * p + lax.rem(s, 4)
            b = plan[SHARD, item]
            place = plan[ROW, item]
            half = pl.ds(pl.multiple_of((b // 8) * 128, 128), 128)
            shift = lax.rem(128 - lax.rem(b, 8) * 16, 128)
            here = plan[HERE, item].astype(F32)
            for r, f in ((0, 0), (1, 1), (2, 2), (4, 3), (5, 4), (6, 5), (3, None)):
                tile = mass[place, :, half] * here if f is None else turned[f * slots_in + place, :, half]
                tile = pltpu.roll(pltpu.roll(tile, shift, 1), 0, 1, stride=16, stride_axis=0)
                near[item, r : r + 1, :] = jnp.sum(jnp.where(keep, tile, 0.0), axis=0, keepdims=True)
            for i in range(8):
                for half in range(halves):
                    at = pl.ds(half * 128, 128)
                    rows = [broad(turned[f * slots_in + s, i : i + 1, at]) for f in range(6)]
                    m = broad(mass[s, i : i + 1, at])
                    acc = tuple(pair(goal[e], rows, m, WIDE, acc[e]) for e in range(2))
            return acc

        acc = lax.fori_loop(0, used, slot, (zeros(), zeros()))
        for e in range(2):
            for c in range(6):
                regular[2 * p + e, c] = acc[e][c]
        return 0

    lax.fori_loop(0, cap // 2, two, 0)


def fill_tiles(parts, tiles, width):
    per = 128 // width
    tiles = list(tiles)
    lane = lax.broadcasted_iota(jnp.int32, (8, 128), 1)
    for f, slot, column in parts:
        t = f // per
        tiles[t] = jnp.where(lane == (f % per) * width + slot * 8, column, tiles[t])
    return tiles


def blank(count):
    return [jnp.zeros((8, 128), F32) for _ in range(count)]


def place_tiles(tiles):
    tiles = [pltpu.roll(tile, 0, 1, stride=1, stride_axis=0) for tile in tiles]
    return [jnp.sum(tile, axis=0, keepdims=True) for tile in tiles]


def send(tiles, pay):
    for t, tile in enumerate(tiles):
        full = jnp.broadcast_to(tile[None], (pay.shape[0], 1, 128))
        pay[:, :, pl.ds(t * 128, 128)] = full


def finish(step, state, plan, cap, regular, irregular, sums, later, pay, lev):
    lane = lax.broadcasted_iota(jnp.int32, (8, 128), 1)
    count = plan[COUNT, 0]
    parts = []
    for s in range(cap):
        k = plan[BLOCK, s]
        level = plan[LEVEL, s]
        place = plan[PLACE, s]
        t = span_of(level)
        tile = state[k]
        x, v, a, j = columns(tile)
        close = [jnp.sum(irregular[s, c], axis=1, keepdims=True) for c in range(6)]
        total = [jnp.sum(regular[s, c], axis=1, keepdims=True) for c in range(6)]
        if sums is not None:
            before = sums[s]
            close = [close[c] + before[:, 8 + c : 9 + c] for c in range(6)]
            total = [total[c] + before[:, c : c + 1] for c in range(6)]
        total = [total[c] + close[c] for c in range(6)]
        half = t * 0.5
        twelfth = t * t * (1.0 / 12.0)
        v1 = [v[c] + (a[c] + total[c]) * half + (j[c] - total[3 + c]) * twelfth for c in range(3)]
        x1 = [x[c] + (v[c] + v1[c]) * half + (a[c] - total[c]) * twelfth for c in range(3)]
        if step == 3:
            for f, column in enumerate(x1 + v1 + total + close):
                parts.append((f, s, column))
            continue
        fresh = tile
        for at, column in zip(XS + VS + AS + JS, x1 + v1 + total):
            fresh = jnp.where(lane == at, column, fresh)

        @pl.when(s < count)
        def _(k=k, fresh=fresh):
            state[k] = fresh

        ahead = forecast(x1, v1, total[:3], total[3:], TICK)
        for f, column in enumerate(ahead):
            parts.append((f, place, column))
        if step == 0:
            parts.append((6, place, tile[:, MS : MS + 1]))
    if step == 0:
        seen = jnp.int32(0)
        for k in range(NB):
            one = lev[k] == 1
            parts.append((7, jnp.where(one, seen, -1000), state[k][:, MS : MS + 1]))
            seen = seen + one.astype(jnp.int32)
        send(place_tiles(fill_tiles(parts, blank(2), 32)), pay)
    elif step == 1:
        send(place_tiles(fill_tiles(parts, blank(3), 64)), pay)
    elif step == 2:
        send(place_tiles(fill_tiles(parts, [later[t] for t in range(3)], 64)), pay)
    else:
        send(place_tiles(fill_tiles(parts, blank(9), 64)), pay)


def fill_later(state, lev, later):
    parts = []
    seen = jnp.int32(4)
    for k in range(NB):
        one = lev[k] == 1
        mark = jnp.where(one, seen, -1000)
        x, v, a, j = columns(state[k])
        for f, column in enumerate(forecast(x, v, a, j, 2 * TICK)):
            parts.append((f, mark, column))
        seen = seen + one.astype(jnp.int32)
    for t, tile in enumerate(fill_tiles(parts, blank(3), 64)):
        later[t] = tile


def pack_kernel(ps, fr, mass, lev, first, rates, own):
    x, v, a, j = ps[0:3, :], ps[3:6, :], fr[0:3, :], fr[3:6, :]
    t2 = TICK * TICK * 0.5
    xp = x + v * TICK + a * t2 + j * (TICK * TICK * TICK / 6.0)
    vp = v + a * TICK + j * t2
    ap = a + j * TICK
    lane = lax.broadcasted_iota(jnp.int32, (8, BS), 1)
    levels = jnp.zeros((8, BS), F32)
    for k in range(NB):
        levels = jnp.where(lane == k, lev[k].astype(F32), levels)
    first[7 * NB : 7 * NB + 8, :] = levels
    rates[0:8, :] = jnp.zeros((8, BS), F32)
    rates[96:112, :] = jnp.zeros((16, BS), F32)
    for k in range(NB):
        at = slice(k * BS, k * BS + BS)
        first[7 * k : 7 * k + 3, :] = xp[:, at]
        first[7 * k + 3 : 7 * k + 4, :] = mass[:, at]
        first[7 * k + 4 : 7 * k + 7, :] = vp[:, at]
        rates[6 * k + 4 : 6 * k + 7, :] = ap[:, at]
        rates[6 * k + 7 : 6 * k + 10, :] = j[:, at]
        own[k] = jnp.zeros((16, BS), F32)
        own[k, 0:3, :] = x[:, at]
        own[k, 3:4, :] = mass[:, at]
        own[k, 4:7, :] = v[:, at]
        own[k, 8:14, :] = fr[:, at]


def first_kernel(own, table, mine, lev, partner, state, pay, targets, regular, irregular, turned, plan):
    me = own[0]
    col = pl.multiple_of(own[1] * 8, 8)
    cap = CAPS[0]
    fill_slots(lev, TOP[0], cap, plan)
    for k in range(NB):
        turned[k, :, 0:16] = mine[k].T
    for k in range(NB):
        state[k] = turned[k, pl.ds(col, 8), :]
    fill_targets(state, plan, cap, targets)
    sweep_table(table.shape[0], lambda b, k: tile_rows(table, b, 7 * k), targets, cap, regular)

    def shard(s, e):
        return partner[plan[BLOCK, s]] // NB if e else me

    close_pairs(
        lambda s, e: tile_rows(table, shard(s, e), 7 * plan[BLOCK, s]),
        lambda s, e: shard(s, e) != me if e else jnp.bool_(True),
        targets, cap, irregular,
    )
    finish(0, state, plan, cap, regular, irregular, None, None, pay, lev)


def ahead_kernel(step, own, table, rates, lev, levall, partner, state, sums, plan, *rest):
    later = None
    if step == 2:
        later, *rest = rest
    predicted, near, targets, regular, irregular = rest
    cap = CAPS[step]
    sent = SENT[step]
    fill_slots(lev, TOP[step], cap, plan)
    fill_near(plan, cap, own[0], levall, partner, sent)
    ahead = Forecast(step * TICK)
    used = fill_sources(table, rates, predicted, ahead, levall, sent)
    fill_targets(state, plan, cap, targets)
    for s in range(cap):
        for e in range(2):
            near[2 * s + e] = ahead(table, rates, plan[SHARD, 2 * s + e], plan[BLOCK, s])
    sweep_table((used + NB - 1) // NB, lambda b, k: tile_rows(predicted, b * NB + k), targets, cap, regular)

    def wanted(s, e):
        other = plan[SHARD, 2 * s + 1] != own[0] if e else jnp.bool_(True)
        return other & (plan[HERE, 2 * s + e] == 0)

    close_pairs(lambda s, e: tile_rows(near, 2 * s + e), wanted, targets, cap, irregular)
    sum_up(regular, irregular, cap, sums)
    if step == 2:
        fill_later(state, lev, later)
    if step == 1:

        def shard(b, most):
            here = jnp.int32(0)
            for k in range(NB):
                here = here + (levall[b * NB + k] == 1).astype(jnp.int32)
            return jnp.maximum(most, here)

        plan[COUNT, 1] = lax.fori_loop(0, table.shape[0], shard, jnp.int32(0))


def after_kernel(step, got, lev, state_in, sums, plan, *rest):
    later = None
    used = SLOTS[step]
    if step > 1:
        masses, before, *rest = rest
        used = jnp.minimum(4 + before[COUNT, 1], used)
    if step == 2:
        later, *rest = rest
    if step == 3:
        state = state_in
    else:
        state, *rest = rest
        state[...] = state_in[...]
    pay, *rest = rest
    if step == 1:
        masses, *rest = rest
    regular, irregular, targets, near, turned = rest
    cap = CAPS[step]
    fill_received(got, turned)
    if step == 1:
        masses[0:4] = turned[24:28]
        masses[4:8] = turned[28:32]
    fill_targets(state, plan, cap, targets)
    sweep_received(turned, masses, SLOTS[step], used, targets, plan, near, cap, regular)
    close_pairs(
        lambda s, e: tile_rows(near, 2 * s + e),
        lambda s, e: plan[HERE, 2 * s + e] == 1,
        targets, cap, irregular,
    )
    finish(step, state, plan, cap, regular, irregular, sums, later, pay, lev)


def last_kernel(got, ps, fr, irr, plan, kin, comb, close):
    count = plan[COUNT, 0]
    kin[...] = ps[...]
    comb[...] = fr[...]
    close[...] = irr[...]
    senders = got.shape[0]
    lane = lax.broadcasted_iota(jnp.int32, (senders, 128), 1)
    row = lax.broadcasted_iota(jnp.int32, (senders, 128), 0)
    spread = [pltpu.roll(got[:, 0, pl.ds(t * 128, 128)], 0, 1, stride=8, stride_axis=0) for t in range(9)]
    for s in range(CAPS[3]):
        rows = []
        for f in range(18):
            t, e = divmod(f, 2)
            start = e * 64 + s * 8
            keep = (lane + (128 - start)) % 128 // 8 == row
            value = jnp.sum(jnp.where(keep, spread[t], 0.0), axis=0, keepdims=True)
            rows.append(pltpu.roll(value, (128 - start) % 128, 1))
        at = pl.ds(pl.multiple_of(plan[BLOCK, s] * BS, BS), BS)

        @pl.when(s < count)
        def _(at=at, rows=rows):
            for f, value in enumerate(rows):
                out = (kin, comb, close)[f // 6]
                out[f % 6 : f % 6 + 1, at] = value


def body(phase_space, force_rates, irregular, stellar_masses, levels, active, partner):
    shards = lax.axis_size("blk")
    columns_ = lax.axis_size("grp")
    everyone = shards * columns_
    own = jnp.stack([lax.axis_index("blk"), lax.axis_index("grp")]).astype(jnp.int32)
    tiles = lambda count: pltpu.VMEM((count, 8, 128), F32)
    parts = lambda cap: pltpu.VMEM((cap, 6, 8, 128), F32)
    array = lambda *shape: jax.ShapeDtypeStruct(shape, F32)
    plan_shape = jax.ShapeDtypeStruct((8, 32), jnp.int32)
    state_shape = array(NB, 8, 128)

    def exchange(pay, axis):
        return lax.all_to_all(pay, axis, split_axis=0, concat_axis=0, tiled=True)

    packed, rates, mine = pl.pallas_call(
        pack_kernel,
        out_shape=(array(7 * NB + 8, BS), array(7 * NB, BS), array(NB, 16, BS)),
        in_specs=[VMEM, VMEM, VMEM, SMEM],
        out_specs=(VMEM, VMEM, VMEM),
        name="pack",
    )(phase_space, force_rates, stellar_masses[None, :], levels)
    table = lax.all_gather(packed, "blk", axis=0, tiled=False)
    levall = table[:, 7 * NB, :NB].astype(jnp.int32).reshape(shards * NB)
    rates = exchange(jnp.broadcast_to(rates[None], (shards, 7 * NB, BS)), "blk")
    state, pay = pl.pallas_call(
        first_kernel,
        out_shape=(state_shape, array(everyone, 1, 256)),
        in_specs=[SMEM, VMEM, VMEM, SMEM, SMEM],
        out_specs=(VMEM, VMEM),
        scratch_shapes=[
            parts(4), parts(4), parts(4), pltpu.VMEM((NB, 128, 128), F32), pltpu.SMEM((8, 32), jnp.int32),
        ],
        name="first",
    )(own, table, mine, levels, partner)
    masses = before = None
    for step in (1, 2, 3):
        cap = CAPS[step]
        lanes = (0, 256, 384, 384)[step]
        got = exchange(pay, ("blk", "grp"))
        outs = pl.pallas_call(
            functools.partial(ahead_kernel, step),
            out_shape=(array(cap, 8, 128), plan_shape) + ((array(3, 8, 128),) if step == 2 else ()),
            in_specs=[SMEM, VMEM, VMEM, SMEM, SMEM, SMEM, VMEM],
            out_specs=(VMEM, SMEM) + ((VMEM,) if step == 2 else ()),
            scratch_shapes=[tiles(shards * NB + NB), tiles(2 * cap), parts(cap), parts(cap), parts(cap)],
            name=f"ahead{step}",
        )(own, table, rates, levels, levall, partner, state)
        sums, plan = outs[:2]
        ins = (got, levels, state, sums, plan)
        specs = [VMEM, SMEM, VMEM, VMEM, SMEM]
        if step > 1:
            ins += (masses, before)
            specs += [VMEM, SMEM]
        if step == 2:
            ins += (outs[2],)
            specs += [VMEM]
        pay_shape = array(everyone if step < 3 else columns_, 1, (0, 384, 384, 1152)[step])
        out_shape = {
            1: (state_shape, pay_shape, array(8, 8, everyone)), 2: (state_shape, pay_shape), 3: (pay_shape,),
        }[step]
        outs = pl.pallas_call(
            functools.partial(after_kernel, step),
            out_shape=out_shape,
            in_specs=specs,
            out_specs=tuple(VMEM for _ in out_shape),
            scratch_shapes=[
                parts(cap), parts(cap), parts(cap), tiles(2 * cap), pltpu.VMEM((lanes // 8, 8, everyone), F32),
            ],
            name=f"after{step}",
        )(*ins)
        if step == 1:
            state, pay, masses = outs
            before = plan
        elif step == 2:
            state, pay = outs
        else:
            (pay,) = outs
    got = exchange(pay, "grp")
    shape = array(6, W)
    return tuple(
        pl.pallas_call(
            last_kernel,
            out_shape=(shape, shape, shape),
            in_specs=[VMEM, VMEM, VMEM, VMEM, SMEM],
            out_specs=(VMEM, VMEM, VMEM),
            name="last",
        )(got, phase_space, force_rates, irregular, plan)
    )


def solution(mesh):
    in_specs = (
        P(None, "blk"), P(None, "blk"), P(None, "blk"), P("blk"), P("blk"), P(None, "blk"), P("blk"),
    )
    out_specs = (P(None, "blk"), P(None, "blk"), P(None, "blk"))
    return jax.shard_map(body, mesh=mesh, in_specs=in_specs, out_specs=out_specs, check_vma=False)
```

```python
import functools
import jax
import jax.numpy as jnp
from jax import lax
from jax.experimental import pallas as pl
from jax.experimental.pallas import tpu as pltpu
from jax.sharding import PartitionSpec as P

WIDE = 0.04
CLOSE = 0.0001
TICK = 0.125
NB = 16
BS = 128
W = NB * BS
F32 = jnp.float32
CAPS = (4, 6, 4, 8)
TOP = (0, 1, 0, 2)
SENT = (-1, 0, 1, 1)
SLOTS = (0, 4, 8, 8)

VMEM = pl.BlockSpec(memory_space=pltpu.VMEM)
SMEM = pl.BlockSpec(memory_space=pltpu.SMEM)


def pair(target, source, mass, soften, acc):
    r = [source[c] - target[c] for c in range(3)]
    w = [source[c] - target[c] for c in range(3, 6)]
    d = (r[0] * r[0] + soften) + r[1] * r[1] + r[2] * r[2]
    s = lax.rsqrt(d)
    s2 = s * s
    weight = (mass * s) * s2
    q = (r[0] * w[0] + r[1] * w[1] + r[2] * w[2]) * (s2 * 3.0)
    acc = list(acc)
    for c in range(3):
        acc[c] = acc[c] + weight * r[c]
        acc[3 + c] = acc[3 + c] + weight * (w[c] - q * r[c])
    return tuple(acc)


def pair_split(target, source, mass, acc):
    r = [source[c] - target[c] for c in range(3)]
    w = [source[c] - target[c] for c in range(3, 6)]
    dd = r[0] * r[0] + r[1] * r[1] + r[2] * r[2]
    rw = (r[0] * w[0] + r[1] * w[1] + r[2] * w[2]) * 3.0
    acc = list(acc)
    for soften, sign in ((CLOSE, 1.0), (WIDE, -1.0)):
        s = lax.rsqrt(dd + soften)
        s2 = s * s
        weight = (mass * s) * (s2 * sign)
        q = rw * s2
        for c in range(3):
            acc[c] = acc[c] + weight * r[c]
            acc[3 + c] = acc[3 + c] + weight * (w[c] - q * r[c])
    return tuple(acc)


def zeros():
    return tuple(jnp.zeros((8, 128), F32) for _ in range(6))


BLOCK, PLACE, LEVEL, SHARD, ROW, HERE, COUNT = range(7)


def fill_slots(lev, top, cap, plan):
    for s in range(cap):
        plan[BLOCK, s] = 0
        plan[PLACE, s] = -1000
        plan[LEVEL, s] = 0
    count = jnp.int32(0)
    ones = [jnp.int32(0), jnp.int32(4)]
    for k in range(NB):
        level = lev[k]
        live = level <= top
        place = jnp.where(level == 0, ones[0], jnp.where(level == 1, ones[1], -1000))
        plan[BLOCK, count] = k
        plan[PLACE, count] = jnp.where(live, place, -1000)
        plan[LEVEL, count] = jnp.where(live, level, 0)
        count = count + live.astype(jnp.int32)
        ones[0] = ones[0] + (level == 0).astype(jnp.int32)
        ones[1] = ones[1] + (level == 1).astype(jnp.int32)
    plan[COUNT, 0] = count


def fill_near(plan, cap, own, levall, partner, sent):
    def slot(s, _):
        k = plan[BLOCK, s]
        q = partner[k] // NB
        level = levall[q, k]
        place = jnp.where(level == 0, 0, 4)
        for e in range(NB):
            place = place + ((levall[q, e] == level) & (e < k)).astype(jnp.int32)
        ours = plan[LEVEL, s] <= sent
        theirs = (q != own) & (level <= sent)
        for e, (b, row, here) in enumerate(((own, plan[PLACE, s], ours), (q, place, theirs))):
            plan[SHARD, 2 * s + e] = b
            plan[ROW, 2 * s + e] = jnp.clip(jnp.where(here, row, 0), 0, 3 if sent == 0 else 7)
            plan[HERE, 2 * s + e] = here.astype(jnp.int32)
        return 0

    lax.fori_loop(0, cap, slot, 0)


def span_of(level):
    return jnp.where(level == 0, TICK, jnp.where(level == 1, 2 * TICK, 4 * TICK)).astype(F32)


XS, MS, VS, AS, JS = (0, 1, 2), 3, (4, 5, 6), (8, 9, 10), (11, 12, 13)


def columns(tile):
    return tuple(
        [tile[:, c : c + 1] for c in group] for group in (XS, VS, AS, JS)
    )


def forecast(x, v, a, j, t):
    t2 = t * t * 0.5
    t3 = t * t * t * (1.0 / 6.0)
    xp = [x[c] + v[c] * t + a[c] * t2 + j[c] * t3 for c in range(3)]
    vp = [v[c] + a[c] * t + j[c] * t2 for c in range(3)]
    return xp + vp


class Forecast:
    def __init__(self, t):
        row = lax.broadcasted_iota(jnp.int32, (8, 128), 0)
        zero = jnp.zeros((8, 128), F32)
        low = row < 3
        high = (row > 3) & (row < 7)
        t2 = t * t * 0.5
        t3 = t * t * t / 6.0
        self.c1 = jnp.where(low, t, zero)
        self.c2 = jnp.where(low | high, t2, zero)
        self.c3 = jnp.where(low, t3, jnp.where(high, t, zero))

    def __call__(self, table, rates, b, k):
        first = table[b, pl.ds(7 * k, 8), :]
        second = rates[b, pl.ds(pl.multiple_of(8 * k, 8), 8), :]
        value = first + self.c1 * pltpu.roll(first, 4, 0)
        return value + self.c2 * second + self.c3 * pltpu.roll(second, 4, 0)


def fill_sources(table, rates, predicted, ahead, levall, sent):
    def shard(b, count):
        for k in range(NB):
            predicted[count] = ahead(table, rates, b, k)
            count = count + (levall[b, k] > sent).astype(jnp.int32)
        return count

    count = lax.fori_loop(0, table.shape[0], shard, jnp.int32(0))
    for e in range(NB):
        predicted[count + e] = jnp.zeros((8, 128), F32)
    return count


def target_of(state, plan, s):
    x, v, a, j = columns(state[plan[BLOCK, s]])
    ahead = forecast(x, v, a, j, span_of(plan[LEVEL, s]))
    return [jnp.broadcast_to(value, (8, 128)) for value in ahead]


def broad(row):
    return jnp.broadcast_to(row, (8, 128))


def tile_rows(tiles, at, start=0):
    rows = [broad(tiles[at, pl.ds(start + r, 1), :]) for r in (0, 1, 2, 4, 5, 6)]
    return rows, broad(tiles[at, pl.ds(start + 3, 1), :])


def slot_pairs(cap, state, plan, sweep, prepare, close, sink, carry):
    def two(p, carry):
        goal = [target_of(state, plan, 2 * p + e) for e in range(2)]
        prepare(p)
        acc = sweep(goal)
        for e in range(2):
            s = 2 * p + e
            near = zeros()
            for part in range(2):
                rows, mass, wanted = close(s, e, part)
                near = pair_split(goal[e], rows, mass * jnp.where(wanted, 1.0, 0.0).astype(F32), near)
            total, inner = (
                [jnp.sum(value, axis=1, keepdims=True) for value in group] for group in (acc[e], near)
            )
            carry = sink(s, total, inner, carry)
        return carry

    return lax.fori_loop(0, cap // 2, two, carry)


def sweep_table(groups, load):
    def sweep(goal):
        def group(b, acc):
            for k in range(NB):
                rows, mass = load(b, k)
                acc = tuple(pair(goal[e], rows, mass, WIDE, acc[e]) for e in range(2))
            return acc

        return lax.fori_loop(0, groups, group, (zeros(), zeros()))

    return sweep


def fill_received(got, turned):
    senders, _, lanes = got.shape
    for t in range(lanes // 128):
        for half in range(senders // 128):
            part = got[pl.ds(half * 128, 128), 0, pl.ds(t * 128, 128)]
            turned[pl.ds(t * 16, 16), :, pl.ds(half * 128, 128)] = part.T.reshape(16, 8, 128)


def sweep_received(turned, mass, slots_in, used):
    def sweep(goal):
        def slot(s, acc):
            for i in range(8):
                for half in range(turned.shape[2] // 128):
                    at = pl.ds(half * 128, 128)
                    rows = [broad(turned[f * slots_in + s, i : i + 1, at]) for f in range(6)]
                    m = broad(mass[s, i : i + 1, at])
                    acc = tuple(pair(goal[e], rows, m, WIDE, acc[e]) for e in range(2))
            return acc

        return lax.fori_loop(0, used, slot, (zeros(), zeros()))

    return sweep


def gather_blocks(turned, mass, slots_in, plan, near, p):
    lane = lax.broadcasted_iota(jnp.int32, (8, 128), 1)
    row = lax.broadcasted_iota(jnp.int32, (8, 128), 0)
    keep = lane // 16 == row
    for item in range(4):
        b = plan[SHARD, 4 * p + item]
        place = plan[ROW, 4 * p + item]
        half = pl.ds(pl.multiple_of((b // 8) * 128, 128), 128)
        shift = lax.rem(128 - lax.rem(b, 8) * 16, 128)
        for r, f in ((0, 0), (1, 1), (2, 2), (4, 3), (5, 4), (6, 5), (3, None)):
            tile = mass[place, :, half] if f is None else turned[f * slots_in + place, :, half]
            tile = pltpu.roll(pltpu.roll(tile, shift, 1), 0, 1, stride=16, stride_axis=0)
            near[item, r : r + 1, :] = jnp.sum(jnp.where(keep, tile, 0.0), axis=0, keepdims=True)


def fill_tiles(parts, tiles, width):
    per = 128 // width
    tiles = list(tiles)
    lane = lax.broadcasted_iota(jnp.int32, (8, 128), 1)
    for f, slot, column in parts:
        t = f // per
        tiles[t] = jnp.where(lane == (f % per) * width + slot * 8, column, tiles[t])
    return tiles


def blank(count):
    return [jnp.zeros((8, 128), F32) for _ in range(count)]


def place_tiles(tiles):
    tiles = [pltpu.roll(tile, 0, 1, stride=1, stride_axis=0) for tile in tiles]
    return [jnp.sum(tile, axis=0, keepdims=True) for tile in tiles]


def send(tiles, pay):
    for t, tile in enumerate(tiles):
        full = jnp.broadcast_to(tile[None], (pay.shape[0], 1, 128))
        pay[:, :, pl.ds(t * 128, 128)] = full


def corrector(step, state, plan, sums):
    lane = lax.broadcasted_iota(jnp.int32, (8, 128), 1)

    def sink(s, total, inner, carry):
        k = plan[BLOCK, s]
        t = span_of(plan[LEVEL, s])
        tile = state[k]
        x, v, a, j = columns(tile)
        if sums is not None:
            before = sums[s]
            total = [total[c] + before[:, c : c + 1] for c in range(6)]
            inner = [inner[c] + before[:, 8 + c : 9 + c] for c in range(6)]
        total = [total[c] + inner[c] for c in range(6)]
        half = t * 0.5
        twelfth = t * t * (1.0 / 12.0)
        v1 = [v[c] + (a[c] + total[c]) * half + (j[c] - total[3 + c]) * twelfth for c in range(3)]
        x1 = [x[c] + (v[c] + v1[c]) * half + (a[c] - total[c]) * twelfth for c in range(3)]
        if step == 3:
            parts = [(f, s, column) for f, column in enumerate(x1 + v1 + total + inner)]
            return tuple(fill_tiles(parts, carry, 64))
        fresh = tile
        for at, column in zip(XS + VS + AS + JS, x1 + v1 + total):
            fresh = jnp.where(lane == at, column, fresh)
        state[jnp.where(s < plan[COUNT, 0], k, NB)] = fresh
        ahead = forecast(x1, v1, total[:3], total[3:], TICK)
        if step == 0:
            ahead = ahead + [tile[:, MS : MS + 1]]
        parts = [(f, plan[PLACE, s], column) for f, column in enumerate(ahead)]
        return tuple(fill_tiles(parts, carry, 32 if step == 0 else 64))

    return sink


def fill_later(state, lev, later):
    parts = []
    seen = jnp.int32(4)
    for k in range(NB):
        one = lev[k] == 1
        mark = jnp.where(one, seen, -1000)
        x, v, a, j = columns(state[k])
        for f, column in enumerate(forecast(x, v, a, j, 2 * TICK)):
            parts.append((f, mark, column))
        seen = seen + one.astype(jnp.int32)
    for t, tile in enumerate(fill_tiles(parts, blank(3), 64)):
        later[t] = tile


def pack_kernel(ps, fr, mass, lev, first, rates, own):
    x, v, a, j = ps[0:3, :], ps[3:6, :], fr[0:3, :], fr[3:6, :]
    t2 = TICK * TICK * 0.5
    xp = x + v * TICK + a * t2 + j * (TICK * TICK * TICK / 6.0)
    vp = v + a * TICK + j * t2
    ap = a + j * TICK
    lane = lax.broadcasted_iota(jnp.int32, (8, BS), 1)
    levels = jnp.zeros((8, BS), F32)
    for k in range(NB):
        levels = jnp.where(lane == k, lev[k].astype(F32), levels)
    first[7 * NB : 7 * NB + 8, :] = levels
    blank_row = jnp.zeros((1, BS), F32)
    for k in range(NB):
        at = slice(k * BS, k * BS + BS)
        first[7 * k : 7 * k + 3, :] = xp[:, at]
        first[7 * k + 3 : 7 * k + 4, :] = mass[:, at]
        first[7 * k + 4 : 7 * k + 7, :] = vp[:, at]
        rates[0, 8 * k : 8 * k + 3, :] = ap[:, at]
        rates[0, 8 * k + 3 : 8 * k + 4, :] = blank_row
        rates[0, 8 * k + 4 : 8 * k + 7, :] = j[:, at]
        rates[0, 8 * k + 7 : 8 * k + 8, :] = blank_row
        own[k] = jnp.zeros((16, BS), F32)
        own[k, 0:3, :] = x[:, at]
        own[k, 3:4, :] = mass[:, at]
        own[k, 4:7, :] = v[:, at]
        own[k, 8:14, :] = fr[:, at]
    for b in range(1, rates.shape[0]):
        rates[b] = rates[0]


def first_kernel(me, col, table, mine, lev, partner, state, pay, turned, plan):
    me = me[0]
    col = pl.multiple_of(col[0] * 8, 8)
    fill_slots(lev, TOP[0], CAPS[0], plan)
    for k in range(NB):
        turned[k, :, 0:16] = mine[k].T
    for k in range(NB):
        state[k] = turned[k, pl.ds(col, 8), :]
    masses = []
    seen = jnp.int32(0)
    for k in range(NB):
        one = lev[k] == 1
        masses.append((7, jnp.where(one, seen, -1000), state[k][:, MS : MS + 1]))
        seen = seen + one.astype(jnp.int32)

    def close(s, e, part):
        k = plan[BLOCK, s]
        b = partner[k] // NB if part else me
        rows, mass = tile_rows(table, b, 7 * k)
        return rows, mass, b != me if part else jnp.bool_(True)

    tiles = slot_pairs(
        CAPS[0], state, plan,
        sweep_table(table.shape[0], lambda b, k: tile_rows(table, b, 7 * k)),
        lambda p: None, close, corrector(0, state, plan, None),
        tuple(fill_tiles(masses, blank(2), 32)),
    )
    send(place_tiles(tiles), pay)


def ahead_kernel(step, me, table, rates, lev, levall, partner, state, sums, plan, *rest):
    later = None
    if step == 2:
        later, *rest = rest
    predicted, near = rest
    me = me[0]
    cap = CAPS[step]
    fill_slots(lev, TOP[step], cap, plan)
    fill_near(plan, cap, me, levall, partner, SENT[step])
    ahead = Forecast(step * TICK)
    used = fill_sources(table, rates, predicted, ahead, levall, SENT[step])
    lane = lax.broadcasted_iota(jnp.int32, (8, 128), 1)

    def prepare(p):
        for item in range(4):
            k = plan[BLOCK, 2 * p + item // 2]
            near[item] = ahead(table, rates, plan[SHARD, 4 * p + item], k)

    def close(s, e, part):
        rows, mass = tile_rows(near, 2 * e + part)
        other = plan[SHARD, 2 * s + 1] != me if part else jnp.bool_(True)
        return rows, mass, other & (plan[HERE, 2 * s + part] == 0)

    def sink(s, total, inner, carry):
        tile = jnp.zeros((8, 128), F32)
        for at, group in ((0, total), (8, inner)):
            for c in range(6):
                tile = jnp.where(lane == at + c, group[c], tile)
        sums[s] = tile
        return carry

    groups = (used + NB - 1) // NB
    sweep = sweep_table(groups, lambda b, k: tile_rows(predicted, b * NB + k))
    slot_pairs(cap, state, plan, sweep, prepare, close, sink, 0)
    if step == 2:
        fill_later(state, lev, later)
    if step == 1:

        def shard(b, most):
            here = jnp.int32(0)
            for k in range(NB):
                here = here + (levall[b, k] == 1).astype(jnp.int32)
            return jnp.maximum(most, here)

        plan[COUNT, 1] = lax.fori_loop(0, table.shape[0], shard, jnp.int32(0))


def after_kernel(step, got, state_in, sums, plan, *rest):
    later = None
    used = SLOTS[step]
    if step > 1:
        masses, before, *rest = rest
        used = jnp.minimum(4 + before[COUNT, 1], used)
    if step == 2:
        later, *rest = rest
    if step == 3:
        state = state_in
    else:
        state, *rest = rest
    pay, *rest = rest
    if step == 1:
        masses, *rest = rest
    near, turned = rest
    if step < 3:
        state[...] = state_in[...]
    fill_received(got, turned)
    if step == 1:
        masses[0:4] = turned[24:28]
        masses[4:8] = turned[28:32]

    def close(s, e, part):
        rows, mass = tile_rows(near, 2 * e + part)
        return rows, mass, plan[HERE, 2 * s + part] == 1

    tiles = slot_pairs(
        CAPS[step], state, plan,
        sweep_received(turned, masses, SLOTS[step], used),
        lambda p: gather_blocks(turned, masses, SLOTS[step], plan, near, p),
        close, corrector(step, state, plan, sums),
        tuple([later[t] for t in range(3)] if step == 2 else blank(9 if step == 3 else 3)),
    )
    send(place_tiles(tiles), pay)


def last_kernel(got, ps, fr, irr, plan, kin, comb, close):
    count = plan[COUNT, 0]
    kin[...] = ps[...]
    comb[...] = fr[...]
    close[...] = irr[...]
    senders = got.shape[0]
    lane = lax.broadcasted_iota(jnp.int32, (senders, 128), 1)
    row = lax.broadcasted_iota(jnp.int32, (senders, 128), 0)
    spread = [pltpu.roll(got[:, 0, pl.ds(t * 128, 128)], 0, 1, stride=8, stride_axis=0) for t in range(9)]
    for s in range(CAPS[3]):
        rows = []
        for f in range(18):
            t, e = divmod(f, 2)
            start = e * 64 + s * 8
            keep = (lane + (128 - start)) % 128 // 8 == row
            value = jnp.sum(jnp.where(keep, spread[t], 0.0), axis=0, keepdims=True)
            rows.append(pltpu.roll(value, (128 - start) % 128, 1))
        at = pl.ds(pl.multiple_of(plan[BLOCK, s] * BS, BS), BS)

        @pl.when(s < count)
        def _(at=at, rows=rows):
            for f, value in enumerate(rows):
                out = (kin, comb, close)[f // 6]
                out[f % 6 : f % 6 + 1, at] = value


def body(phase_space, force_rates, irregular, stellar_masses, levels, active, partner):
    shards = lax.axis_size("blk")
    columns_ = lax.axis_size("grp")
    everyone = shards * columns_
    me = lax.axis_index("blk").astype(jnp.int32).reshape(1)
    col = lax.axis_index("grp").astype(jnp.int32).reshape(1)
    tiles = lambda count: pltpu.VMEM((count, 8, 128), F32)
    array = lambda *shape: jax.ShapeDtypeStruct(shape, F32)
    plan_shape = jax.ShapeDtypeStruct((8, 32), jnp.int32)
    state_shape = array(NB + 1, 8, 128)

    def exchange(pay, axis):
        return lax.all_to_all(pay, axis, split_axis=0, concat_axis=0, tiled=True)

    packed, rates, mine = pl.pallas_call(
        pack_kernel,
        out_shape=(array(7 * NB + 8, BS), array(shards, 8 * NB, BS), array(NB, 16, BS)),
        in_specs=[VMEM, VMEM, VMEM, SMEM],
        out_specs=(VMEM, VMEM, VMEM),
        name="pack",
    )(phase_space, force_rates, stellar_masses[None, :], levels)
    table = lax.all_gather(packed, "blk", axis=0, tiled=False)
    levall = table[:, 7 * NB, :NB].astype(jnp.int32)
    table, rates = lax.optimization_barrier((table, rates))
    rates = exchange(rates, "blk")
    state, pay = pl.pallas_call(
        first_kernel,
        out_shape=(state_shape, array(everyone, 1, 256)),
        in_specs=[SMEM, SMEM, VMEM, VMEM, SMEM, SMEM],
        out_specs=(VMEM, VMEM),
        scratch_shapes=[pltpu.VMEM((NB, 128, 128), F32), pltpu.SMEM((8, 32), jnp.int32)],
        name="first",
    )(me, col, table, mine, levels, partner)
    masses = before = None
    for step in (1, 2, 3):
        cap = CAPS[step]
        lanes = (0, 256, 384, 384)[step]
        got = exchange(pay, ("blk", "grp"))
        outs = pl.pallas_call(
            functools.partial(ahead_kernel, step),
            out_shape=(array(cap, 8, 128), plan_shape) + ((array(3, 8, 128),) if step == 2 else ()),
            in_specs=[SMEM, VMEM, VMEM, SMEM, SMEM, SMEM, VMEM],
            out_specs=(VMEM, SMEM) + ((VMEM,) if step == 2 else ()),
            scratch_shapes=[tiles(shards * NB + NB), tiles(4)],
            name=f"ahead{step}",
        )(me, table, rates, levels, levall, partner, state)
        sums, plan = outs[:2]
        ins = (got, state, sums, plan)
        specs = [VMEM, VMEM, VMEM, SMEM]
        if step > 1:
            ins += (masses, before)
            specs += [VMEM, SMEM]
        if step == 2:
            ins += (outs[2],)
            specs += [VMEM]
        pay_shape = array(everyone if step < 3 else columns_, 1, (0, 384, 384, 1152)[step])
        out_shape = {
            1: (state_shape, pay_shape, array(8, 8, everyone)), 2: (state_shape, pay_shape), 3: (pay_shape,),
        }[step]
        outs = pl.pallas_call(
            functools.partial(after_kernel, step),
            out_shape=out_shape,
            in_specs=specs,
            out_specs=tuple(VMEM for _ in out_shape),
            scratch_shapes=[
                tiles(4),
                pltpu.VMEM((lanes // 8, 8, everyone), F32),
            ],
            name=f"after{step}",
        )(*ins)
        if step == 1:
            state, pay, masses = outs
            before = plan
        elif step == 2:
            state, pay = outs
        else:
            (pay,) = outs
    got = exchange(pay, "grp")
    shape = array(6, W)
    return tuple(
        pl.pallas_call(
            last_kernel,
            out_shape=(shape, shape, shape),
            in_specs=[VMEM, VMEM, VMEM, VMEM, SMEM],
            out_specs=(VMEM, VMEM, VMEM),
            name="last",
        )(got, phase_space, force_rates, irregular, plan)
    )


def solution(mesh):
    in_specs = (
        P(None, "blk"), P(None, "blk"), P(None, "blk"), P("blk"), P("blk"), P(None, "blk"), P("blk"),
    )
    out_specs = (P(None, "blk"), P(None, "blk"), P(None, "blk"))
    return jax.shard_map(body, mesh=mesh, in_specs=in_specs, out_specs=out_specs, check_vma=False)
```

```python
import functools
import jax
import jax.numpy as jnp
from jax import lax
from jax.experimental import pallas as pl
from jax.experimental.pallas import tpu as pltpu
from jax.sharding import PartitionSpec as P

WIDE = 0.04
CLOSE = 0.0001
TICK = 0.125
NB = 16
BS = 128
W = NB * BS
F32 = jnp.float32
CAPS = (4, 6, 4, 8)
TOP = (0, 1, 0, 2)
SENT = (-1, 0, 1, 1)
SLOTS = (0, 4, 8, 8)

VMEM = pl.BlockSpec(memory_space=pltpu.VMEM)
SMEM = pl.BlockSpec(memory_space=pltpu.SMEM)


def pair(target, source, mass, soften, acc):
    r = [source[c] - target[c] for c in range(3)]
    w = [source[c] - target[c] for c in range(3, 6)]
    d = (r[0] * r[0] + soften) + r[1] * r[1] + r[2] * r[2]
    s = lax.rsqrt(d)
    s2 = s * s
    weight = (mass * s) * s2
    q = (r[0] * w[0] + r[1] * w[1] + r[2] * w[2]) * (s2 * 3.0)
    acc = list(acc)
    for c in range(3):
        acc[c] = acc[c] + weight * r[c]
        acc[3 + c] = acc[3 + c] + weight * (w[c] - q * r[c])
    return tuple(acc)


def pair_split(target, source, mass, acc):
    r = [source[c] - target[c] for c in range(3)]
    w = [source[c] - target[c] for c in range(3, 6)]
    dd = r[0] * r[0] + r[1] * r[1] + r[2] * r[2]
    rw = (r[0] * w[0] + r[1] * w[1] + r[2] * w[2]) * 3.0
    acc = list(acc)
    for soften, sign in ((CLOSE, 1.0), (WIDE, -1.0)):
        s = lax.rsqrt(dd + soften)
        s2 = s * s
        weight = (mass * s) * (s2 * sign)
        q = rw * s2
        for c in range(3):
            acc[c] = acc[c] + weight * r[c]
            acc[3 + c] = acc[3 + c] + weight * (w[c] - q * r[c])
    return tuple(acc)


def zeros():
    return tuple(jnp.zeros((8, 128), F32) for _ in range(6))


BLOCK, PLACE, LEVEL, SHARD, ROW, HERE, COUNT = range(7)


def fill_slots(lev, top, cap, plan):
    for s in range(cap):
        plan[BLOCK, s] = 0
        plan[PLACE, s] = -1000
        plan[LEVEL, s] = 0
    count = jnp.int32(0)
    for group in ((2,), (0, 1)) if top == 2 else ((0, 1),):
        ones = [jnp.int32(0), jnp.int32(4)]
        for k in range(NB):
            level = lev[k]
            place = jnp.where(level == 0, ones[0], jnp.where(level == 1, ones[1], -1000))
            live = (level == 2) if group == (2,) else level <= min(top, 1)
            plan[BLOCK, count] = k
            plan[PLACE, count] = jnp.where(live, place, -1000)
            plan[LEVEL, count] = jnp.where(live, level, 0)
            count = count + live.astype(jnp.int32)
            ones[0] = ones[0] + (level == 0).astype(jnp.int32)
            ones[1] = ones[1] + (level == 1).astype(jnp.int32)
        if group == (2,):
            plan[COUNT, 2] = count
    plan[COUNT, 0] = count


def fill_near(plan, cap, own, levall, partner, sent):
    def slot(s, _):
        k = plan[BLOCK, s]
        q = partner[k] // NB
        level = levall[q, k]
        place = jnp.where(level == 0, 0, 4)
        for e in range(NB):
            place = place + ((levall[q, e] == level) & (e < k)).astype(jnp.int32)
        ours = plan[LEVEL, s] <= sent
        theirs = (q != own) & (level <= sent)
        for e, (b, row, here) in enumerate(((own, plan[PLACE, s], ours), (q, place, theirs))):
            plan[SHARD, 2 * s + e] = b
            plan[ROW, 2 * s + e] = jnp.clip(jnp.where(here, row, 0), 0, 3 if sent == 0 else 7)
            plan[HERE, 2 * s + e] = here.astype(jnp.int32)
        return 0

    lax.fori_loop(0, cap, slot, 0)


def span_of(level):
    return jnp.where(level == 0, TICK, jnp.where(level == 1, 2 * TICK, 4 * TICK)).astype(F32)


XS, MS, VS, AS, JS = (0, 1, 2), 3, (4, 5, 6), (8, 9, 10), (11, 12, 13)


def columns(tile):
    return tuple(
        [tile[:, c : c + 1] for c in group] for group in (XS, VS, AS, JS)
    )


def forecast(x, v, a, j, t):
    t2 = t * t * 0.5
    t3 = t * t * t * (1.0 / 6.0)
    xp = [x[c] + v[c] * t + a[c] * t2 + j[c] * t3 for c in range(3)]
    vp = [v[c] + a[c] * t + j[c] * t2 for c in range(3)]
    return xp + vp


QUANTITIES = 7


def fill_sources(table, rates, predicted, t):
    t2 = t * t * 0.5
    t3 = t * t * t / 6.0

    def shard(b, _):
        x, m, v = [[table[b, pl.ds(NB * f, NB), :] for f in group] for group in ((0, 1, 2), (3,), (4, 5, 6))]
        a, j = [[rates[b, pl.ds(NB * f, NB), :] for f in group] for group in ((0, 1, 2), (3, 4, 5))]
        for c in range(3):
            predicted[b, c] = x[c] + v[c] * t + a[c] * t2 + j[c] * t3
            predicted[b, 4 + c] = v[c] + a[c] * t + j[c] * t2
        predicted[b, 3] = m[0]
        return 0

    lax.fori_loop(0, table.shape[0], shard, 0)
    for f in range(QUANTITIES):
        predicted[table.shape[0], f] = jnp.zeros((NB, BS), F32)


def fill_order(levall, sent, order):
    shards = levall.shape[0]

    def shard(b, count):
        for k in range(NB):
            order[count] = b * NB + k
            count = count + (levall[b, k] > sent).astype(jnp.int32)
        return count

    count = lax.fori_loop(0, shards, shard, jnp.int32(0))
    for e in range(NB):
        order[count + e] = shards * NB
    order[(shards + 2) * NB] = count


def target_of(state, plan, s):
    x, v, a, j = columns(state[plan[BLOCK, s]])
    ahead = forecast(x, v, a, j, span_of(plan[LEVEL, s]))
    return [jnp.broadcast_to(value, (8, 128)) for value in ahead]


def broad(row):
    return jnp.broadcast_to(row, (8, 128))


def tile_rows(tile):
    return [broad(tile(r)) for r in (0, 1, 2, 4, 5, 6)], broad(tile(3))


def from_table(table, b, k):
    return tile_rows(lambda r: table[b, pl.ds(NB * r + k, 1), :])


def from_predicted(predicted, b, k):
    return tile_rows(lambda r: predicted[b, r, pl.ds(k, 1), :])


def slot_pairs(first, last, state, plan, sweep, prepare, close, sink, carry):
    def two(p, carry):
        goal = [target_of(state, plan, 2 * p + e) for e in range(2)]
        prepare(p)
        acc = sweep(goal)
        for e in range(2):
            s = 2 * p + e
            near = zeros()
            for part in range(2):
                rows, mass, wanted = close(s, e, part)
                near = pair_split(goal[e], rows, mass * jnp.where(wanted, 1.0, 0.0).astype(F32), near)
            total, inner = (
                [jnp.sum(value, axis=1, keepdims=True) for value in group] for group in (acc[e], near)
            )
            carry = sink(s, total, inner, carry)
        return carry

    return lax.fori_loop(first, last, two, carry)


def pairs_of(plan):
    return (plan[COUNT, 0] + 1) // 2


def sweep_table(groups, load):
    def sweep(goal):
        def group(b, acc):
            for k in range(NB):
                rows, mass = load(b, k)
                acc = tuple(pair(goal[e], rows, mass, WIDE, acc[e]) for e in range(2))
            return acc

        return lax.fori_loop(0, groups, group, (zeros(), zeros()))

    return sweep


def fill_received(got, turned):
    senders, _, lanes = got.shape
    for t in range(lanes // 128):
        for half in range(senders // 128):
            part = got[pl.ds(half * 128, 128), 0, pl.ds(t * 128, 128)]
            turned[pl.ds(t * 16, 16), :, pl.ds(half * 128, 128)] = part.T.reshape(16, 8, 128)


def sweep_received(turned, mass, slots_in, used):
    def sweep(goal):
        def slot(s, acc):
            for i in range(8):
                for half in range(turned.shape[2] // 128):
                    at = pl.ds(half * 128, 128)
                    rows = [broad(turned[f * slots_in + s, i : i + 1, at]) for f in range(6)]
                    m = broad(mass[s, i : i + 1, at])
                    acc = tuple(pair(goal[e], rows, m, WIDE, acc[e]) for e in range(2))
            return acc

        return lax.fori_loop(0, used, slot, (zeros(), zeros()))

    return sweep


def gather_blocks(turned, mass, slots_in, plan, near, p):
    lane = lax.broadcasted_iota(jnp.int32, (8, 128), 1)
    row = lax.broadcasted_iota(jnp.int32, (8, 128), 0)
    keep = lane // 16 == row
    for item in range(4):
        b = plan[SHARD, 4 * p + item]
        place = plan[ROW, 4 * p + item]
        half = pl.ds(pl.multiple_of((b // 8) * 128, 128), 128)
        shift = lax.rem(128 - lax.rem(b, 8) * 16, 128)
        for r, f in ((0, 0), (1, 1), (2, 2), (4, 3), (5, 4), (6, 5), (3, None)):
            tile = mass[place, :, half] if f is None else turned[f * slots_in + place, :, half]
            tile = pltpu.roll(pltpu.roll(tile, shift, 1), 0, 1, stride=16, stride_axis=0)
            near[item, r : r + 1, :] = jnp.sum(jnp.where(keep, tile, 0.0), axis=0, keepdims=True)


def fill_tiles(parts, tiles, width):
    per = 128 // width
    tiles = list(tiles)
    lane = lax.broadcasted_iota(jnp.int32, (8, 128), 1)
    for f, slot, column in parts:
        t = f // per
        tiles[t] = jnp.where(lane == (f % per) * width + slot * 8, column, tiles[t])
    return tiles


def blank(count):
    return [jnp.zeros((8, 128), F32) for _ in range(count)]


def place_tiles(tiles):
    tiles = [pltpu.roll(tile, 0, 1, stride=1, stride_axis=0) for tile in tiles]
    return [jnp.sum(tile, axis=0, keepdims=True) for tile in tiles]


def send(tiles, pay):
    for t, tile in enumerate(tiles):
        full = jnp.broadcast_to(tile[None], (pay.shape[0], 1, 128))
        pay[:, :, pl.ds(t * 128, 128)] = full


def corrector(step, state, plan, sums):
    lane = lax.broadcasted_iota(jnp.int32, (8, 128), 1)

    def sink(s, total, inner, carry):
        k = plan[BLOCK, s]
        t = span_of(plan[LEVEL, s])
        tile = state[k]
        x, v, a, j = columns(tile)
        if sums is not None:
            before = sums[s]
            total = [total[c] + before[:, c : c + 1] for c in range(6)]
            inner = [inner[c] + before[:, 8 + c : 9 + c] for c in range(6)]
        total = [total[c] + inner[c] for c in range(6)]
        half = t * 0.5
        twelfth = t * t * (1.0 / 12.0)
        v1 = [v[c] + (a[c] + total[c]) * half + (j[c] - total[3 + c]) * twelfth for c in range(3)]
        x1 = [x[c] + (v[c] + v1[c]) * half + (a[c] - total[c]) * twelfth for c in range(3)]
        if step == 3:
            parts = [(f, s, column) for f, column in enumerate(x1 + v1 + total + inner)]
            return tuple(fill_tiles(parts, carry, 64))
        fresh = tile
        for at, column in zip(XS + VS + AS + JS, x1 + v1 + total):
            fresh = jnp.where(lane == at, column, fresh)
        state[jnp.where(s < plan[COUNT, 0], k, NB)] = fresh
        ahead = forecast(x1, v1, total[:3], total[3:], TICK)
        if step == 0:
            ahead = ahead + [tile[:, MS : MS + 1]]
        parts = [(f, plan[PLACE, s], column) for f, column in enumerate(ahead)]
        return tuple(fill_tiles(parts, carry, 32 if step == 0 else 64))

    return sink


def fill_later(state, lev, later):
    parts = []
    seen = jnp.int32(4)
    for k in range(NB):
        one = lev[k] == 1
        mark = jnp.where(one, seen, -1000)
        x, v, a, j = columns(state[k])
        for f, column in enumerate(forecast(x, v, a, j, 2 * TICK)):
            parts.append((f, mark, column))
        seen = seen + one.astype(jnp.int32)
    for t, tile in enumerate(fill_tiles(parts, blank(3), 64)):
        later[t] = tile


def pack_kernel(ps, fr, mass, lev, first, rates, own):
    x, v, a, j = ps[0:3, :], ps[3:6, :], fr[0:3, :], fr[3:6, :]
    t2 = TICK * TICK * 0.5
    xp = x + v * TICK + a * t2 + j * (TICK * TICK * TICK / 6.0)
    vp = v + a * TICK + j * t2
    ap = a + j * TICK
    lane = lax.broadcasted_iota(jnp.int32, (8, BS), 1)
    levels = jnp.zeros((8, BS), F32)
    for k in range(NB):
        levels = jnp.where(lane == k, lev[k].astype(F32), levels)
    first[7 * NB : 7 * NB + 8, :] = levels
    for k in range(NB):
        at = slice(k * BS, k * BS + BS)
        for c in range(3):
            first[NB * c + k : NB * c + k + 1, :] = xp[c : c + 1, at]
            first[NB * (4 + c) + k : NB * (4 + c) + k + 1, :] = vp[c : c + 1, at]
            rates[0, NB * c + k : NB * c + k + 1, :] = ap[c : c + 1, at]
            rates[0, NB * (3 + c) + k : NB * (3 + c) + k + 1, :] = j[c : c + 1, at]
        first[NB * 3 + k : NB * 3 + k + 1, :] = mass[:, at]
        own[k] = jnp.zeros((16, BS), F32)
        own[k, 0:3, :] = x[:, at]
        own[k, 3:4, :] = mass[:, at]
        own[k, 4:7, :] = v[:, at]
        own[k, 8:14, :] = fr[:, at]
    for b in range(1, rates.shape[0]):
        rates[b] = rates[0]


def first_kernel(me, col, table, mine, lev, levall, partner, state, pay, turned, plan):
    me = me[0]
    col = pl.multiple_of(col[0] * 8, 8)
    fill_slots(lev, TOP[0], CAPS[0], plan)
    for k in range(NB):
        turned[k, :, 0:16] = mine[k].T
    for k in range(NB):
        state[k] = turned[k, pl.ds(col, 8), :]
    masses = []
    seen = jnp.int32(0)
    for k in range(NB):
        one = lev[k] == 1
        masses.append((7, jnp.where(one, seen, -1000), state[k][:, MS : MS + 1]))
        seen = seen + one.astype(jnp.int32)

    def close(s, e, part):
        k = plan[BLOCK, s]
        b = partner[k] // NB if part else me
        rows, mass = from_table(table, b, k)
        return rows, mass, b != me if part else jnp.bool_(True)

    tiles = slot_pairs(
        0, pairs_of(plan), state, plan,
        sweep_table(table.shape[0], lambda b, k: from_table(table, b, k)),
        lambda p: None, close, corrector(0, state, plan, None),
        tuple(fill_tiles(masses, blank(2), 32)),
    )
    send(place_tiles(tiles), pay)


def ahead_sums(step, first, last, me, plan, order, predicted, state, sums):
    lane = lax.broadcasted_iota(jnp.int32, (8, 128), 1)

    def load(g, e):
        index = order[g * NB + e]
        return from_predicted(predicted, index // NB, lax.rem(index, NB))

    def close(s, e, part):
        rows, mass = from_predicted(predicted, plan[SHARD, 2 * s + part], plan[BLOCK, s])
        other = plan[SHARD, 2 * s + 1] != me if part else jnp.bool_(True)
        return rows, mass, other & (plan[HERE, 2 * s + part] == 0)

    def sink(s, total, inner, carry):
        tile = jnp.zeros((8, 128), F32)
        for at, group in ((0, total), (8, inner)):
            for c in range(6):
                tile = jnp.where(lane == at + c, group[c], tile)
        sums[s] = tile
        return carry

    groups = (order[order.shape[0] - NB] + NB - 1) // NB
    slot_pairs(first, last, state, plan, sweep_table(groups, load), lambda p: None, close, sink, 0)


def early_pairs(plan):
    return jnp.minimum(plan[COUNT, 2] // 2, 2)


def ahead_kernel(step, me, table, rates, lev, levall, partner, state, *rest):
    if step == 1:
        sums, plan, predicted, order = rest
    elif step == 2:
        sums, plan, later, early, order, predicted, plan3 = rest
    else:
        early, order, sums, plan, predicted = rest
    me = me[0]
    fill_slots(lev, TOP[step], CAPS[step], plan)
    fill_near(plan, CAPS[step], me, levall, partner, SENT[step])
    if step < 3:
        fill_order(levall, SENT[step], order)
    fill_sources(table, rates, predicted, step * TICK)
    first = 0
    if step == 3:
        first = early_pairs(plan)
        sums[0:4] = early[...]
    ahead_sums(step, first, pairs_of(plan), me, plan, order, predicted, state, sums)
    if step == 2:
        fill_later(state, lev, later)
        fill_slots(lev, TOP[3], CAPS[3], plan3)
        fill_near(plan3, CAPS[3], me, levall, partner, SENT[3])
        fill_sources(table, rates, predicted, 3 * TICK)
        early[...] = jnp.zeros((4, 8, 128), F32)
        ahead_sums(3, 0, early_pairs(plan3), me, plan3, order, predicted, state, early)
    if step == 1:

        def shard(b, most):
            here = jnp.int32(0)
            for k in range(NB):
                here = here + (levall[b, k] == 1).astype(jnp.int32)
            return jnp.maximum(most, here)

        plan[COUNT, 1] = lax.fori_loop(0, table.shape[0], shard, jnp.int32(0))


def after_kernel(step, got, state_in, sums, plan, *rest):
    later = None
    used = SLOTS[step]
    if step > 1:
        masses, before, *rest = rest
        used = jnp.minimum(4 + before[COUNT, 1], used)
    if step == 2:
        later, *rest = rest
    if step == 3:
        state = state_in
    else:
        state, *rest = rest
    pay, *rest = rest
    if step == 1:
        masses, *rest = rest
    near, turned = rest
    if step < 3:
        state[...] = state_in[...]
    fill_received(got, turned)
    if step == 1:
        masses[0:4] = turned[24:28]
        masses[4:8] = turned[28:32]

    def close(s, e, part):
        rows, mass = tile_rows(lambda r: near[2 * e + part, r : r + 1, :])
        return rows, mass, plan[HERE, 2 * s + part] == 1

    tiles = slot_pairs(
        0, pairs_of(plan), state, plan,
        sweep_received(turned, masses, SLOTS[step], used),
        lambda p: gather_blocks(turned, masses, SLOTS[step], plan, near, p),
        close, corrector(step, state, plan, sums),
        tuple([later[t] for t in range(3)] if step == 2 else blank(9 if step == 3 else 3)),
    )
    send(place_tiles(tiles), pay)


def last_kernel(got, ps, fr, irr, plan, kin, comb, close):
    count = plan[COUNT, 0]
    kin[...] = ps[...]
    comb[...] = fr[...]
    close[...] = irr[...]
    senders = got.shape[0]
    lane = lax.broadcasted_iota(jnp.int32, (senders, 128), 1)
    row = lax.broadcasted_iota(jnp.int32, (senders, 128), 0)
    spread = [pltpu.roll(got[:, 0, pl.ds(t * 128, 128)], 0, 1, stride=8, stride_axis=0) for t in range(9)]
    for s in range(CAPS[3]):
        rows = []
        for f in range(18):
            t, e = divmod(f, 2)
            start = e * 64 + s * 8
            keep = (lane + (128 - start)) % 128 // 8 == row
            value = jnp.sum(jnp.where(keep, spread[t], 0.0), axis=0, keepdims=True)
            rows.append(pltpu.roll(value, (128 - start) % 128, 1))
        at = pl.ds(pl.multiple_of(plan[BLOCK, s] * BS, BS), BS)

        @pl.when(s < count)
        def _(at=at, rows=rows):
            for f, value in enumerate(rows):
                out = (kin, comb, close)[f // 6]
                out[f % 6 : f % 6 + 1, at] = value


def body(phase_space, force_rates, irregular, stellar_masses, levels, active, partner):
    shards = lax.axis_size("blk")
    columns_ = lax.axis_size("grp")
    everyone = shards * columns_
    me = lax.axis_index("blk").astype(jnp.int32).reshape(1)
    col = lax.axis_index("grp").astype(jnp.int32).reshape(1)
    tiles = lambda count: pltpu.VMEM((count, 8, 128), F32)
    array = lambda *shape: jax.ShapeDtypeStruct(shape, F32)
    plan_shape = jax.ShapeDtypeStruct((8, 32), jnp.int32)
    state_shape = array(NB + 1, 8, 128)

    def exchange(pay, axis):
        return lax.all_to_all(pay, axis, split_axis=0, concat_axis=0, tiled=True)

    packed, rates, mine = pl.pallas_call(
        pack_kernel,
        out_shape=(array(7 * NB + 8, BS), array(shards, 6 * NB, BS), array(NB, 16, BS)),
        in_specs=[VMEM, VMEM, VMEM, SMEM],
        out_specs=(VMEM, VMEM, VMEM),
        name="pack",
    )(phase_space, force_rates, stellar_masses[None, :], levels)
    table = lax.all_gather(packed, "blk", axis=0, tiled=False)
    levall = table[:, 7 * NB, :NB].astype(jnp.int32)
    table, rates = lax.optimization_barrier((table, rates))
    rates = exchange(rates, "blk")
    state, pay = pl.pallas_call(
        first_kernel,
        out_shape=(state_shape, array(everyone, 1, 256)),
        in_specs=[SMEM, SMEM, VMEM, VMEM, SMEM, SMEM, SMEM],
        out_specs=(VMEM, VMEM),
        scratch_shapes=[pltpu.VMEM((NB, 128, 128), F32), pltpu.SMEM((8, 32), jnp.int32)],
        name="first",
    )(me, col, table, mine, levels, levall, partner)
    masses = before = None
    for step in (1, 2, 3):
        cap = CAPS[step]
        lanes = (0, 256, 384, 384)[step]
        got = exchange(pay, ("blk", "grp"))
        order_shape = ((shards + 3) * NB,)
        ins = (me, table, rates, levels, levall, partner, state)
        specs = [SMEM, VMEM, VMEM, SMEM, SMEM, SMEM, VMEM]
        out_shape = (array(cap, 8, 128), plan_shape)
        out_specs = (VMEM, SMEM)
        scratch = [pltpu.VMEM((shards + 1, QUANTITIES, NB, BS), F32)]
        if step == 1:
            scratch += [pltpu.SMEM(order_shape, jnp.int32)]
        elif step == 2:
            out_shape += (array(3, 8, 128), array(4, 8, 128), jax.ShapeDtypeStruct(order_shape, jnp.int32))
            out_specs += (VMEM, VMEM, SMEM)
            scratch += [pltpu.SMEM((8, 32), jnp.int32)]
        else:
            ins += (early, order)
            specs += [VMEM, SMEM]
        outs = pl.pallas_call(
            functools.partial(ahead_kernel, step),
            out_shape=out_shape,
            in_specs=specs,
            out_specs=out_specs,
            scratch_shapes=scratch,
            name=f"ahead{step}",
        )(*ins)
        sums, plan = outs[:2]
        if step == 2:
            early, order = outs[3:]
        ins = (got, state, sums, plan)
        specs = [VMEM, VMEM, VMEM, SMEM]
        if step > 1:
            ins += (masses, before)
            specs += [VMEM, SMEM]
        if step == 2:
            ins += (outs[2],)
            specs += [VMEM]
        pay_shape = array(everyone if step < 3 else columns_, 1, (0, 384, 384, 1152)[step])
        out_shape = {
            1: (state_shape, pay_shape, array(8, 8, everyone)), 2: (state_shape, pay_shape), 3: (pay_shape,),
        }[step]
        outs = pl.pallas_call(
            functools.partial(after_kernel, step),
            out_shape=out_shape,
            in_specs=specs,
            out_specs=tuple(VMEM for _ in out_shape),
            scratch_shapes=[
                tiles(4),
                pltpu.VMEM((lanes // 8, 8, everyone), F32),
            ],
            name=f"after{step}",
        )(*ins)
        if step == 1:
            state, pay, masses = outs
            before = plan
        elif step == 2:
            state, pay = outs
        else:
            (pay,) = outs
    got = exchange(pay, "grp")
    shape = array(6, W)
    return tuple(
        pl.pallas_call(
            last_kernel,
            out_shape=(shape, shape, shape),
            in_specs=[VMEM, VMEM, VMEM, VMEM, SMEM],
            out_specs=(VMEM, VMEM, VMEM),
            name="last",
        )(got, phase_space, force_rates, irregular, plan)
    )


def solution(mesh):
    in_specs = (
        P(None, "blk"), P(None, "blk"), P(None, "blk"), P("blk"), P("blk"), P(None, "blk"), P("blk"),
    )
    out_specs = (P(None, "blk"), P(None, "blk"), P(None, "blk"))
    return jax.shard_map(body, mesh=mesh, in_specs=in_specs, out_specs=out_specs, check_vma=False)
```

```python
import functools
import jax
import jax.numpy as jnp
from jax import lax
from jax.experimental import pallas as pl
from jax.experimental.pallas import tpu as pltpu
from jax.sharding import PartitionSpec as P

WIDE = 0.04
CLOSE = 0.0001
TICK = 0.125
NB = 16
BS = 128
W = NB * BS
F32 = jnp.float32
CAPS = (4, 6, 4, 8)
TOP = (0, 1, 0, 2)
SENT = (-1, 0, 1, 1)
SLOTS = (0, 4, 8, 8)

VMEM = pl.BlockSpec(memory_space=pltpu.VMEM)
SMEM = pl.BlockSpec(memory_space=pltpu.SMEM)


def pair(target, source, mass, soften, acc):
    r = [source[c] - target[c] for c in range(3)]
    w = [source[c] - target[c] for c in range(3, 6)]
    d = (r[0] * r[0] + soften) + r[1] * r[1] + r[2] * r[2]
    s = lax.rsqrt(d)
    s2 = s * s
    weight = (mass * s) * s2
    q = (r[0] * w[0] + r[1] * w[1] + r[2] * w[2]) * (s2 * 3.0)
    acc = list(acc)
    for c in range(3):
        acc[c] = acc[c] + weight * r[c]
        acc[3 + c] = acc[3 + c] + weight * (w[c] - q * r[c])
    return tuple(acc)


def pair_split(target, source, mass, acc):
    r = [source[c] - target[c] for c in range(3)]
    w = [source[c] - target[c] for c in range(3, 6)]
    dd = r[0] * r[0] + r[1] * r[1] + r[2] * r[2]
    rw = (r[0] * w[0] + r[1] * w[1] + r[2] * w[2]) * 3.0
    acc = list(acc)
    for soften, sign in ((CLOSE, 1.0), (WIDE, -1.0)):
        s = lax.rsqrt(dd + soften)
        s2 = s * s
        weight = (mass * s) * (s2 * sign)
        q = rw * s2
        for c in range(3):
            acc[c] = acc[c] + weight * r[c]
            acc[3 + c] = acc[3 + c] + weight * (w[c] - q * r[c])
    return tuple(acc)


def zeros():
    return tuple(jnp.zeros((8, 128), F32) for _ in range(6))


BLOCK, PLACE, LEVEL, SHARD, ROW, HERE, COUNT = range(7)


def fill_slots(lev, top, cap, plan):
    for s in range(cap):
        plan[BLOCK, s] = 0
        plan[PLACE, s] = -1000
        plan[LEVEL, s] = 0
    count = jnp.int32(0)
    for group in ((2,), (0, 1)) if top == 2 else ((0, 1),):
        ones = [jnp.int32(0), jnp.int32(4)]
        for k in range(NB):
            level = lev[k]
            place = jnp.where(level == 0, ones[0], jnp.where(level == 1, ones[1], -1000))
            live = (level == 2) if group == (2,) else level <= min(top, 1)
            plan[BLOCK, count] = k
            plan[PLACE, count] = jnp.where(live, place, -1000)
            plan[LEVEL, count] = jnp.where(live, level, 0)
            count = count + live.astype(jnp.int32)
            ones[0] = ones[0] + (level == 0).astype(jnp.int32)
            ones[1] = ones[1] + (level == 1).astype(jnp.int32)
        if group == (2,):
            plan[COUNT, 2] = count
    plan[COUNT, 0] = count


def fill_near(plan, cap, own, levall, partner, sent):
    def slot(s, _):
        k = plan[BLOCK, s]
        q = partner[k] // NB
        level = levall[q, k]
        place = jnp.where(level == 0, 0, 4)
        for e in range(NB):
            place = place + ((levall[q, e] == level) & (e < k)).astype(jnp.int32)
        ours = plan[LEVEL, s] <= sent
        theirs = (q != own) & (level <= sent)
        for e, (b, row, here) in enumerate(((own, plan[PLACE, s], ours), (q, place, theirs))):
            plan[SHARD, 2 * s + e] = b
            plan[ROW, 2 * s + e] = jnp.clip(jnp.where(here, row, 0), 0, 3 if sent == 0 else 7)
            plan[HERE, 2 * s + e] = here.astype(jnp.int32)
        return 0

    lax.fori_loop(0, cap, slot, 0)


def span_of(level):
    return jnp.where(level == 0, TICK, jnp.where(level == 1, 2 * TICK, 4 * TICK)).astype(F32)


XS, MS, VS, AS, JS = (0, 1, 2), 3, (4, 5, 6), (8, 9, 10), (11, 12, 13)


def columns(tile):
    return tuple(
        [tile[:, c : c + 1] for c in group] for group in (XS, VS, AS, JS)
    )


def forecast(x, v, a, j, t):
    t2 = t * t * 0.5
    t3 = t * t * t * (1.0 / 6.0)
    xp = [x[c] + v[c] * t + a[c] * t2 + j[c] * t3 for c in range(3)]
    vp = [v[c] + a[c] * t + j[c] * t2 for c in range(3)]
    return xp + vp


QUANTITIES = 7


def fill_sources(table, rates, predicted, t):
    t2 = t * t * 0.5
    t3 = t * t * t / 6.0

    def shard(b, _):
        x, m, v = [[table[b, pl.ds(NB * f, NB), :] for f in group] for group in ((0, 1, 2), (3,), (4, 5, 6))]
        a, j = [[rates[b, pl.ds(NB * f, NB), :] for f in group] for group in ((0, 1, 2), (3, 4, 5))]
        for c in range(3):
            predicted[b, c] = x[c] + v[c] * t + a[c] * t2 + j[c] * t3
            predicted[b, 4 + c] = v[c] + a[c] * t + j[c] * t2
        predicted[b, 3] = m[0]
        return 0

    lax.fori_loop(0, table.shape[0], shard, 0)
    for f in range(QUANTITIES):
        predicted[table.shape[0], f] = jnp.zeros((NB, BS), F32)


def fill_order(levall, sent, order):
    shards = levall.shape[0]

    def shard(b, count):
        for k in range(NB):
            order[count] = b * NB + k
            count = count + (levall[b, k] > sent).astype(jnp.int32)
        return count

    count = lax.fori_loop(0, shards, shard, jnp.int32(0))
    for e in range(NB):
        order[count + e] = shards * NB
    order[(shards + 2) * NB] = count


def target_of(state, plan, s):
    x, v, a, j = columns(state[plan[BLOCK, s]])
    ahead = forecast(x, v, a, j, span_of(plan[LEVEL, s]))
    return [jnp.broadcast_to(value, (8, 128)) for value in ahead]


def broad(row):
    return jnp.broadcast_to(row, (8, 128))


def tile_rows(tile):
    return [broad(tile(r)) for r in (0, 1, 2, 4, 5, 6)], broad(tile(3))


def from_table(table, b, k):
    return tile_rows(lambda r: table[b, pl.ds(NB * r + k, 1), :])


def from_predicted(predicted, b, k):
    return tile_rows(lambda r: predicted[b, r, pl.ds(k, 1), :])


def slot_pairs(first, last, state, plan, sweep, prepare, close, sink, carry):
    def two(p, carry):
        goal = [target_of(state, plan, 2 * p + e) for e in range(2)]
        prepare(p)
        acc = sweep(goal)
        for e in range(2):
            s = 2 * p + e
            near = zeros()
            for part in range(2):
                rows, mass, wanted = close(s, e, part)
                near = pair_split(goal[e], rows, mass * jnp.where(wanted, 1.0, 0.0).astype(F32), near)
            total, inner = (
                [jnp.sum(value, axis=1, keepdims=True) for value in group] for group in (acc[e], near)
            )
            carry = sink(s, total, inner, carry)
        return carry

    return lax.fori_loop(first, last, two, carry)


def pairs_of(plan):
    return (plan[COUNT, 0] + 1) // 2


def sweep_table(groups, load):
    def sweep(goal):
        def group(b, acc):
            for k in range(NB):
                rows, mass = load(b, k)
                acc = tuple(pair(goal[e], rows, mass, WIDE, acc[e]) for e in range(2))
            return acc

        return lax.fori_loop(0, groups, group, (zeros(), zeros()))

    return sweep


def fill_received(got, turned):
    senders, _, lanes = got.shape
    for t in range(lanes // 128):
        for half in range(senders // 128):
            part = got[pl.ds(half * 128, 128), 0, pl.ds(t * 128, 128)]
            turned[pl.ds(t * 16, 16), :, pl.ds(half * 128, 128)] = part.T.reshape(16, 8, 128)


def sweep_received(turned, mass, slots_in, used):
    def sweep(goal):
        def slot(s, acc):
            for i in range(8):
                for half in range(turned.shape[2] // 128):
                    at = pl.ds(half * 128, 128)
                    rows = [broad(turned[f * slots_in + s, i : i + 1, at]) for f in range(6)]
                    m = broad(mass[s, i : i + 1, at])
                    acc = tuple(pair(goal[e], rows, m, WIDE, acc[e]) for e in range(2))
            return acc

        return lax.fori_loop(0, used, slot, (zeros(), zeros()))

    return sweep


def gather_blocks(turned, mass, slots_in, plan, near, p):
    lane = lax.broadcasted_iota(jnp.int32, (8, 128), 1)
    row = lax.broadcasted_iota(jnp.int32, (8, 128), 0)
    keep = lane // 16 == row
    for item in range(4):
        b = plan[SHARD, 4 * p + item]
        place = plan[ROW, 4 * p + item]
        half = pl.ds(pl.multiple_of((b // 8) * 128, 128), 128)
        shift = lax.rem(128 - lax.rem(b, 8) * 16, 128)
        for r, f in ((0, 0), (1, 1), (2, 2), (4, 3), (5, 4), (6, 5), (3, None)):
            tile = mass[place, :, half] if f is None else turned[f * slots_in + place, :, half]
            tile = pltpu.roll(pltpu.roll(tile, shift, 1), 0, 1, stride=16, stride_axis=0)
            near[item, r : r + 1, :] = jnp.sum(jnp.where(keep, tile, 0.0), axis=0, keepdims=True)


def fill_tiles(parts, tiles, width):
    per = 128 // width
    tiles = list(tiles)
    lane = lax.broadcasted_iota(jnp.int32, (8, 128), 1)
    for f, slot, column in parts:
        t = f // per
        tiles[t] = jnp.where(lane == (f % per) * width + slot * 8, column, tiles[t])
    return tiles


def blank(count):
    return [jnp.zeros((8, 128), F32) for _ in range(count)]


def place_tiles(tiles):
    tiles = [pltpu.roll(tile, 0, 1, stride=1, stride_axis=0) for tile in tiles]
    return [jnp.sum(tile, axis=0, keepdims=True) for tile in tiles]


def send(tiles, pay):
    for t, tile in enumerate(tiles):
        full = jnp.broadcast_to(tile[None], (pay.shape[0], 1, 128))
        pay[:, :, pl.ds(t * 128, 128)] = full


def corrector(step, state, plan, sums):
    lane = lax.broadcasted_iota(jnp.int32, (8, 128), 1)

    def sink(s, total, inner, carry):
        k = plan[BLOCK, s]
        t = span_of(plan[LEVEL, s])
        tile = state[k]
        x, v, a, j = columns(tile)
        if sums is not None:
            before = sums[s]
            total = [total[c] + before[:, c : c + 1] for c in range(6)]
            inner = [inner[c] + before[:, 8 + c : 9 + c] for c in range(6)]
        total = [total[c] + inner[c] for c in range(6)]
        half = t * 0.5
        twelfth = t * t * (1.0 / 12.0)
        v1 = [v[c] + (a[c] + total[c]) * half + (j[c] - total[3 + c]) * twelfth for c in range(3)]
        x1 = [x[c] + (v[c] + v1[c]) * half + (a[c] - total[c]) * twelfth for c in range(3)]
        if step == 3:
            parts = [(f, s, column) for f, column in enumerate(x1 + v1 + total + inner)]
            return tuple(fill_tiles(parts, carry, 64))
        fresh = tile
        for at, column in zip(XS + VS + AS + JS, x1 + v1 + total):
            fresh = jnp.where(lane == at, column, fresh)
        state[jnp.where(s < plan[COUNT, 0], k, NB)] = fresh
        ahead = forecast(x1, v1, total[:3], total[3:], TICK)
        if step == 0:
            ahead = ahead + [tile[:, MS : MS + 1]]
        parts = [(f, plan[PLACE, s], column) for f, column in enumerate(ahead)]
        return tuple(fill_tiles(parts, carry, 32 if step == 0 else 64))

    return sink


def fill_later(state, lev, later):
    parts = []
    seen = jnp.int32(4)
    for k in range(NB):
        one = lev[k] == 1
        mark = jnp.where(one, seen, -1000)
        x, v, a, j = columns(state[k])
        for f, column in enumerate(forecast(x, v, a, j, 2 * TICK)):
            parts.append((f, mark, column))
        seen = seen + one.astype(jnp.int32)
    for t, tile in enumerate(fill_tiles(parts, blank(3), 64)):
        later[t] = tile


def pack_kernel(ps, fr, mass, lev, first, rates, own):
    x, v, a, j = ps[0:3, :], ps[3:6, :], fr[0:3, :], fr[3:6, :]
    t2 = TICK * TICK * 0.5
    xp = x + v * TICK + a * t2 + j * (TICK * TICK * TICK / 6.0)
    vp = v + a * TICK + j * t2
    ap = a + j * TICK
    lane = lax.broadcasted_iota(jnp.int32, (8, BS), 1)
    levels = jnp.zeros((8, BS), F32)
    for k in range(NB):
        levels = jnp.where(lane == k, lev[k].astype(F32), levels)
    first[7 * NB : 7 * NB + 8, :] = levels
    for k in range(NB):
        at = slice(k * BS, k * BS + BS)
        for c in range(3):
            first[NB * c + k : NB * c + k + 1, :] = xp[c : c + 1, at]
            first[NB * (4 + c) + k : NB * (4 + c) + k + 1, :] = vp[c : c + 1, at]
            rates[0, NB * c + k : NB * c + k + 1, :] = ap[c : c + 1, at]
            rates[0, NB * (3 + c) + k : NB * (3 + c) + k + 1, :] = j[c : c + 1, at]
        first[NB * 3 + k : NB * 3 + k + 1, :] = mass[:, at]
        own[k] = jnp.zeros((16, BS), F32)
        own[k, 0:3, :] = x[:, at]
        own[k, 3:4, :] = mass[:, at]
        own[k, 4:7, :] = v[:, at]
        own[k, 8:14, :] = fr[:, at]
    for b in range(1, rates.shape[0]):
        rates[b] = rates[0]


def first_kernel(me, col, table, mine, lev, levall, partner, state, pay, turned, plan):
    me = me[0]
    col = pl.multiple_of(col[0] * 8, 8)
    fill_slots(lev, TOP[0], CAPS[0], plan)
    for k in range(NB):
        turned[k, :, 0:16] = mine[k].T
    for k in range(NB):
        state[k] = turned[k, pl.ds(col, 8), :]
    masses = []
    seen = jnp.int32(0)
    for k in range(NB):
        one = lev[k] == 1
        masses.append((7, jnp.where(one, seen, -1000), state[k][:, MS : MS + 1]))
        seen = seen + one.astype(jnp.int32)

    def close(s, e, part):
        k = plan[BLOCK, s]
        b = partner[k] // NB if part else me
        rows, mass = from_table(table, b, k)
        return rows, mass, b != me if part else jnp.bool_(True)

    tiles = slot_pairs(
        0, pairs_of(plan), state, plan,
        sweep_table(table.shape[0], lambda b, k: from_table(table, b, k)),
        lambda p: None, close, corrector(0, state, plan, None),
        tuple(fill_tiles(masses, blank(2), 32)),
    )
    send(place_tiles(tiles), pay)


def ahead_sums(step, first, last, me, plan, order, predicted, state, sums):
    lane = lax.broadcasted_iota(jnp.int32, (8, 128), 1)

    def load(g, e):
        index = order[g * NB + e]
        return from_predicted(predicted, index // NB, lax.rem(index, NB))

    def close(s, e, part):
        rows, mass = from_predicted(predicted, plan[SHARD, 2 * s + part], plan[BLOCK, s])
        other = plan[SHARD, 2 * s + 1] != me if part else jnp.bool_(True)
        return rows, mass, other & (plan[HERE, 2 * s + part] == 0)

    def sink(s, total, inner, carry):
        tile = jnp.zeros((8, 128), F32)
        for at, group in ((0, total), (8, inner)):
            for c in range(6):
                tile = jnp.where(lane == at + c, group[c], tile)
        sums[s] = tile
        return carry

    groups = (order[order.shape[0] - NB] + NB - 1) // NB
    slot_pairs(first, last, state, plan, sweep_table(groups, load), lambda p: None, close, sink, 0)


def early_pairs(plan):
    return jnp.minimum(plan[COUNT, 2] // 2, 1)


def ahead_kernel(step, me, table, rates, lev, levall, partner, state, *rest):
    if step == 1:
        sums, plan, predicted, order = rest
    elif step == 2:
        sums, plan, later, early, order, predicted, plan3 = rest
    else:
        early, order, sums, plan, predicted = rest
    me = me[0]
    fill_slots(lev, TOP[step], CAPS[step], plan)
    fill_near(plan, CAPS[step], me, levall, partner, SENT[step])
    if step < 3:
        fill_order(levall, SENT[step], order)
    fill_sources(table, rates, predicted, step * TICK)
    first = 0
    if step == 3:
        first = early_pairs(plan)
        sums[0:2] = early[...]
    ahead_sums(step, first, pairs_of(plan), me, plan, order, predicted, state, sums)
    if step == 2:
        fill_later(state, lev, later)
        fill_slots(lev, TOP[3], CAPS[3], plan3)
        fill_near(plan3, CAPS[3], me, levall, partner, SENT[3])
        fill_sources(table, rates, predicted, 3 * TICK)
        early[...] = jnp.zeros((2, 8, 128), F32)
        ahead_sums(3, 0, early_pairs(plan3), me, plan3, order, predicted, state, early)
    if step == 1:
        level = table[:, 7 * NB, :]
        lane = lax.broadcasted_iota(jnp.int32, level.shape, 1)
        one = jnp.where((level == 1.0) & (lane < NB), 1.0, 0.0).astype(F32)
        plan[COUNT, 1] = jnp.max(jnp.sum(one, axis=1, keepdims=True)).astype(jnp.int32)


def after_kernel(step, got, state_in, sums, plan, *rest):
    later = None
    used = SLOTS[step]
    if step > 1:
        masses, before, *rest = rest
        used = jnp.minimum(4 + before[COUNT, 1], used)
    if step == 2:
        later, *rest = rest
    if step == 3:
        state = state_in
    else:
        state, *rest = rest
    pay, *rest = rest
    if step == 1:
        masses, *rest = rest
    near, turned = rest
    if step < 3:
        state[...] = state_in[...]
    fill_received(got, turned)
    if step == 1:
        masses[0:4] = turned[24:28]
        masses[4:8] = turned[28:32]

    def close(s, e, part):
        rows, mass = tile_rows(lambda r: near[2 * e + part, r : r + 1, :])
        return rows, mass, plan[HERE, 2 * s + part] == 1

    tiles = slot_pairs(
        0, pairs_of(plan), state, plan,
        sweep_received(turned, masses, SLOTS[step], used),
        lambda p: gather_blocks(turned, masses, SLOTS[step], plan, near, p),
        close, corrector(step, state, plan, sums),
        tuple([later[t] for t in range(3)] if step == 2 else blank(9 if step == 3 else 3)),
    )
    send(place_tiles(tiles), pay)


def last_kernel(got, ps, fr, irr, plan, kin, comb, close):
    count = plan[COUNT, 0]
    kin[...] = ps[...]
    comb[...] = fr[...]
    close[...] = irr[...]
    senders = got.shape[0]
    lane = lax.broadcasted_iota(jnp.int32, (senders, 128), 1)
    row = lax.broadcasted_iota(jnp.int32, (senders, 128), 0)
    spread = [pltpu.roll(got[:, 0, pl.ds(t * 128, 128)], 0, 1, stride=8, stride_axis=0) for t in range(9)]
    for s in range(CAPS[3]):
        rows = []
        for f in range(18):
            t, e = divmod(f, 2)
            start = e * 64 + s * 8
            keep = (lane + (128 - start)) % 128 // 8 == row
            value = jnp.sum(jnp.where(keep, spread[t], 0.0), axis=0, keepdims=True)
            rows.append(pltpu.roll(value, (128 - start) % 128, 1))
        at = pl.ds(pl.multiple_of(plan[BLOCK, s] * BS, BS), BS)

        @pl.when(s < count)
        def _(at=at, rows=rows):
            for f, value in enumerate(rows):
                out = (kin, comb, close)[f // 6]
                out[f % 6 : f % 6 + 1, at] = value


def body(phase_space, force_rates, irregular, stellar_masses, levels, active, partner):
    shards = lax.axis_size("blk")
    columns_ = lax.axis_size("grp")
    everyone = shards * columns_
    me = lax.axis_index("blk").astype(jnp.int32).reshape(1)
    col = lax.axis_index("grp").astype(jnp.int32).reshape(1)
    tiles = lambda count: pltpu.VMEM((count, 8, 128), F32)
    array = lambda *shape: jax.ShapeDtypeStruct(shape, F32)
    near = lambda *shape: pltpu.VMEM(shape, F32)
    here = lambda x: pltpu.with_memory_space_constraint(x, pltpu.VMEM)
    plan_shape = jax.ShapeDtypeStruct((8, 32), jnp.int32)
    state_shape = near(NB + 1, 8, 128)

    def exchange(pay, axis):
        return lax.all_to_all(pay, axis, split_axis=0, concat_axis=0, tiled=True)

    packed, rates, mine = pl.pallas_call(
        pack_kernel,
        out_shape=(array(7 * NB + 8, BS), array(shards, 6 * NB, BS), near(NB, 16, BS)),
        in_specs=[VMEM, VMEM, VMEM, SMEM],
        out_specs=(VMEM, VMEM, VMEM),
        name="pack",
    )(phase_space, force_rates, stellar_masses[None, :], levels)
    table = lax.all_gather(packed, "blk", axis=0, tiled=False)
    levall = table[:, 7 * NB, :NB].astype(jnp.int32)
    table, rates = lax.optimization_barrier((table, rates))
    rates = exchange(rates, "blk")
    state, pay = pl.pallas_call(
        first_kernel,
        out_shape=(state_shape, array(everyone, 1, 256)),
        in_specs=[SMEM, SMEM, VMEM, VMEM, SMEM, SMEM, SMEM],
        out_specs=(VMEM, VMEM),
        scratch_shapes=[pltpu.VMEM((NB, 128, 128), F32), pltpu.SMEM((8, 32), jnp.int32)],
        name="first",
    )(me, col, here(table), here(mine), levels, levall, partner)
    masses = before = None
    for step in (1, 2, 3):
        cap = CAPS[step]
        lanes = (0, 256, 384, 384)[step]
        got = exchange(pay, ("blk", "grp"))
        order_shape = ((shards + 3) * NB,)
        ins = (me, here(table), here(rates), levels, levall, partner, here(state))
        specs = [SMEM, VMEM, VMEM, SMEM, SMEM, SMEM, VMEM]
        out_shape = (near(cap, 8, 128), plan_shape)
        out_specs = (VMEM, SMEM)
        scratch = [pltpu.VMEM((shards + 1, QUANTITIES, NB, BS), F32)]
        if step == 1:
            scratch += [pltpu.SMEM(order_shape, jnp.int32)]
        elif step == 2:
            out_shape += (near(3, 8, 128), near(2, 8, 128), jax.ShapeDtypeStruct(order_shape, jnp.int32))
            out_specs += (VMEM, VMEM, SMEM)
            scratch += [pltpu.SMEM((8, 32), jnp.int32)]
        else:
            ins += (here(early), order)
            specs += [VMEM, SMEM]
        outs = pl.pallas_call(
            functools.partial(ahead_kernel, step),
            out_shape=out_shape,
            in_specs=specs,
            out_specs=out_specs,
            scratch_shapes=scratch,
            name=f"ahead{step}",
        )(*ins)
        sums, plan = outs[:2]
        if step == 2:
            early, order = outs[3:]
        ins = (here(got), here(state), here(sums), plan)
        specs = [VMEM, VMEM, VMEM, SMEM]
        if step > 1:
            ins += (here(masses), before)
            specs += [VMEM, SMEM]
        if step == 2:
            ins += (here(outs[2]),)
            specs += [VMEM]
        pay_shape = array(everyone if step < 3 else columns_, 1, (0, 384, 384, 1152)[step])
        out_shape = {
            1: (state_shape, pay_shape, near(8, 8, everyone)), 2: (state_shape, pay_shape), 3: (pay_shape,),
        }[step]
        outs = pl.pallas_call(
            functools.partial(after_kernel, step),
            out_shape=out_shape,
            in_specs=specs,
            out_specs=tuple(VMEM for _ in out_shape),
            scratch_shapes=[
                tiles(4),
                pltpu.VMEM((lanes // 8, 8, everyone), F32),
            ],
            name=f"after{step}",
        )(*ins)
        if step == 1:
            state, pay, masses = outs
            before = plan
        elif step == 2:
            state, pay = outs
        else:
            (pay,) = outs
    got = exchange(pay, "grp")
    shape = array(6, W)
    return tuple(
        pl.pallas_call(
            last_kernel,
            out_shape=(shape, shape, shape),
            in_specs=[VMEM, VMEM, VMEM, VMEM, SMEM],
            out_specs=(VMEM, VMEM, VMEM),
            name="last",
        )(here(got), phase_space, force_rates, irregular, plan)
    )


def solution(mesh):
    in_specs = (
        P(None, "blk"), P(None, "blk"), P(None, "blk"), P("blk"), P("blk"), P(None, "blk"), P("blk"),
    )
    out_specs = (P(None, "blk"), P(None, "blk"), P(None, "blk"))
    return jax.shard_map(body, mesh=mesh, in_specs=in_specs, out_specs=out_specs, check_vma=False)
```

```python
import functools
import jax
import jax.numpy as jnp
from jax import lax
from jax.experimental import pallas as pl
from jax.experimental.pallas import tpu as pltpu
from jax.sharding import PartitionSpec as P

WIDE = 0.04
CLOSE = 0.0001
TICK = 0.125
NB = 16
BS = 128
W = NB * BS
F32 = jnp.float32
CAPS = (4, 6, 4, 8)
TOP = (0, 1, 0, 2)
SENT = (-1, 0, 1, 1)
SLOTS = (0, 4, 8, 8)

VMEM = pl.BlockSpec(memory_space=pltpu.VMEM)
SMEM = pl.BlockSpec(memory_space=pltpu.SMEM)


def pair(target, source, mass, soften, acc):
    r = [source[c] - target[c] for c in range(3)]
    w = [source[c] - target[c] for c in range(3, 6)]
    d = (r[0] * r[0] + soften) + r[1] * r[1] + r[2] * r[2]
    s = lax.rsqrt(d)
    s2 = s * s
    weight = (mass * s) * s2
    q = (r[0] * w[0] + r[1] * w[1] + r[2] * w[2]) * (s2 * 3.0)
    acc = list(acc)
    for c in range(3):
        acc[c] = acc[c] + weight * r[c]
        acc[3 + c] = acc[3 + c] + weight * (w[c] - q * r[c])
    return tuple(acc)


def pair_split(target, source, mass, acc):
    r = [source[c] - target[c] for c in range(3)]
    w = [source[c] - target[c] for c in range(3, 6)]
    dd = r[0] * r[0] + r[1] * r[1] + r[2] * r[2]
    rw = (r[0] * w[0] + r[1] * w[1] + r[2] * w[2]) * 3.0
    acc = list(acc)
    for soften, sign in ((CLOSE, 1.0), (WIDE, -1.0)):
        s = lax.rsqrt(dd + soften)
        s2 = s * s
        weight = (mass * s) * (s2 * sign)
        q = rw * s2
        for c in range(3):
            acc[c] = acc[c] + weight * r[c]
            acc[3 + c] = acc[3 + c] + weight * (w[c] - q * r[c])
    return tuple(acc)


def zeros():
    return tuple(jnp.zeros((8, 128), F32) for _ in range(6))


BLOCK, PLACE, LEVEL, SHARD, ROW, HERE, COUNT = range(7)


def fill_slots(lev, top, cap, plan):
    for s in range(cap):
        plan[BLOCK, s] = 0
        plan[PLACE, s] = -1000
        plan[LEVEL, s] = 0
    count = jnp.int32(0)
    for group in ((2,), (0, 1)) if top == 2 else ((0, 1),):
        ones = [jnp.int32(0), jnp.int32(4)]
        for k in range(NB):
            level = lev[k]
            place = jnp.where(level == 0, ones[0], jnp.where(level == 1, ones[1], -1000))
            live = (level == 2) if group == (2,) else level <= min(top, 1)
            plan[BLOCK, count] = k
            plan[PLACE, count] = jnp.where(live, place, -1000)
            plan[LEVEL, count] = jnp.where(live, level, 0)
            count = count + live.astype(jnp.int32)
            ones[0] = ones[0] + (level == 0).astype(jnp.int32)
            ones[1] = ones[1] + (level == 1).astype(jnp.int32)
        if group == (2,):
            plan[COUNT, 2] = count
    plan[COUNT, 0] = count
    plan[COUNT, 3] = ones[0]


def fill_near(plan, cap, own, levall, partner, sent):
    def slot(s, _):
        k = plan[BLOCK, s]
        q = partner[k] // NB
        level = levall[q, k]
        place = jnp.where(level == 0, 0, 4)
        for e in range(NB):
            place = place + ((levall[q, e] == level) & (e < k)).astype(jnp.int32)
        ours = plan[LEVEL, s] <= sent
        theirs = (q != own) & (level <= sent)
        for e, (b, row, here) in enumerate(((own, plan[PLACE, s], ours), (q, place, theirs))):
            plan[SHARD, 2 * s + e] = b
            plan[ROW, 2 * s + e] = jnp.clip(jnp.where(here, row, 0), 0, 3 if sent == 0 else 7)
            plan[HERE, 2 * s + e] = here.astype(jnp.int32)
        return 0

    lax.fori_loop(0, cap, slot, 0)


def span_of(level):
    return jnp.where(level == 0, TICK, jnp.where(level == 1, 2 * TICK, 4 * TICK)).astype(F32)


XS, MS, VS, AS, JS = (0, 1, 2), 3, (4, 5, 6), (8, 9, 10), (11, 12, 13)


def columns(tile):
    return tuple(
        [tile[:, c : c + 1] for c in group] for group in (XS, VS, AS, JS)
    )


def forecast(x, v, a, j, t):
    t2 = t * t * 0.5
    t3 = t * t * t * (1.0 / 6.0)
    xp = [x[c] + v[c] * t + a[c] * t2 + j[c] * t3 for c in range(3)]
    vp = [v[c] + a[c] * t + j[c] * t2 for c in range(3)]
    return xp + vp


QUANTITIES = 7


def fill_sources(table, rates, predicted, t):
    t2 = t * t * 0.5
    t3 = t * t * t / 6.0

    def shard(b, _):
        x, m, v = [[table[b, pl.ds(NB * f, NB), :] for f in group] for group in ((0, 1, 2), (3,), (4, 5, 6))]
        a, j = [[rates[b, pl.ds(NB * f, NB), :] for f in group] for group in ((0, 1, 2), (3, 4, 5))]
        for c in range(3):
            predicted[b, c] = x[c] + v[c] * t + a[c] * t2 + j[c] * t3
            predicted[b, 4 + c] = v[c] + a[c] * t + j[c] * t2
        predicted[b, 3] = m[0]
        return 0

    lax.fori_loop(0, table.shape[0], shard, 0)
    for f in range(QUANTITIES):
        predicted[table.shape[0], f] = jnp.zeros((NB, BS), F32)


def target_of(state, plan, s):
    x, v, a, j = columns(state[plan[BLOCK, s]])
    ahead = forecast(x, v, a, j, span_of(plan[LEVEL, s]))
    return [jnp.broadcast_to(value, (8, 128)) for value in ahead]


def broad(row):
    return jnp.broadcast_to(row, (8, 128))


def tile_rows(tile):
    return [broad(tile(r)) for r in (0, 1, 2, 4, 5, 6)], broad(tile(3))


def from_table(table, b, k):
    return tile_rows(lambda r: table[b, pl.ds(NB * r + k, 1), :])


def from_predicted(predicted, b, k):
    return tile_rows(lambda r: predicted[b, r, pl.ds(k, 1), :])


def slot_pairs(first, last, state, plan, sweep, prepare, close, sink, carry):
    def two(p, carry):
        goal = [target_of(state, plan, 2 * p + e) for e in range(2)]
        prepare(p)
        acc = sweep(goal)
        for e in range(2):
            s = 2 * p + e
            near = zeros()
            for part in range(2):
                rows, mass, wanted = close(s, e, part)
                near = pair_split(goal[e], rows, mass * jnp.where(wanted, 1.0, 0.0).astype(F32), near)
            total, inner = (
                [jnp.sum(value, axis=1, keepdims=True) for value in group] for group in (acc[e], near)
            )
            carry = sink(s, total, inner, carry)
        return carry

    return lax.fori_loop(first, last, two, carry)


def pairs_of(plan):
    return (plan[COUNT, 0] + 1) // 2


def sweep_table(groups, load):
    def sweep(goal):
        def group(b, acc):
            for k in range(NB):
                rows, mass = load(b, k)
                acc = tuple(pair(goal[e], rows, mass, WIDE, acc[e]) for e in range(2))
            return acc

        return lax.fori_loop(0, groups, group, (zeros(), zeros()))

    return sweep


def fill_received(got, turned):
    senders, _, lanes = got.shape
    for t in range(lanes // 128):
        for half in range(senders // 128):
            part = got[pl.ds(half * 128, 128), 0, pl.ds(t * 128, 128)]
            turned[pl.ds(t * 16, 16), :, pl.ds(half * 128, 128)] = part.T.reshape(16, 8, 128)


def sweep_received(turned, mass, slots_in, used):
    def sweep(goal):
        def slot(s, acc):
            for i in range(8):
                for half in range(turned.shape[2] // 128):
                    at = pl.ds(half * 128, 128)
                    rows = [broad(turned[f * slots_in + s, i : i + 1, at]) for f in range(6)]
                    m = broad(mass[s, i : i + 1, at])
                    acc = tuple(pair(goal[e], rows, m, WIDE, acc[e]) for e in range(2))
            return acc

        return lax.fori_loop(0, used, slot, (zeros(), zeros()))

    return sweep


def gather_blocks(turned, mass, slots_in, plan, near, p):
    lane = lax.broadcasted_iota(jnp.int32, (8, 128), 1)
    row = lax.broadcasted_iota(jnp.int32, (8, 128), 0)
    keep = lane // 16 == row
    for item in range(4):
        b = plan[SHARD, 4 * p + item]
        place = plan[ROW, 4 * p + item]
        half = pl.ds(pl.multiple_of((b // 8) * 128, 128), 128)
        shift = lax.rem(128 - lax.rem(b, 8) * 16, 128)
        for r, f in ((0, 0), (1, 1), (2, 2), (4, 3), (5, 4), (6, 5), (3, None)):
            tile = mass[place, :, half] if f is None else turned[f * slots_in + place, :, half]
            tile = pltpu.roll(pltpu.roll(tile, shift, 1), 0, 1, stride=16, stride_axis=0)
            near[item, r : r + 1, :] = jnp.sum(jnp.where(keep, tile, 0.0), axis=0, keepdims=True)


def fill_tiles(parts, tiles, width):
    per = 128 // width
    tiles = list(tiles)
    lane = lax.broadcasted_iota(jnp.int32, (8, 128), 1)
    for f, slot, column in parts:
        t = f // per
        tiles[t] = jnp.where(lane == (f % per) * width + slot * 8, column, tiles[t])
    return tiles


def blank(count):
    return [jnp.zeros((8, 128), F32) for _ in range(count)]


def place_tiles(tiles):
    tiles = [pltpu.roll(tile, 0, 1, stride=1, stride_axis=0) for tile in tiles]
    return [jnp.sum(tile, axis=0, keepdims=True) for tile in tiles]


def send(tiles, pay):
    for t, tile in enumerate(tiles):
        full = jnp.broadcast_to(tile[None], (pay.shape[0], 1, 128))
        pay[:, :, pl.ds(t * 128, 128)] = full


def corrector(step, state, plan, sums):
    lane = lax.broadcasted_iota(jnp.int32, (8, 128), 1)

    def sink(s, total, inner, carry):
        k = plan[BLOCK, s]
        t = span_of(plan[LEVEL, s])
        tile = state[k]
        x, v, a, j = columns(tile)
        if sums is not None:
            before = sums[s]
            total = [total[c] + before[:, c : c + 1] for c in range(6)]
            inner = [inner[c] + before[:, 8 + c : 9 + c] for c in range(6)]
        total = [total[c] + inner[c] for c in range(6)]
        half = t * 0.5
        twelfth = t * t * (1.0 / 12.0)
        v1 = [v[c] + (a[c] + total[c]) * half + (j[c] - total[3 + c]) * twelfth for c in range(3)]
        x1 = [x[c] + (v[c] + v1[c]) * half + (a[c] - total[c]) * twelfth for c in range(3)]
        if step == 3:
            parts = [(f, s, column) for f, column in enumerate(x1 + v1 + total + inner)]
            return tuple(fill_tiles(parts, carry, 64))
        fresh = tile
        for at, column in zip(XS + VS + AS + JS, x1 + v1 + total):
            fresh = jnp.where(lane == at, column, fresh)
        state[jnp.where(s < plan[COUNT, 0], k, NB)] = fresh
        ahead = forecast(x1, v1, total[:3], total[3:], TICK)
        if step == 0:
            ahead = ahead + [tile[:, MS : MS + 1]]
        parts = [(f, plan[PLACE, s], column) for f, column in enumerate(ahead)]
        return tuple(fill_tiles(parts, carry, 32 if step == 0 else 64))

    return sink


def fill_later(state, lev, later):
    parts = []
    seen = jnp.int32(4)
    for k in range(NB):
        one = lev[k] == 1
        mark = jnp.where(one, seen, -1000)
        x, v, a, j = columns(state[k])
        for f, column in enumerate(forecast(x, v, a, j, 2 * TICK)):
            parts.append((f, mark, column))
        seen = seen + one.astype(jnp.int32)
    for t, tile in enumerate(fill_tiles(parts, blank(3), 64)):
        later[t] = tile


def pack_kernel(ps, fr, mass, lev, first, rates, own):
    x, v, a, j = ps[0:3, :], ps[3:6, :], fr[0:3, :], fr[3:6, :]
    t2 = TICK * TICK * 0.5
    xp = x + v * TICK + a * t2 + j * (TICK * TICK * TICK / 6.0)
    vp = v + a * TICK + j * t2
    ap = a + j * TICK
    lane = lax.broadcasted_iota(jnp.int32, (8, BS), 1)
    levels = jnp.zeros((8, BS), F32)
    for k in range(NB):
        levels = jnp.where(lane == k, lev[k].astype(F32), levels)
    first[7 * NB : 7 * NB + 8, :] = levels
    for k in range(NB):
        at = slice(k * BS, k * BS + BS)
        for c in range(3):
            first[NB * c + k : NB * c + k + 1, :] = xp[c : c + 1, at]
            first[NB * (4 + c) + k : NB * (4 + c) + k + 1, :] = vp[c : c + 1, at]
            rates[0, NB * c + k : NB * c + k + 1, :] = ap[c : c + 1, at]
            rates[0, NB * (3 + c) + k : NB * (3 + c) + k + 1, :] = j[c : c + 1, at]
        first[NB * 3 + k : NB * 3 + k + 1, :] = mass[:, at]
        own[k] = jnp.zeros((16, BS), F32)
        own[k, 0:3, :] = x[:, at]
        own[k, 3:4, :] = mass[:, at]
        own[k, 4:7, :] = v[:, at]
        own[k, 8:14, :] = fr[:, at]
    for b in range(1, rates.shape[0]):
        rates[b] = rates[0]


def first_kernel(me, col, table, mine, lev, levall, partner, state, pay, order0, order1, turned, plan):
    me = me[0]
    col = pl.multiple_of(col[0] * 8, 8)
    fill_slots(lev, TOP[0], CAPS[0], plan)
    for k in range(NB):
        turned[k, :, 0:16] = mine[k].T
    for k in range(NB):
        state[k] = turned[k, pl.ds(col, 8), :]
    masses = []
    seen = jnp.int32(0)
    for k in range(NB):
        one = lev[k] == 1
        masses.append((7, jnp.where(one, seen, -1000), state[k][:, MS : MS + 1]))
        seen = seen + one.astype(jnp.int32)

    def close(s, e, part):
        k = plan[BLOCK, s]
        b = partner[k] // NB if part else me
        rows, mass = from_table(table, b, k)
        return rows, mass, b != me if part else jnp.bool_(True)

    shards = table.shape[0]
    orders = (order0, order1)

    def sweep(goal):
        def group(b, carry):
            acc, counts = carry
            for k in range(NB):
                rows, mass = from_table(table, b, k)
                acc = tuple(pair(goal[e], rows, mass, WIDE, acc[e]) for e in range(2))
                for order, count in zip(orders, counts):
                    order[count] = b * NB + k
                counts = tuple(counts[e] + (levall[b, k] > e).astype(jnp.int32) for e in range(2))
            return acc, counts

        start = ((zeros(), zeros()), (jnp.int32(0), jnp.int32(0)))
        acc, counts = lax.fori_loop(0, shards, group, start)
        for order, count in zip(orders, counts):
            for e in range(NB):
                order[count + e] = shards * NB
            order[(shards + 2) * NB] = count
        return acc

    tiles = slot_pairs(
        0, pairs_of(plan), state, plan, sweep,
        lambda p: None, close, corrector(0, state, plan, None),
        tuple(fill_tiles(masses, blank(2), 32)),
    )
    send(place_tiles(tiles), pay)


def ahead_sums(step, first, last, me, plan, order, predicted, state, sums):
    lane = lax.broadcasted_iota(jnp.int32, (8, 128), 1)

    def load(g, e):
        index = order[g * NB + e]
        return from_predicted(predicted, index // NB, lax.rem(index, NB))

    def close(s, e, part):
        rows, mass = from_predicted(predicted, plan[SHARD, 2 * s + part], plan[BLOCK, s])
        other = plan[SHARD, 2 * s + 1] != me if part else jnp.bool_(True)
        return rows, mass, other & (plan[HERE, 2 * s + part] == 0)

    def sink(s, total, inner, carry):
        tile = jnp.zeros((8, 128), F32)
        for at, group in ((0, total), (8, inner)):
            for c in range(6):
                tile = jnp.where(lane == at + c, group[c], tile)
        sums[s] = tile
        return carry

    groups = (order[order.shape[0] - NB] + NB - 1) // NB
    slot_pairs(first, last, state, plan, sweep_table(groups, load), lambda p: None, close, sink, 0)


def early_pairs(plan):
    return jnp.where((plan[COUNT, 2] >= 2) & (plan[COUNT, 3] <= 2), 1, 0)


def ahead_kernel(step, me, table, rates, lev, levall, partner, order, state, *rest):
    if step == 1:
        sums, plan, predicted = rest
    elif step == 2:
        sums, plan, later, early, predicted, plan3 = rest
    else:
        early, sums, plan, predicted = rest
    me = me[0]
    fill_slots(lev, TOP[step], CAPS[step], plan)
    fill_near(plan, CAPS[step], me, levall, partner, SENT[step])
    fill_sources(table, rates, predicted, step * TICK)
    first = 0
    if step == 3:
        first = early_pairs(plan)
        sums[0:2] = early[...]
    ahead_sums(step, first, pairs_of(plan), me, plan, order, predicted, state, sums)
    if step == 2:
        fill_later(state, lev, later)
        fill_slots(lev, TOP[3], CAPS[3], plan3)
        fill_near(plan3, 2, me, levall, partner, SENT[3])
        fill_sources(table, rates, predicted, 3 * TICK)
        early[...] = jnp.zeros((2, 8, 128), F32)
        ahead_sums(3, 0, early_pairs(plan3), me, plan3, order, predicted, state, early)
    if step == 1:
        level = table[:, 7 * NB, :]
        lane = lax.broadcasted_iota(jnp.int32, level.shape, 1)
        one = jnp.where((level == 1.0) & (lane < NB), 1.0, 0.0).astype(F32)
        plan[COUNT, 1] = jnp.max(jnp.sum(one, axis=1, keepdims=True)).astype(jnp.int32)


def after_kernel(step, got, state_in, sums, plan, *rest):
    later = None
    used = SLOTS[step]
    if step > 1:
        masses, before, *rest = rest
        used = jnp.minimum(4 + before[COUNT, 1], used)
    if step == 2:
        later, *rest = rest
    if step == 3:
        state = state_in
    else:
        state, *rest = rest
    pay, *rest = rest
    if step == 1:
        masses, *rest = rest
    near, turned = rest
    if step < 3:
        state[...] = state_in[...]
    fill_received(got, turned)
    if step == 1:
        masses[0:4] = turned[24:28]
        masses[4:8] = turned[28:32]

    def close(s, e, part):
        rows, mass = tile_rows(lambda r: near[2 * e + part, r : r + 1, :])
        return rows, mass, plan[HERE, 2 * s + part] == 1

    tiles = slot_pairs(
        0, pairs_of(plan), state, plan,
        sweep_received(turned, masses, SLOTS[step], used),
        lambda p: gather_blocks(turned, masses, SLOTS[step], plan, near, p),
        close, corrector(step, state, plan, sums),
        tuple([later[t] for t in range(3)] if step == 2 else blank(9 if step == 3 else 3)),
    )
    send(place_tiles(tiles), pay)


def last_kernel(got, ps, fr, irr, plan, kin, comb, close):
    count = plan[COUNT, 0]
    kin[...] = ps[...]
    comb[...] = fr[...]
    close[...] = irr[...]
    senders = got.shape[0]
    lane = lax.broadcasted_iota(jnp.int32, (senders, 128), 1)
    row = lax.broadcasted_iota(jnp.int32, (senders, 128), 0)
    spread = [pltpu.roll(got[:, 0, pl.ds(t * 128, 128)], 0, 1, stride=8, stride_axis=0) for t in range(9)]
    place = lane - row * 8

    def slot(s, _):
        at = pl.ds(pl.multiple_of(plan[BLOCK, s] * BS, BS), BS)
        for f in range(18):
            t, e = divmod(f, 2)
            start = e * 64 + s * 8
            keep = (((place - start) & 127) >> 3) == 0
            value = jnp.sum(jnp.where(keep, spread[t], 0.0), axis=0, keepdims=True)
            out = (kin, comb, close)[f // 6]
            out[f % 6 : f % 6 + 1, at] = pltpu.roll(value, (128 - start) & 127, 1)
        return 0

    lax.fori_loop(0, count, slot, 0)


def body(phase_space, force_rates, irregular, stellar_masses, levels, active, partner):
    shards = lax.axis_size("blk")
    columns_ = lax.axis_size("grp")
    everyone = shards * columns_
    me = lax.axis_index("blk").astype(jnp.int32).reshape(1)
    col = lax.axis_index("grp").astype(jnp.int32).reshape(1)
    tiles = lambda count: pltpu.VMEM((count, 8, 128), F32)
    array = lambda *shape: jax.ShapeDtypeStruct(shape, F32)
    near = lambda *shape: pltpu.VMEM(shape, F32)
    here = lambda x: pltpu.with_memory_space_constraint(x, pltpu.VMEM)
    plan_shape = jax.ShapeDtypeStruct((8, 32), jnp.int32)
    state_shape = near(NB + 1, 8, 128)

    def exchange(pay, axis):
        return lax.all_to_all(pay, axis, split_axis=0, concat_axis=0, tiled=True)

    packed, rates, mine = pl.pallas_call(
        pack_kernel,
        out_shape=(array(7 * NB + 8, BS), array(shards, 6 * NB, BS), near(NB, 16, BS)),
        in_specs=[VMEM, VMEM, VMEM, SMEM],
        out_specs=(VMEM, VMEM, VMEM),
        name="pack",
    )(phase_space, force_rates, stellar_masses[None, :], levels)
    table = lax.all_gather(packed, "blk", axis=0, tiled=False)
    levall = table[:, 7 * NB, :NB].astype(jnp.int32)
    table, rates = lax.optimization_barrier((table, rates))
    rates = exchange(rates, "blk")
    order_shape = jax.ShapeDtypeStruct(((shards + 3) * NB,), jnp.int32)
    state, pay, *orders = pl.pallas_call(
        first_kernel,
        out_shape=(state_shape, array(everyone, 1, 256), order_shape, order_shape),
        in_specs=[SMEM, SMEM, VMEM, VMEM, SMEM, SMEM, SMEM],
        out_specs=(VMEM, VMEM, SMEM, SMEM),
        scratch_shapes=[pltpu.VMEM((NB, 128, 128), F32), pltpu.SMEM((8, 32), jnp.int32)],
        name="first",
    )(me, col, here(table), here(mine), levels, levall, partner)
    masses = before = None
    for step in (1, 2, 3):
        cap = CAPS[step]
        lanes = (0, 256, 384, 384)[step]
        got = exchange(pay, ("blk", "grp"))
        ins = (me, here(table), here(rates), levels, levall, partner, orders[SENT[step]], here(state))
        specs = [SMEM, VMEM, VMEM, SMEM, SMEM, SMEM, SMEM, VMEM]
        out_shape = (near(cap, 8, 128), plan_shape)
        out_specs = (VMEM, SMEM)
        scratch = [pltpu.VMEM((shards + 1, QUANTITIES, NB, BS), F32)]
        if step == 2:
            out_shape += (near(3, 8, 128), near(2, 8, 128))
            out_specs += (VMEM, VMEM)
            scratch += [pltpu.SMEM((8, 32), jnp.int32)]
        elif step == 3:
            ins += (here(early),)
            specs += [VMEM]
        outs = pl.pallas_call(
            functools.partial(ahead_kernel, step),
            out_shape=out_shape,
            in_specs=specs,
            out_specs=out_specs,
            scratch_shapes=scratch,
            name=f"ahead{step}",
        )(*ins)
        sums, plan = outs[:2]
        if step == 2:
            early = outs[3]
        ins = (here(got), here(state), here(sums), plan)
        specs = [VMEM, VMEM, VMEM, SMEM]
        if step > 1:
            ins += (here(masses), before)
            specs += [VMEM, SMEM]
        if step == 2:
            ins += (here(outs[2]),)
            specs += [VMEM]
        pay_shape = array(everyone if step < 3 else columns_, 1, (0, 384, 384, 1152)[step])
        out_shape = {
            1: (state_shape, pay_shape, near(8, 8, everyone)), 2: (state_shape, pay_shape), 3: (pay_shape,),
        }[step]
        outs = pl.pallas_call(
            functools.partial(after_kernel, step),
            out_shape=out_shape,
            in_specs=specs,
            out_specs=tuple(VMEM for _ in out_shape),
            scratch_shapes=[
                tiles(4),
                pltpu.VMEM((lanes // 8, 8, everyone), F32),
            ],
            name=f"after{step}",
        )(*ins)
        if step == 1:
            state, pay, masses = outs
            before = plan
        elif step == 2:
            state, pay = outs
        else:
            (pay,) = outs
    got = exchange(pay, "grp")
    shape = array(6, W)
    return tuple(
        pl.pallas_call(
            last_kernel,
            out_shape=(shape, shape, shape),
            in_specs=[VMEM, VMEM, VMEM, VMEM, SMEM],
            out_specs=(VMEM, VMEM, VMEM),
            name="last",
        )(here(got), phase_space, force_rates, irregular, plan)
    )


def solution(mesh):
    in_specs = (
        P(None, "blk"), P(None, "blk"), P(None, "blk"), P("blk"), P("blk"), P(None, "blk"), P("blk"),
    )
    out_specs = (P(None, "blk"), P(None, "blk"), P(None, "blk"))
    return jax.shard_map(body, mesh=mesh, in_specs=in_specs, out_specs=out_specs, check_vma=False)
```

```python
import functools
import jax
import jax.numpy as jnp
from jax import lax
from jax.experimental import pallas as pl
from jax.experimental.pallas import tpu as pltpu
from jax.sharding import PartitionSpec as P

WIDE = 0.04
CLOSE = 0.0001
TICK = 0.125
NB = 16
BS = 128
W = NB * BS
F32 = jnp.float32
CAPS = (4, 6, 4, 8)
TOP = (0, 1, 0, 2)
SENT = (-1, 0, 1, 1)
SLOTS = (0, 4, 8, 8)

VMEM = pl.BlockSpec(memory_space=pltpu.VMEM)
SMEM = pl.BlockSpec(memory_space=pltpu.SMEM)


def pair(target, source, mass, soften, acc):
    r = [source[c] - target[c] for c in range(3)]
    w = [source[c] - target[c] for c in range(3, 6)]
    d = (r[0] * r[0] + soften) + r[1] * r[1] + r[2] * r[2]
    s = lax.rsqrt(d)
    s2 = s * s
    weight = (mass * s) * s2
    q = (r[0] * w[0] + r[1] * w[1] + r[2] * w[2]) * (s2 * 3.0)
    acc = list(acc)
    for c in range(3):
        acc[c] = acc[c] + weight * r[c]
        acc[3 + c] = acc[3 + c] + weight * (w[c] - q * r[c])
    return tuple(acc)


def pair_split(target, source, mass, acc):
    r = [source[c] - target[c] for c in range(3)]
    w = [source[c] - target[c] for c in range(3, 6)]
    dd = r[0] * r[0] + r[1] * r[1] + r[2] * r[2]
    rw = (r[0] * w[0] + r[1] * w[1] + r[2] * w[2]) * 3.0
    acc = list(acc)
    for soften, sign in ((CLOSE, 1.0), (WIDE, -1.0)):
        s = lax.rsqrt(dd + soften)
        s2 = s * s
        weight = (mass * s) * (s2 * sign)
        q = rw * s2
        for c in range(3):
            acc[c] = acc[c] + weight * r[c]
            acc[3 + c] = acc[3 + c] + weight * (w[c] - q * r[c])
    return tuple(acc)


def zeros():
    return tuple(jnp.zeros((8, 128), F32) for _ in range(6))


BLOCK, PLACE, LEVEL, SHARD, ROW, HERE, COUNT = range(7)


def fill_slots(lev, top, cap, plan):
    for s in range(cap):
        plan[BLOCK, s] = 0
        plan[PLACE, s] = -1000
        plan[LEVEL, s] = 0
    count = jnp.int32(0)
    for group in ((2,), (0, 1)) if top == 2 else ((0, 1),):
        ones = [jnp.int32(0), jnp.int32(4)]
        for k in range(NB):
            level = lev[k]
            place = jnp.where(level == 0, ones[0], jnp.where(level == 1, ones[1], -1000))
            live = (level == 2) if group == (2,) else level <= min(top, 1)
            plan[BLOCK, count] = k
            plan[PLACE, count] = jnp.where(live, place, -1000)
            plan[LEVEL, count] = jnp.where(live, level, 0)
            count = count + live.astype(jnp.int32)
            ones[0] = ones[0] + (level == 0).astype(jnp.int32)
            ones[1] = ones[1] + (level == 1).astype(jnp.int32)
        if group == (2,):
            plan[COUNT, 2] = count
    plan[COUNT, 0] = count


def fill_near(plan, cap, own, levall, partner, sent):
    def slot(s, _):
        k = plan[BLOCK, s]
        q = partner[k] // NB
        level = levall[q, k]
        place = jnp.where(level == 0, 0, 4)
        for e in range(NB):
            place = place + ((levall[q, e] == level) & (e < k)).astype(jnp.int32)
        ours = plan[LEVEL, s] <= sent
        theirs = (q != own) & (level <= sent)
        for e, (b, row, here) in enumerate(((own, plan[PLACE, s], ours), (q, place, theirs))):
            plan[SHARD, 2 * s + e] = b
            plan[ROW, 2 * s + e] = jnp.clip(jnp.where(here, row, 0), 0, 3 if sent == 0 else 7)
            plan[HERE, 2 * s + e] = here.astype(jnp.int32)
        return 0

    lax.fori_loop(0, cap, slot, 0)


def span_of(level):
    return jnp.where(level == 0, TICK, jnp.where(level == 1, 2 * TICK, 4 * TICK)).astype(F32)


XS, MS, VS, AS, JS = (0, 1, 2), 3, (4, 5, 6), (8, 9, 10), (11, 12, 13)


def columns(tile):
    return tuple(
        [tile[:, c : c + 1] for c in group] for group in (XS, VS, AS, JS)
    )


def forecast(x, v, a, j, t):
    t2 = t * t * 0.5
    t3 = t * t * t * (1.0 / 6.0)
    xp = [x[c] + v[c] * t + a[c] * t2 + j[c] * t3 for c in range(3)]
    vp = [v[c] + a[c] * t + j[c] * t2 for c in range(3)]
    return xp + vp


QUANTITIES = 7


def fill_sources(table, rates, predicted, t):
    t2 = t * t * 0.5
    t3 = t * t * t / 6.0

    def shard(b, _):
        x, m, v = [[table[b, pl.ds(NB * f, NB), :] for f in group] for group in ((0, 1, 2), (3,), (4, 5, 6))]
        a, j = [[rates[b, pl.ds(NB * f, NB), :] for f in group] for group in ((0, 1, 2), (3, 4, 5))]
        for c in range(3):
            predicted[b, c] = x[c] + v[c] * t + a[c] * t2 + j[c] * t3
            predicted[b, 4 + c] = v[c] + a[c] * t + j[c] * t2
        predicted[b, 3] = m[0]
        return 0

    lax.fori_loop(0, table.shape[0], shard, 0)
    for f in range(QUANTITIES):
        predicted[table.shape[0], f] = jnp.zeros((NB, BS), F32)


def target_of(state, plan, s):
    x, v, a, j = columns(state[plan[BLOCK, s]])
    ahead = forecast(x, v, a, j, span_of(plan[LEVEL, s]))
    return [jnp.broadcast_to(value, (8, 128)) for value in ahead]


def broad(row):
    return jnp.broadcast_to(row, (8, 128))


def tile_rows(tile):
    return [broad(tile(r)) for r in (0, 1, 2, 4, 5, 6)], broad(tile(3))


def from_table(table, b, k):
    return tile_rows(lambda r: table[b, pl.ds(NB * r + k, 1), :])


def from_predicted(predicted, b, k):
    return tile_rows(lambda r: predicted[b, r, pl.ds(k, 1), :])


def slot_pairs(first, last, state, plan, sweep, prepare, close, sink, carry):
    def two(p, carry):
        goal = [target_of(state, plan, 2 * p + e) for e in range(2)]
        prepare(p)
        acc = sweep(goal)
        for e in range(2):
            s = 2 * p + e
            near = zeros()
            for part in range(2):
                rows, mass, wanted = close(s, e, part)
                near = pair_split(goal[e], rows, mass * jnp.where(wanted, 1.0, 0.0).astype(F32), near)
            total, inner = (
                [jnp.sum(value, axis=1, keepdims=True) for value in group] for group in (acc[e], near)
            )
            carry = sink(s, total, inner, carry)
        return carry

    return lax.fori_loop(first, last, two, carry)


def pairs_of(plan):
    return (plan[COUNT, 0] + 1) // 2


def sweep_table(groups, load):
    def sweep(goal):
        def group(b, acc):
            for k in range(NB):
                rows, mass = load(b, k)
                acc = tuple(pair(goal[e], rows, mass, WIDE, acc[e]) for e in range(2))
            return acc

        return lax.fori_loop(0, groups, group, (zeros(), zeros()))

    return sweep


def fill_received(got, turned):
    senders, _, lanes = got.shape
    for t in range(lanes // 128):
        for half in range(senders // 128):
            part = got[pl.ds(half * 128, 128), 0, pl.ds(t * 128, 128)]
            turned[pl.ds(t * 16, 16), :, pl.ds(half * 128, 128)] = part.T.reshape(16, 8, 128)


def sweep_received(turned, mass, slots_in, used):
    def sweep(goal):
        def slot(s, acc):
            for i in range(8):
                for half in range(turned.shape[2] // 128):
                    at = pl.ds(half * 128, 128)
                    rows = [broad(turned[f * slots_in + s, i : i + 1, at]) for f in range(6)]
                    m = broad(mass[s, i : i + 1, at])
                    acc = tuple(pair(goal[e], rows, m, WIDE, acc[e]) for e in range(2))
            return acc

        return lax.fori_loop(0, used, slot, (zeros(), zeros()))

    return sweep


def gather_blocks(turned, mass, slots_in, plan, near, p):
    lane = lax.broadcasted_iota(jnp.int32, (8, 128), 1)
    row = lax.broadcasted_iota(jnp.int32, (8, 128), 0)
    keep = lane // 16 == row
    for item in range(4):
        b = plan[SHARD, 4 * p + item]
        place = plan[ROW, 4 * p + item]
        half = pl.ds(pl.multiple_of((b // 8) * 128, 128), 128)
        shift = lax.rem(128 - lax.rem(b, 8) * 16, 128)
        for r, f in ((0, 0), (1, 1), (2, 2), (4, 3), (5, 4), (6, 5), (3, None)):
            tile = mass[place, :, half] if f is None else turned[f * slots_in + place, :, half]
            tile = pltpu.roll(pltpu.roll(tile, shift, 1), 0, 1, stride=16, stride_axis=0)
            near[item, r : r + 1, :] = jnp.sum(jnp.where(keep, tile, 0.0), axis=0, keepdims=True)


def fill_tiles(parts, tiles, width):
    per = 128 // width
    tiles = list(tiles)
    lane = lax.broadcasted_iota(jnp.int32, (8, 128), 1)
    for f, slot, column in parts:
        t = f // per
        tiles[t] = jnp.where(lane == (f % per) * width + slot * 8, column, tiles[t])
    return tiles


def blank(count):
    return [jnp.zeros((8, 128), F32) for _ in range(count)]


def place_tiles(tiles):
    tiles = [pltpu.roll(tile, 0, 1, stride=1, stride_axis=0) for tile in tiles]
    return [jnp.sum(tile, axis=0, keepdims=True) for tile in tiles]


def send(tiles, pay):
    for t, tile in enumerate(tiles):
        full = jnp.broadcast_to(tile[None], (pay.shape[0], 1, 128))
        pay[:, :, pl.ds(t * 128, 128)] = full


def corrector(step, state, plan, sums):
    lane = lax.broadcasted_iota(jnp.int32, (8, 128), 1)

    def sink(s, total, inner, carry):
        k = plan[BLOCK, s]
        t = span_of(plan[LEVEL, s])
        tile = state[k]
        x, v, a, j = columns(tile)
        if sums is not None:
            before = sums[s]
            total = [total[c] + before[:, c : c + 1] for c in range(6)]
            inner = [inner[c] + before[:, 8 + c : 9 + c] for c in range(6)]
        total = [total[c] + inner[c] for c in range(6)]
        half = t * 0.5
        twelfth = t * t * (1.0 / 12.0)
        v1 = [v[c] + (a[c] + total[c]) * half + (j[c] - total[3 + c]) * twelfth for c in range(3)]
        x1 = [x[c] + (v[c] + v1[c]) * half + (a[c] - total[c]) * twelfth for c in range(3)]
        if step == 3:
            parts = [(f, s, column) for f, column in enumerate(x1 + v1 + total + inner)]
            return tuple(fill_tiles(parts, carry, 64))
        fresh = tile
        for at, column in zip(XS + VS + AS + JS, x1 + v1 + total):
            fresh = jnp.where(lane == at, column, fresh)
        state[jnp.where(s < plan[COUNT, 0], k, NB)] = fresh
        ahead = forecast(x1, v1, total[:3], total[3:], TICK)
        if step == 0:
            ahead = ahead + [tile[:, MS : MS + 1]]
        parts = [(f, plan[PLACE, s], column) for f, column in enumerate(ahead)]
        return tuple(fill_tiles(parts, carry, 32 if step == 0 else 64))

    return sink


def fill_later(state, lev, later):
    parts = []
    seen = jnp.int32(4)
    for k in range(NB):
        one = lev[k] == 1
        mark = jnp.where(one, seen, -1000)
        x, v, a, j = columns(state[k])
        for f, column in enumerate(forecast(x, v, a, j, 2 * TICK)):
            parts.append((f, mark, column))
        seen = seen + one.astype(jnp.int32)
    for t, tile in enumerate(fill_tiles(parts, blank(3), 64)):
        later[t] = tile


def pack_kernel(ps, fr, mass, lev, first, rates, own):
    x, v, a, j = ps[0:3, :], ps[3:6, :], fr[0:3, :], fr[3:6, :]
    t2 = TICK * TICK * 0.5
    xp = x + v * TICK + a * t2 + j * (TICK * TICK * TICK / 6.0)
    vp = v + a * TICK + j * t2
    ap = a + j * TICK
    lane = lax.broadcasted_iota(jnp.int32, (8, BS), 1)
    levels = jnp.zeros((8, BS), F32)
    for k in range(NB):
        levels = jnp.where(lane == k, lev[k].astype(F32), levels)
    first[7 * NB : 7 * NB + 8, :] = levels
    for k in range(NB):
        at = slice(k * BS, k * BS + BS)
        for c in range(3):
            first[NB * c + k : NB * c + k + 1, :] = xp[c : c + 1, at]
            first[NB * (4 + c) + k : NB * (4 + c) + k + 1, :] = vp[c : c + 1, at]
            rates[0, NB * c + k : NB * c + k + 1, :] = ap[c : c + 1, at]
            rates[0, NB * (3 + c) + k : NB * (3 + c) + k + 1, :] = j[c : c + 1, at]
        first[NB * 3 + k : NB * 3 + k + 1, :] = mass[:, at]
        own[k] = jnp.zeros((16, BS), F32)
        own[k, 0:3, :] = x[:, at]
        own[k, 3:4, :] = mass[:, at]
        own[k, 4:7, :] = v[:, at]
        own[k, 8:14, :] = fr[:, at]
    for b in range(1, rates.shape[0]):
        rates[b] = rates[0]


def first_kernel(me, col, table, mine, lev, levall, partner, state, pay, order0, order1, turned, plan):
    me = me[0]
    col = pl.multiple_of(col[0] * 8, 8)
    fill_slots(lev, TOP[0], CAPS[0], plan)
    for k in range(NB):
        turned[k, :, 0:16] = mine[k].T
    for k in range(NB):
        state[k] = turned[k, pl.ds(col, 8), :]
    masses = []
    seen = jnp.int32(0)
    for k in range(NB):
        one = lev[k] == 1
        masses.append((7, jnp.where(one, seen, -1000), state[k][:, MS : MS + 1]))
        seen = seen + one.astype(jnp.int32)

    def close(s, e, part):
        k = plan[BLOCK, s]
        b = partner[k] // NB if part else me
        rows, mass = from_table(table, b, k)
        return rows, mass, b != me if part else jnp.bool_(True)

    shards = table.shape[0]
    orders = (order0, order1)

    def sweep(goal):
        def group(b, carry):
            acc, counts = carry
            for k in range(NB):
                rows, mass = from_table(table, b, k)
                acc = tuple(pair(goal[e], rows, mass, WIDE, acc[e]) for e in range(2))
                for order, count in zip(orders, counts):
                    order[count] = b * NB + k
                counts = tuple(counts[e] + (levall[b, k] > e).astype(jnp.int32) for e in range(2))
            return acc, counts

        start = ((zeros(), zeros()), (jnp.int32(0), jnp.int32(0)))
        acc, counts = lax.fori_loop(0, shards, group, start)
        for order, count in zip(orders, counts):
            for e in range(NB):
                order[count + e] = shards * NB
            order[(shards + 2) * NB] = count
        return acc

    tiles = slot_pairs(
        0, pairs_of(plan), state, plan, sweep,
        lambda p: None, close, corrector(0, state, plan, None),
        tuple(fill_tiles(masses, blank(2), 32)),
    )
    send(place_tiles(tiles), pay)


def ahead_sums(step, first, last, me, plan, order, predicted, state, sums):
    lane = lax.broadcasted_iota(jnp.int32, (8, 128), 1)

    def load(g, e):
        index = order[g * NB + e]
        return from_predicted(predicted, index // NB, lax.rem(index, NB))

    def close(s, e, part):
        rows, mass = from_predicted(predicted, plan[SHARD, 2 * s + part], plan[BLOCK, s])
        other = plan[SHARD, 2 * s + 1] != me if part else jnp.bool_(True)
        return rows, mass, other & (plan[HERE, 2 * s + part] == 0)

    def sink(s, total, inner, carry):
        tile = jnp.zeros((8, 128), F32)
        for at, group in ((0, total), (8, inner)):
            for c in range(6):
                tile = jnp.where(lane == at + c, group[c], tile)
        sums[s] = tile
        return carry

    groups = (order[order.shape[0] - NB] + NB - 1) // NB
    slot_pairs(first, last, state, plan, sweep_table(groups, load), lambda p: None, close, sink, 0)


def early_pairs(plan):
    return jnp.minimum(plan[COUNT, 2] // 2, 1)


def ahead_kernel(step, me, table, rates, lev, levall, partner, order, state, *rest):
    if step == 1:
        sums, plan, predicted = rest
    elif step == 2:
        sums, plan, later, early, predicted, plan3 = rest
    else:
        early, sums, plan, predicted = rest
    me = me[0]
    fill_slots(lev, TOP[step], CAPS[step], plan)
    fill_near(plan, CAPS[step], me, levall, partner, SENT[step])
    fill_sources(table, rates, predicted, step * TICK)
    first = 0
    if step == 3:
        first = early_pairs(plan)
        sums[0:2] = early[...]
    ahead_sums(step, first, pairs_of(plan), me, plan, order, predicted, state, sums)
    if step == 2:
        fill_later(state, lev, later)
        fill_slots(lev, TOP[3], CAPS[3], plan3)
        fill_near(plan3, 2, me, levall, partner, SENT[3])
        fill_sources(table, rates, predicted, 3 * TICK)
        early[...] = jnp.zeros((2, 8, 128), F32)
        ahead_sums(3, 0, early_pairs(plan3), me, plan3, order, predicted, state, early)
    if step == 1:
        level = table[:, 7 * NB, :]
        lane = lax.broadcasted_iota(jnp.int32, level.shape, 1)
        one = jnp.where((level == 1.0) & (lane < NB), 1.0, 0.0).astype(F32)
        plan[COUNT, 1] = jnp.max(jnp.sum(one, axis=1, keepdims=True)).astype(jnp.int32)


def after_kernel(step, got, state_in, sums, plan, *rest):
    later = None
    used = SLOTS[step]
    if step > 1:
        masses, before, *rest = rest
        used = jnp.minimum(4 + before[COUNT, 1], used)
    if step == 2:
        later, *rest = rest
    if step == 3:
        state = state_in
    else:
        state, *rest = rest
    pay, *rest = rest
    if step == 1:
        masses, *rest = rest
    near, turned = rest
    if step < 3:
        state[...] = state_in[...]
    fill_received(got, turned)
    if step == 1:
        masses[0:4] = turned[24:28]
        masses[4:8] = turned[28:32]

    def close(s, e, part):
        rows, mass = tile_rows(lambda r: near[2 * e + part, r : r + 1, :])
        return rows, mass, plan[HERE, 2 * s + part] == 1

    tiles = slot_pairs(
        0, pairs_of(plan), state, plan,
        sweep_received(turned, masses, SLOTS[step], used),
        lambda p: gather_blocks(turned, masses, SLOTS[step], plan, near, p),
        close, corrector(step, state, plan, sums),
        tuple([later[t] for t in range(3)] if step == 2 else blank(9 if step == 3 else 3)),
    )
    send(place_tiles(tiles), pay)


def last_kernel(got, ps, fr, irr, plan, kin, comb, close):
    count = plan[COUNT, 0]
    kin[...] = ps[...]
    comb[...] = fr[...]
    close[...] = irr[...]
    senders = got.shape[0]
    lane = lax.broadcasted_iota(jnp.int32, (senders, 128), 1)
    row = lax.broadcasted_iota(jnp.int32, (senders, 128), 0)
    spread = [pltpu.roll(got[:, 0, pl.ds(t * 128, 128)], 0, 1, stride=8, stride_axis=0) for t in range(9)]
    place = lane - row * 8

    def slot(s, _):
        at = pl.ds(pl.multiple_of(plan[BLOCK, s] * BS, BS), BS)
        for f in range(18):
            t, e = divmod(f, 2)
            start = e * 64 + s * 8
            keep = (((place - start) & 127) >> 3) == 0
            value = jnp.sum(jnp.where(keep, spread[t], 0.0), axis=0, keepdims=True)
            out = (kin, comb, close)[f // 6]
            out[f % 6 : f % 6 + 1, at] = pltpu.roll(value, (128 - start) & 127, 1)
        return 0

    lax.fori_loop(0, count, slot, 0)


def body(phase_space, force_rates, irregular, stellar_masses, levels, active, partner):
    shards = lax.axis_size("blk")
    columns_ = lax.axis_size("grp")
    everyone = shards * columns_
    me = lax.axis_index("blk").astype(jnp.int32).reshape(1)
    col = lax.axis_index("grp").astype(jnp.int32).reshape(1)
    tiles = lambda count: pltpu.VMEM((count, 8, 128), F32)
    array = lambda *shape: jax.ShapeDtypeStruct(shape, F32)
    near = lambda *shape: pltpu.VMEM(shape, F32)
    here = lambda x: pltpu.with_memory_space_constraint(x, pltpu.VMEM)
    kept = lambda x: pltpu.with_memory_space_constraint(x, pltpu.SMEM)
    plan_shape = pltpu.SMEM((8, 32), jnp.int32)
    state_shape = near(NB + 1, 8, 128)

    def exchange(pay, axis):
        return lax.all_to_all(pay, axis, split_axis=0, concat_axis=0, tiled=True)

    packed, rates, mine = pl.pallas_call(
        pack_kernel,
        out_shape=(array(7 * NB + 8, BS), array(shards, 6 * NB, BS), near(NB, 16, BS)),
        in_specs=[VMEM, VMEM, VMEM, SMEM],
        out_specs=(VMEM, VMEM, VMEM),
        name="pack",
    )(phase_space, force_rates, stellar_masses[None, :], levels)
    table = lax.all_gather(packed, "blk", axis=0, tiled=False)
    levall = table[:, 7 * NB, :NB].astype(jnp.int32)
    table, rates = lax.optimization_barrier((table, rates))
    rates = exchange(rates, "blk")
    order_shape = pltpu.SMEM(((shards + 3) * NB,), jnp.int32)
    state, pay, *orders = pl.pallas_call(
        first_kernel,
        out_shape=(state_shape, array(everyone, 1, 256), order_shape, order_shape),
        in_specs=[SMEM, SMEM, VMEM, VMEM, SMEM, SMEM, SMEM],
        out_specs=(VMEM, VMEM, SMEM, SMEM),
        scratch_shapes=[pltpu.VMEM((NB, 128, 128), F32), pltpu.SMEM((8, 32), jnp.int32)],
        name="first",
    )(me, col, here(table), here(mine), levels, levall, partner)
    masses = before = None
    for step in (1, 2, 3):
        cap = CAPS[step]
        lanes = (0, 256, 384, 384)[step]
        got = exchange(pay, ("blk", "grp"))
        ins = (me, here(table), here(rates), levels, levall, partner, kept(orders[SENT[step]]), here(state))
        specs = [SMEM, VMEM, VMEM, SMEM, SMEM, SMEM, SMEM, VMEM]
        out_shape = (near(cap, 8, 128), plan_shape)
        out_specs = (VMEM, SMEM)
        scratch = [pltpu.VMEM((shards + 1, QUANTITIES, NB, BS), F32)]
        if step == 2:
            out_shape += (near(3, 8, 128), near(2, 8, 128))
            out_specs += (VMEM, VMEM)
            scratch += [pltpu.SMEM((8, 32), jnp.int32)]
        elif step == 3:
            ins += (here(early),)
            specs += [VMEM]
        outs = pl.pallas_call(
            functools.partial(ahead_kernel, step),
            out_shape=out_shape,
            in_specs=specs,
            out_specs=out_specs,
            scratch_shapes=scratch,
            name=f"ahead{step}",
        )(*ins)
        sums, plan = outs[:2]
        if step == 2:
            early = outs[3]
        ins = (here(got), here(state), here(sums), kept(plan))
        specs = [VMEM, VMEM, VMEM, SMEM]
        if step > 1:
            ins += (here(masses), kept(before))
            specs += [VMEM, SMEM]
        if step == 2:
            ins += (here(outs[2]),)
            specs += [VMEM]
        pay_shape = array(everyone if step < 3 else columns_, 1, (0, 384, 384, 1152)[step])
        out_shape = {
            1: (state_shape, pay_shape, near(8, 8, everyone)), 2: (state_shape, pay_shape), 3: (pay_shape,),
        }[step]
        outs = pl.pallas_call(
            functools.partial(after_kernel, step),
            out_shape=out_shape,
            in_specs=specs,
            out_specs=tuple(VMEM for _ in out_shape),
            scratch_shapes=[
                tiles(4),
                pltpu.VMEM((lanes // 8, 8, everyone), F32),
            ],
            name=f"after{step}",
        )(*ins)
        if step == 1:
            state, pay, masses = outs
            before = plan
        elif step == 2:
            state, pay = outs
        else:
            (pay,) = outs
    got = exchange(pay, "grp")
    shape = array(6, W)
    return tuple(
        pl.pallas_call(
            last_kernel,
            out_shape=(shape, shape, shape),
            in_specs=[VMEM, VMEM, VMEM, VMEM, SMEM],
            out_specs=(VMEM, VMEM, VMEM),
            name="last",
        )(here(got), phase_space, force_rates, irregular, kept(plan))
    )


def solution(mesh):
    in_specs = (
        P(None, "blk"), P(None, "blk"), P(None, "blk"), P("blk"), P("blk"), P(None, "blk"), P("blk"),
    )
    out_specs = (P(None, "blk"), P(None, "blk"), P(None, "blk"))
    return jax.shard_map(body, mesh=mesh, in_specs=in_specs, out_specs=out_specs, check_vma=False)
```

```python
import functools
import jax
import jax.numpy as jnp
from jax import lax
from jax.experimental import pallas as pl
from jax.experimental.pallas import tpu as pltpu
from jax.sharding import PartitionSpec as P

WIDE = 0.04
CLOSE = 0.0001
TICK = 0.125
NB = 16
SHIFT = 4
BS = 128
W = NB * BS
F32 = jnp.float32
CAPS = (4, 6, 4, 8)
TOP = (0, 1, 0, 2)
SENT = (-1, 0, 1, 1)
SLOTS = (0, 4, 8, 8)

VMEM = pl.BlockSpec(memory_space=pltpu.VMEM)
SMEM = pl.BlockSpec(memory_space=pltpu.SMEM)


def pair(target, source, mass, soften, acc):
    r = [source[c] - target[c] for c in range(3)]
    w = [source[c] - target[c] for c in range(3, 6)]
    d = (r[0] * r[0] + soften) + r[1] * r[1] + r[2] * r[2]
    s = lax.rsqrt(d)
    s2 = s * s
    weight = (mass * s) * s2
    q = (r[0] * w[0] + r[1] * w[1] + r[2] * w[2]) * (s2 * 3.0)
    acc = list(acc)
    for c in range(3):
        acc[c] = acc[c] + weight * r[c]
        acc[3 + c] = acc[3 + c] + weight * (w[c] - q * r[c])
    return tuple(acc)


def pair_split(target, source, mass, acc):
    r = [source[c] - target[c] for c in range(3)]
    w = [source[c] - target[c] for c in range(3, 6)]
    dd = r[0] * r[0] + r[1] * r[1] + r[2] * r[2]
    rw = (r[0] * w[0] + r[1] * w[1] + r[2] * w[2]) * 3.0
    acc = list(acc)
    for soften, sign in ((CLOSE, 1.0), (WIDE, -1.0)):
        s = lax.rsqrt(dd + soften)
        s2 = s * s
        weight = (mass * s) * (s2 * sign)
        q = rw * s2
        for c in range(3):
            acc[c] = acc[c] + weight * r[c]
            acc[3 + c] = acc[3 + c] + weight * (w[c] - q * r[c])
    return tuple(acc)


def zeros():
    return tuple(jnp.zeros((8, 128), F32) for _ in range(6))


BLOCK, PLACE, LEVEL, SHARD, ROW, HERE, COUNT = range(7)
OWN, MATE, RANK, MATELEVEL, ME = range(5)


def fill_slots(lev, top, cap, plan):
    for s in range(cap):
        plan[BLOCK, s] = 0
        plan[PLACE, s] = -1000
        plan[LEVEL, s] = 0
    count = jnp.int32(0)
    for group in ((2,), (0, 1)) if top == 2 else ((0, 1),):
        ones = [jnp.int32(0), jnp.int32(4)]
        for k in range(NB):
            level = lev(k)
            place = jnp.where(level == 0, ones[0], jnp.where(level == 1, ones[1], -1000))
            live = (level == 2) if group == (2,) else level <= min(top, 1)
            plan[BLOCK, count] = k
            plan[PLACE, count] = jnp.where(live, place, -1000)
            plan[LEVEL, count] = jnp.where(live, level, 0)
            count = count + live.astype(jnp.int32)
            ones[0] = ones[0] + (level == 0).astype(jnp.int32)
            ones[1] = ones[1] + (level == 1).astype(jnp.int32)
        if group == (2,):
            plan[COUNT, 2] = count
    plan[COUNT, 0] = count


def fill_near(plan, cap, known, sent):
    me = known[ME, 0]

    def slot(s, _):
        k = plan[BLOCK, s]
        q = known[MATE, k]
        ours = plan[LEVEL, s] <= sent
        theirs = (q != me) & (known[MATELEVEL, k] <= sent)
        for e, (b, row, here) in enumerate(((me, plan[PLACE, s], ours), (q, known[RANK, k], theirs))):
            plan[SHARD, 2 * s + e] = b
            plan[ROW, 2 * s + e] = jnp.clip(jnp.where(here, row, 0), 0, 3 if sent == 0 else 7)
            plan[HERE, 2 * s + e] = here.astype(jnp.int32)
        return 0

    lax.fori_loop(0, cap, slot, 0)


def span_of(level):
    return jnp.where(level == 0, TICK, jnp.where(level == 1, 2 * TICK, 4 * TICK)).astype(F32)


XS, MS, VS, AS, JS = (0, 1, 2), 3, (4, 5, 6), (8, 9, 10), (11, 12, 13)


def columns(tile):
    return tuple(
        [tile[:, c : c + 1] for c in group] for group in (XS, VS, AS, JS)
    )


def forecast(x, v, a, j, t):
    t2 = t * t * 0.5
    t3 = t * t * t * (1.0 / 6.0)
    xp = [x[c] + v[c] * t + a[c] * t2 + j[c] * t3 for c in range(3)]
    vp = [v[c] + a[c] * t + j[c] * t2 for c in range(3)]
    return xp + vp


QUANTITIES = 7


def fill_sources(table, rates, predicted, t):
    t2 = t * t * 0.5
    t3 = t * t * t / 6.0

    def shard(b, _):
        x, m, v = [[table[b, pl.ds(NB * f, NB), :] for f in group] for group in ((0, 1, 2), (3,), (4, 5, 6))]
        a, j = [[rates[b, pl.ds(NB * f, NB), :] for f in group] for group in ((0, 1, 2), (3, 4, 5))]
        for c in range(3):
            predicted[b, c] = x[c] + v[c] * t + a[c] * t2 + j[c] * t3
            predicted[b, 4 + c] = v[c] + a[c] * t + j[c] * t2
        predicted[b, 3] = m[0]
        return 0

    lax.fori_loop(0, table.shape[0], shard, 0)
    for f in range(QUANTITIES):
        predicted[table.shape[0], f] = jnp.zeros((NB, BS), F32)


def target_of(state, plan, s):
    x, v, a, j = columns(state[plan[BLOCK, s]])
    ahead = forecast(x, v, a, j, span_of(plan[LEVEL, s]))
    return [jnp.broadcast_to(value, (8, 128)) for value in ahead]


def broad(row):
    return jnp.broadcast_to(row, (8, 128))


def tile_rows(tile):
    return [broad(tile(r)) for r in (0, 1, 2, 4, 5, 6)], broad(tile(3))


def from_table(table, b, k):
    return tile_rows(lambda r: table[b, pl.ds(NB * r + k, 1), :])


def from_predicted(predicted, b, k):
    return tile_rows(lambda r: predicted[b, r, pl.ds(k, 1), :])


def slot_pairs(first, last, state, plan, sweep, prepare, close, sink, carry):
    def two(p, carry):
        goal = [target_of(state, plan, 2 * p + e) for e in range(2)]
        prepare(p)
        acc = sweep(goal)
        for e in range(2):
            s = 2 * p + e
            near = zeros()
            for part in range(2):
                rows, mass, wanted = close(s, e, part)
                near = pair_split(goal[e], rows, mass * jnp.where(wanted, 1.0, 0.0).astype(F32), near)
            total, inner = (
                [jnp.sum(value, axis=1, keepdims=True) for value in group] for group in (acc[e], near)
            )
            carry = sink(s, total, inner, carry)
        return carry

    return lax.fori_loop(first, last, two, carry)


def pairs_of(plan):
    return (plan[COUNT, 0] + 1) // 2


def sweep_table(groups, load):
    def sweep(goal):
        def group(b, acc):
            for k in range(NB):
                rows, mass = load(b, k)
                acc = tuple(pair(goal[e], rows, mass, WIDE, acc[e]) for e in range(2))
            return acc

        return lax.fori_loop(0, groups, group, (zeros(), zeros()))

    return sweep


def fill_received(got, turned):
    senders, _, lanes = got.shape
    for t in range(lanes // 128):
        for half in range(senders // 128):
            part = got[pl.ds(half * 128, 128), 0, pl.ds(t * 128, 128)]
            turned[pl.ds(t * 16, 16), :, pl.ds(half * 128, 128)] = part.T.reshape(16, 8, 128)


def sweep_received(turned, mass, slots_in, used):
    def sweep(goal):
        def slot(s, acc):
            for i in range(8):
                for half in range(turned.shape[2] // 128):
                    at = pl.ds(half * 128, 128)
                    rows = [broad(turned[f * slots_in + s, i : i + 1, at]) for f in range(6)]
                    m = broad(mass[s, i : i + 1, at])
                    acc = tuple(pair(goal[e], rows, m, WIDE, acc[e]) for e in range(2))
            return acc

        return lax.fori_loop(0, used, slot, (zeros(), zeros()))

    return sweep


def gather_blocks(turned, mass, slots_in, plan, near, p):
    lane = lax.broadcasted_iota(jnp.int32, (8, 128), 1)
    row = lax.broadcasted_iota(jnp.int32, (8, 128), 0)
    keep = lane // 16 == row
    for item in range(4):
        b = plan[SHARD, 4 * p + item]
        place = plan[ROW, 4 * p + item]
        half = pl.ds(pl.multiple_of((b // 8) * 128, 128), 128)
        shift = lax.rem(128 - lax.rem(b, 8) * 16, 128)
        for r, f in ((0, 0), (1, 1), (2, 2), (4, 3), (5, 4), (6, 5), (3, None)):
            tile = mass[place, :, half] if f is None else turned[f * slots_in + place, :, half]
            tile = pltpu.roll(pltpu.roll(tile, shift, 1), 0, 1, stride=16, stride_axis=0)
            near[item, r : r + 1, :] = jnp.sum(jnp.where(keep, tile, 0.0), axis=0, keepdims=True)


def fill_tiles(parts, tiles, width):
    per = 128 // width
    tiles = list(tiles)
    lane = lax.broadcasted_iota(jnp.int32, (8, 128), 1)
    for f, slot, column in parts:
        t = f // per
        tiles[t] = jnp.where(lane == (f % per) * width + slot * 8, column, tiles[t])
    return tiles


def blank(count):
    return [jnp.zeros((8, 128), F32) for _ in range(count)]


def place_tiles(tiles):
    tiles = [pltpu.roll(tile, 0, 1, stride=1, stride_axis=0) for tile in tiles]
    return [jnp.sum(tile, axis=0, keepdims=True) for tile in tiles]


def send(tiles, pay):
    for t, tile in enumerate(tiles):
        full = jnp.broadcast_to(tile[None], (pay.shape[0], 1, 128))
        pay[:, :, pl.ds(t * 128, 128)] = full


def corrector(step, state, plan, sums):
    lane = lax.broadcasted_iota(jnp.int32, (8, 128), 1)

    def sink(s, total, inner, carry):
        k = plan[BLOCK, s]
        t = span_of(plan[LEVEL, s])
        tile = state[k]
        x, v, a, j = columns(tile)
        if sums is not None:
            before = sums[s]
            total = [total[c] + before[:, c : c + 1] for c in range(6)]
            inner = [inner[c] + before[:, 8 + c : 9 + c] for c in range(6)]
        total = [total[c] + inner[c] for c in range(6)]
        half = t * 0.5
        twelfth = t * t * (1.0 / 12.0)
        v1 = [v[c] + (a[c] + total[c]) * half + (j[c] - total[3 + c]) * twelfth for c in range(3)]
        x1 = [x[c] + (v[c] + v1[c]) * half + (a[c] - total[c]) * twelfth for c in range(3)]
        if step == 3:
            parts = [(f, s, column) for f, column in enumerate(x1 + v1 + total + inner)]
            return tuple(fill_tiles(parts, carry, 64))
        fresh = tile
        for at, column in zip(XS + VS + AS + JS, x1 + v1 + total):
            fresh = jnp.where(lane == at, column, fresh)
        state[jnp.where(s < plan[COUNT, 0], k, NB)] = fresh
        ahead = forecast(x1, v1, total[:3], total[3:], TICK)
        if step == 0:
            ahead = ahead + [tile[:, MS : MS + 1]]
        parts = [(f, plan[PLACE, s], column) for f, column in enumerate(ahead)]
        return tuple(fill_tiles(parts, carry, 32 if step == 0 else 64))

    return sink


def fill_later(state, lev, later):
    parts = []
    seen = jnp.int32(4)
    for k in range(NB):
        one = lev(k) == 1
        mark = jnp.where(one, seen, -1000)
        x, v, a, j = columns(state[k])
        for f, column in enumerate(forecast(x, v, a, j, 2 * TICK)):
            parts.append((f, mark, column))
        seen = seen + one.astype(jnp.int32)
    for t, tile in enumerate(fill_tiles(parts, blank(3), 64)):
        later[t] = tile


def pack_kernel(ps, fr, mass, lev, first, rates, own):
    x, v, a, j = ps[0:3, :], ps[3:6, :], fr[0:3, :], fr[3:6, :]
    t2 = TICK * TICK * 0.5
    xp = x + v * TICK + a * t2 + j * (TICK * TICK * TICK / 6.0)
    vp = v + a * TICK + j * t2
    ap = a + j * TICK
    lane = lax.broadcasted_iota(jnp.int32, (8, BS), 1)
    levels = jnp.zeros((8, BS), F32)
    for k in range(NB):
        levels = jnp.where(lane == k, lev[k].astype(F32), levels)
    first[7 * NB : 7 * NB + 8, :] = levels
    for k in range(NB):
        at = slice(k * BS, k * BS + BS)
        for c in range(3):
            first[NB * c + k : NB * c + k + 1, :] = xp[c : c + 1, at]
            first[NB * (4 + c) + k : NB * (4 + c) + k + 1, :] = vp[c : c + 1, at]
            rates[0, NB * c + k : NB * c + k + 1, :] = ap[c : c + 1, at]
            rates[0, NB * (3 + c) + k : NB * (3 + c) + k + 1, :] = j[c : c + 1, at]
        first[NB * 3 + k : NB * 3 + k + 1, :] = mass[:, at]
        own[k] = jnp.zeros((16, BS), F32)
        own[k, 0:3, :] = x[:, at]
        own[k, 3:4, :] = mass[:, at]
        own[k, 4:7, :] = v[:, at]
        own[k, 8:14, :] = fr[:, at]
    for b in range(1, rates.shape[0]):
        rates[b] = rates[0]


def first_kernel(me, col, table, mine, lev, levall, partner, state, pay, order0, order1, known, turned, plan):
    me = me[0]
    col = pl.multiple_of(col[0] * 8, 8)
    known[ME, 0] = me
    for k in range(NB):
        known[OWN, k] = lev[k]
        known[MATE, k] = partner[k] >> SHIFT
    fill_slots(lambda k: lev[k], TOP[0], CAPS[0], plan)
    for k in range(NB):
        turned[k, :, 0:16] = mine[k].T
    for k in range(NB):
        state[k] = turned[k, pl.ds(col, 8), :]
    masses = []
    seen = jnp.int32(0)
    for k in range(NB):
        one = lev[k] == 1
        masses.append((7, jnp.where(one, seen, -1000), state[k][:, MS : MS + 1]))
        seen = seen + one.astype(jnp.int32)

    def close(s, e, part):
        k = plan[BLOCK, s]
        b = known[MATE, k] if part else me
        rows, mass = from_table(table, b, k)
        return rows, mass, b != me if part else jnp.bool_(True)

    shards = table.shape[0]
    orders = (order0, order1)

    def sweep(goal):
        def group(b, carry):
            acc, counts = carry
            ranks = [jnp.int32(0), jnp.int32(4)]
            for k in range(NB):
                rows, mass = from_table(table, b, k)
                acc = tuple(pair(goal[e], rows, mass, WIDE, acc[e]) for e in range(2))
                for order, count in zip(orders, counts):
                    order[count] = b * NB + k
                level = levall[b, k]
                counts = tuple(counts[e] + (level > e).astype(jnp.int32) for e in range(2))
                at = jnp.where(known[MATE, k] == b, k, 31)
                known[RANK, at] = jnp.where(level == 0, ranks[0], ranks[1])
                known[MATELEVEL, at] = level
                ranks = [ranks[e] + (level == e).astype(jnp.int32) for e in range(2)]
            return acc, counts

        start = ((zeros(), zeros()), (jnp.int32(0), jnp.int32(0)))
        acc, counts = lax.fori_loop(0, shards, group, start)
        for order, count in zip(orders, counts):
            for e in range(NB):
                order[count + e] = shards * NB
            order[(shards + 2) * NB] = count
        return acc

    tiles = slot_pairs(
        0, pairs_of(plan), state, plan, sweep,
        lambda p: None, close, corrector(0, state, plan, None),
        tuple(fill_tiles(masses, blank(2), 32)),
    )
    send(place_tiles(tiles), pay)


def ahead_sums(step, first, last, me, plan, order, predicted, state, sums):
    lane = lax.broadcasted_iota(jnp.int32, (8, 128), 1)

    def load(g, e):
        index = order[g * NB + e]
        return from_predicted(predicted, index >> SHIFT, index & (NB - 1))

    def close(s, e, part):
        rows, mass = from_predicted(predicted, plan[SHARD, 2 * s + part], plan[BLOCK, s])
        other = plan[SHARD, 2 * s + 1] != me if part else jnp.bool_(True)
        return rows, mass, other & (plan[HERE, 2 * s + part] == 0)

    def sink(s, total, inner, carry):
        tile = jnp.zeros((8, 128), F32)
        for at, group in ((0, total), (8, inner)):
            for c in range(6):
                tile = jnp.where(lane == at + c, group[c], tile)
        sums[s] = tile
        return carry

    groups = (order[order.shape[0] - NB] + NB - 1) // NB
    slot_pairs(first, last, state, plan, sweep_table(groups, load), lambda p: None, close, sink, 0)


def early_pairs(plan):
    return jnp.minimum(plan[COUNT, 2] // 2, 1)


def ahead_kernel(step, known, table, rates, order, state, *rest):
    if step == 1:
        sums, plan, predicted = rest
    elif step == 2:
        sums, plan, later, early, predicted, plan3 = rest
    else:
        early, sums, plan, predicted = rest
    me = known[ME, 0]
    lev = lambda k: known[OWN, k]
    fill_slots(lev, TOP[step], CAPS[step], plan)
    fill_near(plan, CAPS[step], known, SENT[step])
    fill_sources(table, rates, predicted, step * TICK)
    first = 0
    if step == 3:
        first = early_pairs(plan)
        sums[0:2] = early[...]
    ahead_sums(step, first, pairs_of(plan), me, plan, order, predicted, state, sums)
    if step == 2:
        fill_later(state, lev, later)
        fill_slots(lev, TOP[3], CAPS[3], plan3)
        fill_near(plan3, 2, known, SENT[3])
        fill_sources(table, rates, predicted, 3 * TICK)
        early[...] = jnp.zeros((2, 8, 128), F32)
        ahead_sums(3, 0, early_pairs(plan3), me, plan3, order, predicted, state, early)
    if step == 1:
        level = table[:, 7 * NB, :]
        lane = lax.broadcasted_iota(jnp.int32, level.shape, 1)
        one = jnp.where((level == 1.0) & (lane < NB), 1.0, 0.0).astype(F32)
        plan[COUNT, 1] = jnp.max(jnp.sum(one, axis=1, keepdims=True)).astype(jnp.int32)


def after_kernel(step, got, state_in, sums, plan, *rest):
    later = None
    used = SLOTS[step]
    if step > 1:
        masses, before, *rest = rest
        used = jnp.minimum(4 + before[COUNT, 1], used)
    if step == 2:
        later, *rest = rest
    if step == 3:
        state = state_in
    else:
        state, *rest = rest
    pay, *rest = rest
    if step == 1:
        masses, *rest = rest
    near, turned = rest
    if step < 3:
        state[...] = state_in[...]
    fill_received(got, turned)
    if step == 1:
        masses[0:4] = turned[24:28]
        masses[4:8] = turned[28:32]

    def close(s, e, part):
        rows, mass = tile_rows(lambda r: near[2 * e + part, r : r + 1, :])
        return rows, mass, plan[HERE, 2 * s + part] == 1

    tiles = slot_pairs(
        0, pairs_of(plan), state, plan,
        sweep_received(turned, masses, SLOTS[step], used),
        lambda p: gather_blocks(turned, masses, SLOTS[step], plan, near, p),
        close, corrector(step, state, plan, sums),
        tuple([later[t] for t in range(3)] if step == 2 else blank(9 if step == 3 else 3)),
    )
    send(place_tiles(tiles), pay)


def last_kernel(got, ps, fr, irr, plan, kin, comb, close):
    count = plan[COUNT, 0]
    kin[...] = ps[...]
    comb[...] = fr[...]
    close[...] = irr[...]
    senders = got.shape[0]
    lane = lax.broadcasted_iota(jnp.int32, (senders, 128), 1)
    row = lax.broadcasted_iota(jnp.int32, (senders, 128), 0)
    spread = [pltpu.roll(got[:, 0, pl.ds(t * 128, 128)], 0, 1, stride=8, stride_axis=0) for t in range(9)]
    place = lane - row * 8

    def slot(s, _):
        at = pl.ds(pl.multiple_of(plan[BLOCK, s] * BS, BS), BS)
        for f in range(18):
            t, e = divmod(f, 2)
            start = e * 64 + s * 8
            keep = (((place - start) & 127) >> 3) == 0
            value = jnp.sum(jnp.where(keep, spread[t], 0.0), axis=0, keepdims=True)
            out = (kin, comb, close)[f // 6]
            out[f % 6 : f % 6 + 1, at] = pltpu.roll(value, (128 - start) & 127, 1)
        return 0

    lax.fori_loop(0, count, slot, 0)


def body(phase_space, force_rates, irregular, stellar_masses, levels, active, partner):
    shards = lax.axis_size("blk")
    columns_ = lax.axis_size("grp")
    everyone = shards * columns_
    me = lax.axis_index("blk").astype(jnp.int32).reshape(1)
    col = lax.axis_index("grp").astype(jnp.int32).reshape(1)
    tiles = lambda count: pltpu.VMEM((count, 8, 128), F32)
    array = lambda *shape: jax.ShapeDtypeStruct(shape, F32)
    near = lambda *shape: pltpu.VMEM(shape, F32)
    here = lambda x: pltpu.with_memory_space_constraint(x, pltpu.VMEM)
    kept = lambda x: pltpu.with_memory_space_constraint(x, pltpu.SMEM)
    plan_shape = pltpu.SMEM((8, 32), jnp.int32)
    state_shape = near(NB + 1, 8, 128)

    def exchange(pay, axis):
        return lax.all_to_all(pay, axis, split_axis=0, concat_axis=0, tiled=True)

    packed, rates, mine = pl.pallas_call(
        pack_kernel,
        out_shape=(near(7 * NB + 8, BS), array(shards, 6 * NB, BS), near(NB, 16, BS)),
        in_specs=[VMEM, VMEM, VMEM, SMEM],
        out_specs=(VMEM, VMEM, VMEM),
        name="pack",
    )(phase_space, force_rates, stellar_masses[None, :], levels)
    table = lax.all_gather(packed, "blk", axis=0, tiled=False)
    levall = table[:, 7 * NB, :NB].astype(jnp.int32)
    table, rates = lax.optimization_barrier((table, rates))
    rates = exchange(rates, "blk")
    order_shape = pltpu.SMEM(((shards + 3) * NB,), jnp.int32)
    known_shape = pltpu.SMEM((8, 32), jnp.int32)
    state, pay, *orders, known = pl.pallas_call(
        first_kernel,
        out_shape=(state_shape, array(everyone, 1, 256), order_shape, order_shape, known_shape),
        in_specs=[SMEM, SMEM, VMEM, VMEM, SMEM, SMEM, SMEM],
        out_specs=(VMEM, VMEM, SMEM, SMEM, SMEM),
        scratch_shapes=[pltpu.VMEM((NB, 128, 128), F32), pltpu.SMEM((8, 32), jnp.int32)],
        name="first",
    )(me, col, here(table), here(mine), levels, levall, partner)
    masses = before = None
    for step in (1, 2, 3):
        cap = CAPS[step]
        lanes = (0, 256, 384, 384)[step]
        got = exchange(pay, ("blk", "grp"))
        ins = (kept(known), here(table), here(rates), kept(orders[SENT[step]]), here(state))
        specs = [SMEM, VMEM, VMEM, SMEM, VMEM]
        out_shape = (near(cap, 8, 128), plan_shape)
        out_specs = (VMEM, SMEM)
        scratch = [pltpu.VMEM((shards + 1, QUANTITIES, NB, BS), F32)]
        if step == 2:
            out_shape += (near(3, 8, 128), near(2, 8, 128))
            out_specs += (VMEM, VMEM)
            scratch += [pltpu.SMEM((8, 32), jnp.int32)]
        elif step == 3:
            ins += (here(early),)
            specs += [VMEM]
        outs = pl.pallas_call(
            functools.partial(ahead_kernel, step),
            out_shape=out_shape,
            in_specs=specs,
            out_specs=out_specs,
            scratch_shapes=scratch,
            name=f"ahead{step}",
        )(*ins)
        sums, plan = outs[:2]
        if step == 2:
            early = outs[3]
        ins = (here(got), here(state), here(sums), kept(plan))
        specs = [VMEM, VMEM, VMEM, SMEM]
        if step > 1:
            ins += (here(masses), kept(before))
            specs += [VMEM, SMEM]
        if step == 2:
            ins += (here(outs[2]),)
            specs += [VMEM]
        pay_shape = array(everyone if step < 3 else columns_, 1, (0, 384, 384, 1152)[step])
        out_shape = {
            1: (state_shape, pay_shape, near(8, 8, everyone)), 2: (state_shape, pay_shape), 3: (pay_shape,),
        }[step]
        outs = pl.pallas_call(
            functools.partial(after_kernel, step),
            out_shape=out_shape,
            in_specs=specs,
            out_specs=tuple(VMEM for _ in out_shape),
            scratch_shapes=[
                tiles(4),
                pltpu.VMEM((lanes // 8, 8, everyone), F32),
            ],
            name=f"after{step}",
        )(*ins)
        if step == 1:
            state, pay, masses = outs
            before = plan
        elif step == 2:
            state, pay = outs
        else:
            (pay,) = outs
    got = exchange(pay, "grp")
    shape = array(6, W)
    return tuple(
        pl.pallas_call(
            last_kernel,
            out_shape=(shape, shape, shape),
            in_specs=[VMEM, VMEM, VMEM, VMEM, SMEM],
            out_specs=(VMEM, VMEM, VMEM),
            name="last",
        )(here(got), phase_space, force_rates, irregular, kept(plan))
    )


def solution(mesh):
    in_specs = (
        P(None, "blk"), P(None, "blk"), P(None, "blk"), P("blk"), P("blk"), P(None, "blk"), P("blk"),
    )
    out_specs = (P(None, "blk"), P(None, "blk"), P(None, "blk"))
    return jax.shard_map(body, mesh=mesh, in_specs=in_specs, out_specs=out_specs, check_vma=False)
```

```python
import functools
import jax
import jax.numpy as jnp
from jax import lax
from jax.experimental import pallas as pl
from jax.experimental.pallas import tpu as pltpu
from jax.sharding import PartitionSpec as P

WIDE = 0.04
CLOSE = 0.0001
TICK = 0.125
NB = 16
SHIFT = 4
BS = 128
W = NB * BS
F32 = jnp.float32
CAPS = (4, 6, 4, 8)
TOP = (0, 1, 0, 2)
SENT = (-1, 0, 1, 1)
SLOTS = (0, 4, 8, 8)

VMEM = pl.BlockSpec(memory_space=pltpu.VMEM)
SMEM = pl.BlockSpec(memory_space=pltpu.SMEM)


def pair(target, source, mass, soften, acc):
    r = [source[c] - target[c] for c in range(3)]
    w = [source[c] - target[c] for c in range(3, 6)]
    d = (r[0] * r[0] + soften) + r[1] * r[1] + r[2] * r[2]
    s = lax.rsqrt(d)
    s2 = s * s
    weight = (mass * s) * s2
    q = (r[0] * w[0] + r[1] * w[1] + r[2] * w[2]) * (s2 * 3.0)
    acc = list(acc)
    for c in range(3):
        acc[c] = acc[c] + weight * r[c]
        acc[3 + c] = acc[3 + c] + weight * (w[c] - q * r[c])
    return tuple(acc)


def pair_split(target, source, mass, acc):
    r = [source[c] - target[c] for c in range(3)]
    w = [source[c] - target[c] for c in range(3, 6)]
    dd = r[0] * r[0] + r[1] * r[1] + r[2] * r[2]
    rw = (r[0] * w[0] + r[1] * w[1] + r[2] * w[2]) * 3.0
    acc = list(acc)
    for soften, sign in ((CLOSE, 1.0), (WIDE, -1.0)):
        s = lax.rsqrt(dd + soften)
        s2 = s * s
        weight = (mass * s) * (s2 * sign)
        q = rw * s2
        for c in range(3):
            acc[c] = acc[c] + weight * r[c]
            acc[3 + c] = acc[3 + c] + weight * (w[c] - q * r[c])
    return tuple(acc)


def zeros():
    return tuple(jnp.zeros((8, 128), F32) for _ in range(6))


BLOCK, PLACE, LEVEL, SHARD, ROW, HERE, COUNT = range(7)
OWN, MATE, RANK, MATELEVEL, ME = range(5)


def fill_slots(lev, top, cap, plan):
    for s in range(cap):
        plan[BLOCK, s] = 0
        plan[PLACE, s] = -1000
        plan[LEVEL, s] = 0
    count = jnp.int32(0)
    for group in ((2,), (0, 1)) if top == 2 else ((0, 1),):
        ones = [jnp.int32(0), jnp.int32(4)]
        for k in range(NB):
            level = lev(k)
            place = jnp.where(level == 0, ones[0], jnp.where(level == 1, ones[1], -1000))
            live = (level == 2) if group == (2,) else level <= min(top, 1)
            plan[BLOCK, count] = k
            plan[PLACE, count] = jnp.where(live, place, -1000)
            plan[LEVEL, count] = jnp.where(live, level, 0)
            count = count + live.astype(jnp.int32)
            ones[0] = ones[0] + (level == 0).astype(jnp.int32)
            ones[1] = ones[1] + (level == 1).astype(jnp.int32)
        if group == (2,):
            plan[COUNT, 2] = count
    plan[COUNT, 0] = count


def fill_near(plan, cap, known, sent):
    me = known[ME, 0]

    def slot(s, _):
        k = plan[BLOCK, s]
        q = known[MATE, k]
        ours = plan[LEVEL, s] <= sent
        theirs = (q != me) & (known[MATELEVEL, k] <= sent)
        for e, (b, row, here) in enumerate(((me, plan[PLACE, s], ours), (q, known[RANK, k], theirs))):
            plan[SHARD, 2 * s + e] = b
            plan[ROW, 2 * s + e] = jnp.clip(jnp.where(here, row, 0), 0, 3 if sent == 0 else 7)
            plan[HERE, 2 * s + e] = here.astype(jnp.int32)
        return 0

    lax.fori_loop(0, cap, slot, 0)


def span_of(level):
    return jnp.where(level == 0, TICK, jnp.where(level == 1, 2 * TICK, 4 * TICK)).astype(F32)


XS, MS, VS, AS, JS = (0, 1, 2), 3, (4, 5, 6), (8, 9, 10), (11, 12, 13)


def columns(tile):
    return tuple(
        [tile[:, c : c + 1] for c in group] for group in (XS, VS, AS, JS)
    )


def forecast(x, v, a, j, t):
    t2 = t * t * 0.5
    t3 = t * t * t * (1.0 / 6.0)
    xp = [x[c] + v[c] * t + a[c] * t2 + j[c] * t3 for c in range(3)]
    vp = [v[c] + a[c] * t + j[c] * t2 for c in range(3)]
    return xp + vp


QUANTITIES = 7


def fill_sources(table, rates, predicted, t):
    t2 = t * t * 0.5
    t3 = t * t * t / 6.0

    def shard(b, _):
        x, m, v = [[table[b, pl.ds(NB * f, NB), :] for f in group] for group in ((0, 1, 2), (3,), (4, 5, 6))]
        a, j = [[rates[b, pl.ds(NB * f, NB), :] for f in group] for group in ((0, 1, 2), (3, 4, 5))]
        for c in range(3):
            predicted[b, c] = x[c] + v[c] * t + a[c] * t2 + j[c] * t3
            predicted[b, 4 + c] = v[c] + a[c] * t + j[c] * t2
        predicted[b, 3] = m[0]
        return 0

    lax.fori_loop(0, table.shape[0], shard, 0)
    for f in range(QUANTITIES):
        predicted[table.shape[0], f] = jnp.zeros((NB, BS), F32)


def target_of(state, plan, s):
    x, v, a, j = columns(state[plan[BLOCK, s]])
    ahead = forecast(x, v, a, j, span_of(plan[LEVEL, s]))
    return [jnp.broadcast_to(value, (8, 128)) for value in ahead]


def broad(row):
    return jnp.broadcast_to(row, (8, 128))


def tile_rows(tile):
    return [broad(tile(r)) for r in (0, 1, 2, 4, 5, 6)], broad(tile(3))


def from_table(table, b, k):
    return tile_rows(lambda r: table[b, pl.ds(NB * r + k, 1), :])


def from_predicted(predicted, b, k):
    return tile_rows(lambda r: predicted[b, r, pl.ds(k, 1), :])


def slot_pairs(first, last, state, plan, sweep, prepare, close, sink, carry):
    def two(p, carry):
        goal = [target_of(state, plan, 2 * p + e) for e in range(2)]
        prepare(p)
        acc = sweep(goal)
        for e in range(2):
            s = 2 * p + e
            near = zeros()
            for part in range(2):
                rows, mass, wanted = close(s, e, part)
                near = pair_split(goal[e], rows, mass * jnp.where(wanted, 1.0, 0.0).astype(F32), near)
            total, inner = (
                [jnp.sum(value, axis=1, keepdims=True) for value in group] for group in (acc[e], near)
            )
            carry = sink(s, total, inner, carry)
        return carry

    return lax.fori_loop(first, last, two, carry)


def pairs_of(plan):
    return (plan[COUNT, 0] + 1) // 2


def sweep_table(groups, load):
    def sweep(goal):
        def group(b, acc):
            for k in range(NB):
                rows, mass = load(b, k)
                acc = tuple(pair(goal[e], rows, mass, WIDE, acc[e]) for e in range(2))
            return acc

        return lax.fori_loop(0, groups, group, (zeros(), zeros()))

    return sweep


def fill_received(got, turned):
    senders, _, lanes = got.shape
    for t in range(lanes // 128):
        for half in range(senders // 128):
            part = got[pl.ds(half * 128, 128), 0, pl.ds(t * 128, 128)]
            turned[pl.ds(t * 16, 16), :, pl.ds(half * 128, 128)] = part.T.reshape(16, 8, 128)


def sweep_received(turned, mass, slots_in, used):
    def sweep(goal):
        def slot(s, acc):
            for i in range(8):
                for half in range(turned.shape[2] // 128):
                    at = pl.ds(half * 128, 128)
                    rows = [broad(turned[f * slots_in + s, i : i + 1, at]) for f in range(6)]
                    m = broad(mass[s, i : i + 1, at])
                    acc = tuple(pair(goal[e], rows, m, WIDE, acc[e]) for e in range(2))
            return acc

        return lax.fori_loop(0, used, slot, (zeros(), zeros()))

    return sweep


def gather_blocks(turned, mass, slots_in, plan, near, p):
    lane = lax.broadcasted_iota(jnp.int32, (8, 128), 1)
    row = lax.broadcasted_iota(jnp.int32, (8, 128), 0)
    keep = lane // 16 == row
    for item in range(4):
        b = plan[SHARD, 4 * p + item]
        place = plan[ROW, 4 * p + item]
        half = pl.ds(pl.multiple_of((b // 8) * 128, 128), 128)
        shift = lax.rem(128 - lax.rem(b, 8) * 16, 128)
        for r, f in ((0, 0), (1, 1), (2, 2), (4, 3), (5, 4), (6, 5), (3, None)):
            tile = mass[place, :, half] if f is None else turned[f * slots_in + place, :, half]
            tile = pltpu.roll(pltpu.roll(tile, shift, 1), 0, 1, stride=16, stride_axis=0)
            near[item, r : r + 1, :] = jnp.sum(jnp.where(keep, tile, 0.0), axis=0, keepdims=True)


def fill_tiles(parts, tiles, width):
    per = 128 // width
    tiles = list(tiles)
    lane = lax.broadcasted_iota(jnp.int32, (8, 128), 1)
    for f, slot, column in parts:
        t = f // per
        tiles[t] = jnp.where(lane == (f % per) * width + slot * 8, column, tiles[t])
    return tiles


def blank(count):
    return [jnp.zeros((8, 128), F32) for _ in range(count)]


def place_tiles(tiles):
    tiles = [pltpu.roll(tile, 0, 1, stride=1, stride_axis=0) for tile in tiles]
    return [jnp.sum(tile, axis=0, keepdims=True) for tile in tiles]


def send(tiles, pay):
    for t, tile in enumerate(tiles):
        full = jnp.broadcast_to(tile[None], (pay.shape[0], 1, 128))
        pay[:, :, pl.ds(t * 128, 128)] = full


def corrector(step, state, plan, sums):
    lane = lax.broadcasted_iota(jnp.int32, (8, 128), 1)

    def sink(s, total, inner, carry):
        k = plan[BLOCK, s]
        t = span_of(plan[LEVEL, s])
        tile = state[k]
        x, v, a, j = columns(tile)
        if sums is not None:
            before = sums[s]
            total = [total[c] + before[:, c : c + 1] for c in range(6)]
            inner = [inner[c] + before[:, 8 + c : 9 + c] for c in range(6)]
        total = [total[c] + inner[c] for c in range(6)]
        half = t * 0.5
        twelfth = t * t * (1.0 / 12.0)
        v1 = [v[c] + (a[c] + total[c]) * half + (j[c] - total[3 + c]) * twelfth for c in range(3)]
        x1 = [x[c] + (v[c] + v1[c]) * half + (a[c] - total[c]) * twelfth for c in range(3)]
        if step == 3:
            parts = [(f, s, column) for f, column in enumerate(x1 + v1 + total + inner)]
            return tuple(fill_tiles(parts, carry, 64))
        fresh = tile
        for at, column in zip(XS + VS + AS + JS, x1 + v1 + total):
            fresh = jnp.where(lane == at, column, fresh)
        state[jnp.where(s < plan[COUNT, 0], k, NB)] = fresh
        ahead = forecast(x1, v1, total[:3], total[3:], TICK)
        if step == 0:
            ahead = ahead + [tile[:, MS : MS + 1]]
        parts = [(f, plan[PLACE, s], column) for f, column in enumerate(ahead)]
        return tuple(fill_tiles(parts, carry, 32 if step == 0 else 64))

    return sink


def fill_later(state, lev, later):
    parts = []
    seen = jnp.int32(4)
    for k in range(NB):
        one = lev(k) == 1
        mark = jnp.where(one, seen, -1000)
        x, v, a, j = columns(state[k])
        for f, column in enumerate(forecast(x, v, a, j, 2 * TICK)):
            parts.append((f, mark, column))
        seen = seen + one.astype(jnp.int32)
    for t, tile in enumerate(fill_tiles(parts, blank(3), 64)):
        later[t] = tile


def pack_kernel(ps, fr, mass, lev, first, rates, own):
    x, v, a, j = ps[0:3, :], ps[3:6, :], fr[0:3, :], fr[3:6, :]
    t2 = TICK * TICK * 0.5
    xp = x + v * TICK + a * t2 + j * (TICK * TICK * TICK / 6.0)
    vp = v + a * TICK + j * t2
    ap = a + j * TICK
    lane = lax.broadcasted_iota(jnp.int32, (8, BS), 1)
    levels = jnp.zeros((8, BS), F32)
    for k in range(NB):
        levels = jnp.where(lane == k, lev[k].astype(F32), levels)
    first[7 * NB : 7 * NB + 8, :] = levels
    for k in range(NB):
        at = slice(k * BS, k * BS + BS)
        for c in range(3):
            first[NB * c + k : NB * c + k + 1, :] = xp[c : c + 1, at]
            first[NB * (4 + c) + k : NB * (4 + c) + k + 1, :] = vp[c : c + 1, at]
            rates[0, NB * c + k : NB * c + k + 1, :] = ap[c : c + 1, at]
            rates[0, NB * (3 + c) + k : NB * (3 + c) + k + 1, :] = j[c : c + 1, at]
        first[NB * 3 + k : NB * 3 + k + 1, :] = mass[:, at]
        own[k] = jnp.zeros((16, BS), F32)
        own[k, 0:3, :] = x[:, at]
        own[k, 3:4, :] = mass[:, at]
        own[k, 4:7, :] = v[:, at]
        own[k, 8:14, :] = fr[:, at]
    for b in range(1, rates.shape[0]):
        rates[b] = rates[0]


def first_kernel(me, col, table, mine, lev, levall, partner, state, pay, order0, order1, known, turned, plan):
    me = me[0]
    col = pl.multiple_of(col[0] * 8, 8)
    known[ME, 0] = me
    for k in range(NB):
        known[OWN, k] = lev[k]
        known[MATE, k] = partner[k] >> SHIFT
    fill_slots(lambda k: lev[k], TOP[0], CAPS[0], plan)
    for k in range(NB):
        turned[k, :, 0:16] = mine[k].T
    for k in range(NB):
        state[k] = turned[k, pl.ds(col, 8), :]
    masses = []
    seen = jnp.int32(0)
    for k in range(NB):
        one = lev[k] == 1
        masses.append((7, jnp.where(one, seen, -1000), state[k][:, MS : MS + 1]))
        seen = seen + one.astype(jnp.int32)

    def close(s, e, part):
        k = plan[BLOCK, s]
        b = known[MATE, k] if part else me
        rows, mass = from_table(table, b, k)
        return rows, mass, b != me if part else jnp.bool_(True)

    shards = table.shape[0]
    orders = (order0, order1)

    def sweep(goal):
        def group(b, carry):
            acc, counts = carry
            ranks = [jnp.int32(0), jnp.int32(4)]
            for k in range(NB):
                rows, mass = from_table(table, b, k)
                acc = tuple(pair(goal[e], rows, mass, WIDE, acc[e]) for e in range(2))
                for order, count in zip(orders, counts):
                    order[count] = b * NB + k
                level = levall[b, k]
                counts = tuple(counts[e] + (level > e).astype(jnp.int32) for e in range(2))
                at = jnp.where(known[MATE, k] == b, k, 31)
                known[RANK, at] = jnp.where(level == 0, ranks[0], ranks[1])
                known[MATELEVEL, at] = level
                ranks = [ranks[e] + (level == e).astype(jnp.int32) for e in range(2)]
            return acc, counts

        start = ((zeros(), zeros()), (jnp.int32(0), jnp.int32(0)))
        acc, counts = lax.fori_loop(0, shards, group, start)
        for order, count in zip(orders, counts):
            for e in range(NB):
                order[count + e] = shards * NB
            order[(shards + 2) * NB] = count
        return acc

    tiles = slot_pairs(
        0, pairs_of(plan), state, plan, sweep,
        lambda p: None, close, corrector(0, state, plan, None),
        tuple(fill_tiles(masses, blank(2), 32)),
    )
    send(place_tiles(tiles), pay)


def ahead_sums(step, first, last, me, plan, order, predicted, state, sums):
    lane = lax.broadcasted_iota(jnp.int32, (8, 128), 1)

    def load(g, e):
        index = order[g * NB + e]
        return from_predicted(predicted, index >> SHIFT, index & (NB - 1))

    def close(s, e, part):
        rows, mass = from_predicted(predicted, plan[SHARD, 2 * s + part], plan[BLOCK, s])
        other = plan[SHARD, 2 * s + 1] != me if part else jnp.bool_(True)
        return rows, mass, other & (plan[HERE, 2 * s + part] == 0)

    def sink(s, total, inner, carry):
        tile = jnp.zeros((8, 128), F32)
        for at, group in ((0, total), (8, inner)):
            for c in range(6):
                tile = jnp.where(lane == at + c, group[c], tile)
        sums[s] = tile
        return carry

    groups = (order[order.shape[0] - NB] + NB - 1) // NB
    slot_pairs(first, last, state, plan, sweep_table(groups, load), lambda p: None, close, sink, 0)


def early_pairs(plan):
    return jnp.minimum(plan[COUNT, 2] // 2, 1)


def ahead_kernel(step, known, table, rates, order, state, *rest):
    if step == 1:
        sums, plan, predicted = rest
    elif step == 2:
        sums, plan, later, early, predicted, plan3 = rest
    else:
        early, sums, plan, predicted = rest
    me = known[ME, 0]
    lev = lambda k: known[OWN, k]
    fill_slots(lev, TOP[step], CAPS[step], plan)
    fill_near(plan, CAPS[step], known, SENT[step])
    fill_sources(table, rates, predicted, step * TICK)
    first = 0
    if step == 3:
        first = early_pairs(plan)
        sums[0:2] = early[...]
    ahead_sums(step, first, pairs_of(plan), me, plan, order, predicted, state, sums)
    if step == 2:
        fill_later(state, lev, later)
        fill_slots(lev, TOP[3], CAPS[3], plan3)
        fill_near(plan3, 2, known, SENT[3])
        fill_sources(table, rates, predicted, 3 * TICK)
        early[...] = jnp.zeros((2, 8, 128), F32)
        ahead_sums(3, 0, early_pairs(plan3), me, plan3, order, predicted, state, early)
    if step == 1:
        level = table[:, 7 * NB, :]
        lane = lax.broadcasted_iota(jnp.int32, level.shape, 1)
        one = jnp.where((level == 1.0) & (lane < NB), 1.0, 0.0).astype(F32)
        plan[COUNT, 1] = jnp.max(jnp.sum(one, axis=1, keepdims=True)).astype(jnp.int32)


def after_kernel(step, got, state_in, sums, plan, *rest):
    later = None
    used = SLOTS[step]
    if step > 1:
        masses, before, *rest = rest
        used = jnp.minimum(4 + before[COUNT, 1], used)
    if step == 2:
        later, *rest = rest
    if step == 3:
        state = state_in
    else:
        state, *rest = rest
    pay, *rest = rest
    if step == 1:
        masses, *rest = rest
    near, turned = rest
    if step < 3:
        state[...] = state_in[...]
    fill_received(got, turned)
    if step == 1:
        masses[0:4] = turned[24:28]
        masses[4:8] = turned[28:32]

    def close(s, e, part):
        rows, mass = tile_rows(lambda r: near[2 * e + part, r : r + 1, :])
        return rows, mass, plan[HERE, 2 * s + part] == 1

    tiles = slot_pairs(
        0, pairs_of(plan), state, plan,
        sweep_received(turned, masses, SLOTS[step], used),
        lambda p: gather_blocks(turned, masses, SLOTS[step], plan, near, p),
        close, corrector(step, state, plan, sums),
        tuple([later[t] for t in range(3)] if step == 2 else blank(9 if step == 3 else 3)),
    )
    send(place_tiles(tiles), pay)


def last_kernel(got, ps, fr, irr, plan, kin, comb, close):
    count = plan[COUNT, 0]
    kin[...] = ps[...]
    comb[...] = fr[...]
    close[...] = irr[...]
    senders = got.shape[0]
    lane = lax.broadcasted_iota(jnp.int32, (senders, 128), 1)
    row = lax.broadcasted_iota(jnp.int32, (senders, 128), 0)
    spread = [pltpu.roll(got[:, 0, pl.ds(t * 128, 128)], 0, 1, stride=8, stride_axis=0) for t in range(9)]
    place = lane - row * 8

    def slot(s, _):
        at = pl.ds(pl.multiple_of(plan[BLOCK, s] * BS, BS), BS)
        for f in range(18):
            t, e = divmod(f, 2)
            start = e * 64 + s * 8
            keep = (((place - start) & 127) >> 3) == 0
            value = jnp.sum(jnp.where(keep, spread[t], 0.0), axis=0, keepdims=True)
            out = (kin, comb, close)[f // 6]
            out[f % 6 : f % 6 + 1, at] = pltpu.roll(value, (128 - start) & 127, 1)
        return 0

    lax.fori_loop(0, count, slot, 0)


def body(phase_space, force_rates, irregular, stellar_masses, levels, active, partner):
    shards = lax.axis_size("blk")
    columns_ = lax.axis_size("grp")
    everyone = shards * columns_
    me = lax.axis_index("blk").astype(jnp.int32).reshape(1)
    col = lax.axis_index("grp").astype(jnp.int32).reshape(1)
    tiles = lambda count: pltpu.VMEM((count, 8, 128), F32)
    array = lambda *shape: jax.ShapeDtypeStruct(shape, F32)
    near = lambda *shape: pltpu.VMEM(shape, F32)
    here = lambda x: pltpu.with_memory_space_constraint(x, pltpu.VMEM)
    kept = lambda x: pltpu.with_memory_space_constraint(x, pltpu.SMEM)
    plan_shape = pltpu.SMEM((8, 32), jnp.int32)
    state_shape = near(NB + 1, 8, 128)

    def exchange(pay, axis):
        return lax.all_to_all(pay, axis, split_axis=0, concat_axis=0, tiled=True)

    packed, rates, mine = pl.pallas_call(
        pack_kernel,
        out_shape=(near(7 * NB + 8, BS), array(shards, 6 * NB, BS), near(NB, 16, BS)),
        in_specs=[VMEM, VMEM, VMEM, SMEM],
        out_specs=(VMEM, VMEM, VMEM),
        name="pack",
    )(phase_space, force_rates, stellar_masses[None, :], levels)
    table = lax.all_gather(packed, "blk", axis=0, tiled=False)
    levall = table[:, 7 * NB, :NB].astype(jnp.int32)
    table, rates = lax.optimization_barrier((table, rates))
    rates = exchange(rates, "blk")
    order_shape = pltpu.SMEM(((shards + 3) * NB,), jnp.int32)
    known_shape = pltpu.SMEM((8, 32), jnp.int32)
    state, pay, *orders, known = pl.pallas_call(
        first_kernel,
        out_shape=(state_shape, array(everyone, 1, 256), order_shape, order_shape, known_shape),
        in_specs=[SMEM, SMEM, VMEM, VMEM, SMEM, SMEM, SMEM],
        out_specs=(VMEM, VMEM, SMEM, SMEM, SMEM),
        scratch_shapes=[pltpu.VMEM((NB, 128, 128), F32), pltpu.SMEM((8, 32), jnp.int32)],
        name="first",
    )(me, col, here(table), here(mine), levels, levall, partner)
    masses = before = None
    for step in (1, 2, 3):
        cap = CAPS[step]
        lanes = (0, 256, 384, 384)[step]
        got = exchange(pay, ("blk", "grp"))
        ins = (kept(known), here(table), here(rates), kept(orders[SENT[step]]), here(state))
        specs = [SMEM, VMEM, VMEM, SMEM, VMEM]
        out_shape = (near(cap, 8, 128), plan_shape)
        out_specs = (VMEM, SMEM)
        scratch = [pltpu.VMEM((shards + 1, QUANTITIES, NB, BS), F32)]
        if step == 2:
            out_shape += (near(3, 8, 128), near(2, 8, 128))
            out_specs += (VMEM, VMEM)
            scratch += [pltpu.SMEM((8, 32), jnp.int32)]
        elif step == 3:
            ins += (here(early),)
            specs += [VMEM]
        outs = pl.pallas_call(
            functools.partial(ahead_kernel, step),
            out_shape=out_shape,
            in_specs=specs,
            out_specs=out_specs,
            scratch_shapes=scratch,
            name=f"ahead{step}",
        )(*ins)
        sums, plan = outs[:2]
        if step == 2:
            early = outs[3]
        ins = (here(got), here(state), here(sums), kept(plan))
        specs = [VMEM, VMEM, VMEM, SMEM]
        if step > 1:
            ins += (here(masses), kept(before))
            specs += [VMEM, SMEM]
        if step == 2:
            ins += (here(outs[2]),)
            specs += [VMEM]
        pay_shape = array(everyone, 1, 384) if step < 3 else near(columns_, 1, 1152)
        out_shape = {
            1: (state_shape, pay_shape, near(8, 8, everyone)), 2: (state_shape, pay_shape), 3: (pay_shape,),
        }[step]
        outs = pl.pallas_call(
            functools.partial(after_kernel, step),
            out_shape=out_shape,
            in_specs=specs,
            out_specs=tuple(VMEM for _ in out_shape),
            scratch_shapes=[
                tiles(4),
                pltpu.VMEM((lanes // 8, 8, everyone), F32),
            ],
            name=f"after{step}",
        )(*ins)
        if step == 1:
            state, pay, masses = outs
            before = plan
        elif step == 2:
            state, pay = outs
        else:
            (pay,) = outs
    got = exchange(pay, "grp")
    shape = array(6, W)
    return tuple(
        pl.pallas_call(
            last_kernel,
            out_shape=(shape, shape, shape),
            in_specs=[VMEM, VMEM, VMEM, VMEM, SMEM],
            out_specs=(VMEM, VMEM, VMEM),
            name="last",
        )(here(got), here(phase_space), here(force_rates), here(irregular), kept(plan))
    )


def solution(mesh):
    in_specs = (
        P(None, "blk"), P(None, "blk"), P(None, "blk"), P("blk"), P("blk"), P(None, "blk"), P("blk"),
    )
    out_specs = (P(None, "blk"), P(None, "blk"), P(None, "blk"))
    return jax.shard_map(body, mesh=mesh, in_specs=in_specs, out_specs=out_specs, check_vma=False)
```

```python
import functools
import jax
import jax.numpy as jnp
from jax import lax
from jax.experimental import pallas as pl
from jax.experimental.pallas import tpu as pltpu
from jax.sharding import PartitionSpec as P

WIDE = 0.04
CLOSE = 0.0001
TICK = 0.125
NB = 16
SHIFT = 4
BS = 128
W = NB * BS
F32 = jnp.float32
CAPS = (4, 6, 4, 8)
TOP = (0, 1, 0, 2)
SENT = (-1, 0, 1, 1)
SLOTS = (0, 4, 8, 8)

VMEM = pl.BlockSpec(memory_space=pltpu.VMEM)
SMEM = pl.BlockSpec(memory_space=pltpu.SMEM)


def pair(target, source, mass, soften, acc):
    r = [source[c] - target[c] for c in range(3)]
    w = [source[c] - target[c] for c in range(3, 6)]
    d = (r[0] * r[0] + soften) + r[1] * r[1] + r[2] * r[2]
    s = lax.rsqrt(d)
    s2 = s * s
    weight = (mass * s) * s2
    q = (r[0] * w[0] + r[1] * w[1] + r[2] * w[2]) * (s2 * 3.0)
    acc = list(acc)
    for c in range(3):
        acc[c] = acc[c] + weight * r[c]
        acc[3 + c] = acc[3 + c] + weight * (w[c] - q * r[c])
    return tuple(acc)


def pair_split(target, source, mass, acc):
    r = [source[c] - target[c] for c in range(3)]
    w = [source[c] - target[c] for c in range(3, 6)]
    dd = r[0] * r[0] + r[1] * r[1] + r[2] * r[2]
    rw = (r[0] * w[0] + r[1] * w[1] + r[2] * w[2]) * 3.0
    acc = list(acc)
    for soften, sign in ((CLOSE, 1.0), (WIDE, -1.0)):
        s = lax.rsqrt(dd + soften)
        s2 = s * s
        weight = (mass * s) * (s2 * sign)
        q = rw * s2
        for c in range(3):
            acc[c] = acc[c] + weight * r[c]
            acc[3 + c] = acc[3 + c] + weight * (w[c] - q * r[c])
    return tuple(acc)


def zeros():
    return tuple(jnp.zeros((8, 128), F32) for _ in range(6))


BLOCK, PLACE, LEVEL, SHARD, ROW, HERE, COUNT = range(7)
OWN, MATE, RANK, MATELEVEL, ME = range(5)


def fill_slots(lev, top, cap, plan):
    for s in range(cap):
        plan[BLOCK, s] = 0
        plan[PLACE, s] = -1000
        plan[LEVEL, s] = 0
    count = jnp.int32(0)
    for group in ((2,), (0, 1)) if top == 2 else ((0, 1),):
        ones = [jnp.int32(0), jnp.int32(4)]
        for k in range(NB):
            level = lev(k)
            place = jnp.where(level == 0, ones[0], jnp.where(level == 1, ones[1], -1000))
            live = (level == 2) if group == (2,) else level <= min(top, 1)
            plan[BLOCK, count] = k
            plan[PLACE, count] = jnp.where(live, place, -1000)
            plan[LEVEL, count] = jnp.where(live, level, 0)
            count = count + live.astype(jnp.int32)
            ones[0] = ones[0] + (level == 0).astype(jnp.int32)
            ones[1] = ones[1] + (level == 1).astype(jnp.int32)
        if group == (2,):
            plan[COUNT, 2] = count
    plan[COUNT, 0] = count


def fill_near(plan, cap, known, sent):
    me = known[ME, 0]

    def slot(s, _):
        k = plan[BLOCK, s]
        q = known[MATE, k]
        ours = plan[LEVEL, s] <= sent
        theirs = (q != me) & (known[MATELEVEL, k] <= sent)
        for e, (b, row, here) in enumerate(((me, plan[PLACE, s], ours), (q, known[RANK, k], theirs))):
            plan[SHARD, 2 * s + e] = b
            plan[ROW, 2 * s + e] = jnp.clip(jnp.where(here, row, 0), 0, 3 if sent == 0 else 7)
            plan[HERE, 2 * s + e] = here.astype(jnp.int32)
        return 0

    lax.fori_loop(0, cap, slot, 0)


def span_of(level):
    return jnp.where(level == 0, TICK, jnp.where(level == 1, 2 * TICK, 4 * TICK)).astype(F32)


XS, MS, VS, AS, JS = (0, 1, 2), 3, (4, 5, 6), (8, 9, 10), (11, 12, 13)


def columns(tile):
    return tuple(
        [tile[:, c : c + 1] for c in group] for group in (XS, VS, AS, JS)
    )


def forecast(x, v, a, j, t):
    t2 = t * t * 0.5
    t3 = t * t * t * (1.0 / 6.0)
    xp = [x[c] + v[c] * t + a[c] * t2 + j[c] * t3 for c in range(3)]
    vp = [v[c] + a[c] * t + j[c] * t2 for c in range(3)]
    return xp + vp


QUANTITIES = 7


def fill_sources(table, rates, predicted, t):
    t2 = t * t * 0.5
    t3 = t * t * t / 6.0

    def shard(b, _):
        x, m, v = [[table[b, pl.ds(NB * f, NB), :] for f in group] for group in ((0, 1, 2), (3,), (4, 5, 6))]
        a, j = [[rates[b, pl.ds(NB * f, NB), :] for f in group] for group in ((0, 1, 2), (3, 4, 5))]
        for c in range(3):
            predicted[b, c] = x[c] + v[c] * t + a[c] * t2 + j[c] * t3
            predicted[b, 4 + c] = v[c] + a[c] * t + j[c] * t2
        predicted[b, 3] = m[0]
        return 0

    lax.fori_loop(0, table.shape[0], shard, 0)
    for f in range(QUANTITIES):
        predicted[table.shape[0], f] = jnp.zeros((NB, BS), F32)


def target_of(state, plan, s):
    x, v, a, j = columns(state[plan[BLOCK, s]])
    ahead = forecast(x, v, a, j, span_of(plan[LEVEL, s]))
    return [jnp.broadcast_to(value, (8, 128)) for value in ahead]


def broad(row):
    return jnp.broadcast_to(row, (8, 128))


def tile_rows(tile):
    return [broad(tile(r)) for r in (0, 1, 2, 4, 5, 6)], broad(tile(3))


def from_table(table, b, k):
    return tile_rows(lambda r: table[b, pl.ds(NB * r + k, 1), :])


def from_predicted(predicted, b, k):
    return tile_rows(lambda r: predicted[b, r, pl.ds(k, 1), :])


def slot_pairs(first, last, state, plan, sweep, prepare, close, sink, carry):
    def two(p, carry):
        goal = [target_of(state, plan, 2 * p + e) for e in range(2)]
        prepare(p)
        acc = sweep(goal)
        for e in range(2):
            s = 2 * p + e
            near = zeros()
            for part in range(2):
                rows, mass, wanted = close(s, e, part)
                near = pair_split(goal[e], rows, mass * jnp.where(wanted, 1.0, 0.0).astype(F32), near)
            total, inner = (
                [jnp.sum(value, axis=1, keepdims=True) for value in group] for group in (acc[e], near)
            )
            carry = sink(s, total, inner, carry)
        return carry

    return lax.fori_loop(first, last, two, carry)


def pairs_of(plan):
    return (plan[COUNT, 0] + 1) // 2


def sweep_table(groups, load):
    def sweep(goal):
        def group(b, acc):
            for k in range(NB):
                rows, mass = load(b, k)
                acc = tuple(pair(goal[e], rows, mass, WIDE, acc[e]) for e in range(2))
            return acc

        return lax.fori_loop(0, groups, group, (zeros(), zeros()))

    return sweep


def fill_received(got, turned):
    senders, _, lanes = got.shape
    for t in range(lanes // 128):
        for half in range(senders // 128):
            part = got[pl.ds(half * 128, 128), 0, pl.ds(t * 128, 128)]
            turned[pl.ds(t * 16, 16), :, pl.ds(half * 128, 128)] = part.T.reshape(16, 8, 128)


def sweep_received(turned, mass, slots_in, used):
    def sweep(goal):
        def slot(s, acc):
            for i in range(8):
                for half in range(turned.shape[2] // 128):
                    at = pl.ds(half * 128, 128)
                    rows = [broad(turned[f * slots_in + s, i : i + 1, at]) for f in range(6)]
                    m = broad(mass[s, i : i + 1, at])
                    acc = tuple(pair(goal[e], rows, m, WIDE, acc[e]) for e in range(2))
            return acc

        return lax.fori_loop(0, used, slot, (zeros(), zeros()))

    return sweep


def gather_blocks(turned, mass, slots_in, plan, near, p):
    lane = lax.broadcasted_iota(jnp.int32, (8, 128), 1)
    row = lax.broadcasted_iota(jnp.int32, (8, 128), 0)
    keep = lane // 16 == row
    for item in range(4):
        b = plan[SHARD, 4 * p + item]
        place = plan[ROW, 4 * p + item]
        half = pl.ds(pl.multiple_of((b // 8) * 128, 128), 128)
        shift = lax.rem(128 - lax.rem(b, 8) * 16, 128)
        for r, f in ((0, 0), (1, 1), (2, 2), (4, 3), (5, 4), (6, 5), (3, None)):
            tile = mass[place, :, half] if f is None else turned[f * slots_in + place, :, half]
            tile = pltpu.roll(pltpu.roll(tile, shift, 1), 0, 1, stride=16, stride_axis=0)
            near[item, r : r + 1, :] = jnp.sum(jnp.where(keep, tile, 0.0), axis=0, keepdims=True)


def fill_tiles(parts, tiles, width):
    per = 128 // width
    tiles = list(tiles)
    lane = lax.broadcasted_iota(jnp.int32, (8, 128), 1)
    for f, slot, column in parts:
        t = f // per
        tiles[t] = jnp.where(lane == (f % per) * width + slot * 8, column, tiles[t])
    return tiles


def blank(count):
    return [jnp.zeros((8, 128), F32) for _ in range(count)]


def place_tiles(tiles):
    tiles = [pltpu.roll(tile, 0, 1, stride=1, stride_axis=0) for tile in tiles]
    return [jnp.sum(tile, axis=0, keepdims=True) for tile in tiles]


def send(tiles, pay):
    if len(pay.shape) == 3 and pay.shape[1] == 1:
        for t, tile in enumerate(tiles):
            pay[:, :, pl.ds(t * 128, 128)] = jnp.broadcast_to(tile[None], (pay.shape[0], 1, 128))
        return
    count = len(tiles)
    row = lax.broadcasted_iota(jnp.int32, (8, 128), 0)
    wide = [jnp.broadcast_to(tile, (8, 128)) for tile in tiles]
    for e in range(count):
        part = lax.rem(row + 8 * e, count)
        value = wide[0]
        for t in range(1, count):
            value = jnp.where(part == t, wide[t], value)
        for m in range(e, pay.shape[0], count):
            pay[m] = value


def corrector(step, state, plan, sums):
    lane = lax.broadcasted_iota(jnp.int32, (8, 128), 1)

    def sink(s, total, inner, carry):
        k = plan[BLOCK, s]
        t = span_of(plan[LEVEL, s])
        tile = state[k]
        x, v, a, j = columns(tile)
        if sums is not None:
            before = sums[s]
            total = [total[c] + before[:, c : c + 1] for c in range(6)]
            inner = [inner[c] + before[:, 8 + c : 9 + c] for c in range(6)]
        total = [total[c] + inner[c] for c in range(6)]
        half = t * 0.5
        twelfth = t * t * (1.0 / 12.0)
        v1 = [v[c] + (a[c] + total[c]) * half + (j[c] - total[3 + c]) * twelfth for c in range(3)]
        x1 = [x[c] + (v[c] + v1[c]) * half + (a[c] - total[c]) * twelfth for c in range(3)]
        if step == 3:
            parts = [(f, s, column) for f, column in enumerate(x1 + v1 + total + inner)]
            return tuple(fill_tiles(parts, carry, 64))
        fresh = tile
        for at, column in zip(XS + VS + AS + JS, x1 + v1 + total):
            fresh = jnp.where(lane == at, column, fresh)
        state[jnp.where(s < plan[COUNT, 0], k, NB)] = fresh
        ahead = forecast(x1, v1, total[:3], total[3:], TICK)
        if step == 0:
            ahead = ahead + [tile[:, MS : MS + 1]]
        parts = [(f, plan[PLACE, s], column) for f, column in enumerate(ahead)]
        return tuple(fill_tiles(parts, carry, 32 if step == 0 else 64))

    return sink


def fill_later(state, lev, later):
    parts = []
    seen = jnp.int32(4)
    for k in range(NB):
        one = lev(k) == 1
        mark = jnp.where(one, seen, -1000)
        x, v, a, j = columns(state[k])
        for f, column in enumerate(forecast(x, v, a, j, 2 * TICK)):
            parts.append((f, mark, column))
        seen = seen + one.astype(jnp.int32)
    for t, tile in enumerate(fill_tiles(parts, blank(3), 64)):
        later[t] = tile


def pack_kernel(ps, fr, mass, lev, first, rates, own):
    x, v, a, j = ps[0:3, :], ps[3:6, :], fr[0:3, :], fr[3:6, :]
    t2 = TICK * TICK * 0.5
    xp = x + v * TICK + a * t2 + j * (TICK * TICK * TICK / 6.0)
    vp = v + a * TICK + j * t2
    ap = a + j * TICK
    lane = lax.broadcasted_iota(jnp.int32, (8, BS), 1)
    levels = jnp.zeros((8, BS), F32)
    for k in range(NB):
        levels = jnp.where(lane == k, lev[k].astype(F32), levels)
    first[7 * NB : 7 * NB + 8, :] = levels
    for k in range(NB):
        at = slice(k * BS, k * BS + BS)
        for c in range(3):
            first[NB * c + k : NB * c + k + 1, :] = xp[c : c + 1, at]
            first[NB * (4 + c) + k : NB * (4 + c) + k + 1, :] = vp[c : c + 1, at]
            rates[0, NB * c + k : NB * c + k + 1, :] = ap[c : c + 1, at]
            rates[0, NB * (3 + c) + k : NB * (3 + c) + k + 1, :] = j[c : c + 1, at]
        first[NB * 3 + k : NB * 3 + k + 1, :] = mass[:, at]
        own[k] = jnp.zeros((16, BS), F32)
        own[k, 0:3, :] = x[:, at]
        own[k, 3:4, :] = mass[:, at]
        own[k, 4:7, :] = v[:, at]
        own[k, 8:14, :] = fr[:, at]
    for b in range(1, rates.shape[0]):
        rates[b] = rates[0]


def first_kernel(me, col, table, mine, lev, levall, partner, state, pay, order0, order1, known, turned, plan):
    me = me[0]
    col = pl.multiple_of(col[0] * 8, 8)
    known[ME, 0] = me
    for k in range(NB):
        known[OWN, k] = lev[k]
        known[MATE, k] = partner[k] >> SHIFT
    fill_slots(lambda k: lev[k], TOP[0], CAPS[0], plan)
    for k in range(NB):
        turned[k, :, 0:16] = mine[k].T
    for k in range(NB):
        state[k] = turned[k, pl.ds(col, 8), :]
    masses = []
    seen = jnp.int32(0)
    for k in range(NB):
        one = lev[k] == 1
        masses.append((7, jnp.where(one, seen, -1000), state[k][:, MS : MS + 1]))
        seen = seen + one.astype(jnp.int32)

    def close(s, e, part):
        k = plan[BLOCK, s]
        b = known[MATE, k] if part else me
        rows, mass = from_table(table, b, k)
        return rows, mass, b != me if part else jnp.bool_(True)

    shards = table.shape[0]
    orders = (order0, order1)

    def sweep(goal):
        def group(b, carry):
            acc, counts = carry
            ranks = [jnp.int32(0), jnp.int32(4)]
            for k in range(NB):
                rows, mass = from_table(table, b, k)
                acc = tuple(pair(goal[e], rows, mass, WIDE, acc[e]) for e in range(2))
                for order, count in zip(orders, counts):
                    order[count] = b * NB + k
                level = levall[b, k]
                counts = tuple(counts[e] + (level > e).astype(jnp.int32) for e in range(2))
                at = jnp.where(known[MATE, k] == b, k, 31)
                known[RANK, at] = jnp.where(level == 0, ranks[0], ranks[1])
                known[MATELEVEL, at] = level
                ranks = [ranks[e] + (level == e).astype(jnp.int32) for e in range(2)]
            return acc, counts

        start = ((zeros(), zeros()), (jnp.int32(0), jnp.int32(0)))
        acc, counts = lax.fori_loop(0, shards, group, start)
        for order, count in zip(orders, counts):
            for e in range(NB):
                order[count + e] = shards * NB
            order[(shards + 2) * NB] = count
        return acc

    tiles = slot_pairs(
        0, pairs_of(plan), state, plan, sweep,
        lambda p: None, close, corrector(0, state, plan, None),
        tuple(fill_tiles(masses, blank(2), 32)),
    )
    send(place_tiles(tiles), pay)


def ahead_sums(step, first, last, me, plan, order, predicted, state, sums):
    lane = lax.broadcasted_iota(jnp.int32, (8, 128), 1)

    def load(g, e):
        index = order[g * NB + e]
        return from_predicted(predicted, index >> SHIFT, index & (NB - 1))

    def close(s, e, part):
        rows, mass = from_predicted(predicted, plan[SHARD, 2 * s + part], plan[BLOCK, s])
        other = plan[SHARD, 2 * s + 1] != me if part else jnp.bool_(True)
        return rows, mass, other & (plan[HERE, 2 * s + part] == 0)

    def sink(s, total, inner, carry):
        tile = jnp.zeros((8, 128), F32)
        for at, group in ((0, total), (8, inner)):
            for c in range(6):
                tile = jnp.where(lane == at + c, group[c], tile)
        sums[s] = tile
        return carry

    groups = (order[order.shape[0] - NB] + NB - 1) // NB
    slot_pairs(first, last, state, plan, sweep_table(groups, load), lambda p: None, close, sink, 0)


def early_pairs(plan):
    return jnp.minimum(plan[COUNT, 2] // 2, 1)


def ahead_kernel(step, known, table, rates, order, state, *rest):
    if step == 1:
        sums, plan, predicted = rest
    elif step == 2:
        sums, plan, later, early, predicted, plan3 = rest
    else:
        early, sums, plan, predicted = rest
    me = known[ME, 0]
    lev = lambda k: known[OWN, k]
    fill_slots(lev, TOP[step], CAPS[step], plan)
    fill_near(plan, CAPS[step], known, SENT[step])
    fill_sources(table, rates, predicted, step * TICK)
    first = 0
    if step == 3:
        first = early_pairs(plan)
        sums[0:2] = early[...]
    ahead_sums(step, first, pairs_of(plan), me, plan, order, predicted, state, sums)
    if step == 2:
        fill_later(state, lev, later)
        fill_slots(lev, TOP[3], CAPS[3], plan3)
        fill_near(plan3, 2, known, SENT[3])
        fill_sources(table, rates, predicted, 3 * TICK)
        early[...] = jnp.zeros((2, 8, 128), F32)
        ahead_sums(3, 0, early_pairs(plan3), me, plan3, order, predicted, state, early)
    if step == 1:
        level = table[:, 7 * NB, :]
        lane = lax.broadcasted_iota(jnp.int32, level.shape, 1)
        one = jnp.where((level == 1.0) & (lane < NB), 1.0, 0.0).astype(F32)
        plan[COUNT, 1] = jnp.max(jnp.sum(one, axis=1, keepdims=True)).astype(jnp.int32)


def after_kernel(step, got, state_in, sums, plan, *rest):
    later = None
    used = SLOTS[step]
    if step > 1:
        masses, before, *rest = rest
        used = jnp.minimum(4 + before[COUNT, 1], used)
    if step == 2:
        later, *rest = rest
    if step == 3:
        state = state_in
    else:
        state, *rest = rest
    pay, *rest = rest
    if step == 1:
        masses, *rest = rest
    near, turned = rest
    if step < 3:
        state[...] = state_in[...]
    fill_received(got, turned)
    if step == 1:
        masses[0:4] = turned[24:28]
        masses[4:8] = turned[28:32]

    def close(s, e, part):
        rows, mass = tile_rows(lambda r: near[2 * e + part, r : r + 1, :])
        return rows, mass, plan[HERE, 2 * s + part] == 1

    tiles = slot_pairs(
        0, pairs_of(plan), state, plan,
        sweep_received(turned, masses, SLOTS[step], used),
        lambda p: gather_blocks(turned, masses, SLOTS[step], plan, near, p),
        close, corrector(step, state, plan, sums),
        tuple([later[t] for t in range(3)] if step == 2 else blank(9 if step == 3 else 3)),
    )
    send(place_tiles(tiles), pay)


def last_kernel(got, ps, fr, irr, plan, kin, comb, close):
    count = plan[COUNT, 0]
    kin[...] = ps[...]
    comb[...] = fr[...]
    close[...] = irr[...]
    senders = got.shape[0]
    lane = lax.broadcasted_iota(jnp.int32, (senders, 128), 1)
    row = lax.broadcasted_iota(jnp.int32, (senders, 128), 0)
    spread = [pltpu.roll(got[:, 0, pl.ds(t * 128, 128)], 0, 1, stride=8, stride_axis=0) for t in range(9)]
    place = lane - row * 8

    def slot(s, _):
        at = pl.ds(pl.multiple_of(plan[BLOCK, s] * BS, BS), BS)
        for f in range(18):
            t, e = divmod(f, 2)
            start = e * 64 + s * 8
            keep = (((place - start) & 127) >> 3) == 0
            value = jnp.sum(jnp.where(keep, spread[t], 0.0), axis=0, keepdims=True)
            out = (kin, comb, close)[f // 6]
            out[f % 6 : f % 6 + 1, at] = pltpu.roll(value, (128 - start) & 127, 1)
        return 0

    lax.fori_loop(0, count, slot, 0)


def body(phase_space, force_rates, irregular, stellar_masses, levels, active, partner):
    shards = lax.axis_size("blk")
    columns_ = lax.axis_size("grp")
    everyone = shards * columns_
    me = lax.axis_index("blk").astype(jnp.int32).reshape(1)
    col = lax.axis_index("grp").astype(jnp.int32).reshape(1)
    tiles = lambda count: pltpu.VMEM((count, 8, 128), F32)
    array = lambda *shape: jax.ShapeDtypeStruct(shape, F32)
    near = lambda *shape: pltpu.VMEM(shape, F32)
    here = lambda x: pltpu.with_memory_space_constraint(x, pltpu.VMEM)
    kept = lambda x: pltpu.with_memory_space_constraint(x, pltpu.SMEM)
    plan_shape = pltpu.SMEM((8, 32), jnp.int32)
    state_shape = near(NB + 1, 8, 128)

    def exchange(pay, axis):
        return lax.all_to_all(pay, axis, split_axis=0, concat_axis=0, tiled=True)

    packed, rates, mine = pl.pallas_call(
        pack_kernel,
        out_shape=(near(7 * NB + 8, BS), array(shards, 6 * NB, BS), near(NB, 16, BS)),
        in_specs=[VMEM, VMEM, VMEM, SMEM],
        out_specs=(VMEM, VMEM, VMEM),
        name="pack",
    )(phase_space, force_rates, stellar_masses[None, :], levels)
    table = lax.all_gather(packed, "blk", axis=0, tiled=False)
    levall = table[:, 7 * NB, :NB].astype(jnp.int32)
    table, rates = lax.optimization_barrier((table, rates))
    rates = exchange(rates, "blk")
    order_shape = pltpu.SMEM(((shards + 3) * NB,), jnp.int32)
    known_shape = pltpu.SMEM((8, 32), jnp.int32)
    state, pay, *orders, known = pl.pallas_call(
        first_kernel,
        out_shape=(state_shape, array(everyone * 2 // 8, 8, 128), order_shape, order_shape, known_shape),
        in_specs=[SMEM, SMEM, VMEM, VMEM, SMEM, SMEM, SMEM],
        out_specs=(VMEM, VMEM, SMEM, SMEM, SMEM),
        scratch_shapes=[pltpu.VMEM((NB, 128, 128), F32), pltpu.SMEM((8, 32), jnp.int32)],
        name="first",
    )(me, col, here(table), here(mine), levels, levall, partner)
    masses = before = None
    for step in (1, 2, 3):
        cap = CAPS[step]
        lanes = (0, 256, 384, 384)[step]
        got = exchange(pay.reshape(everyone, 1, lanes), ("blk", "grp"))
        ins = (kept(known), here(table), here(rates), kept(orders[SENT[step]]), here(state))
        specs = [SMEM, VMEM, VMEM, SMEM, VMEM]
        out_shape = (near(cap, 8, 128), plan_shape)
        out_specs = (VMEM, SMEM)
        scratch = [pltpu.VMEM((shards + 1, QUANTITIES, NB, BS), F32)]
        if step == 2:
            out_shape += (near(3, 8, 128), near(2, 8, 128))
            out_specs += (VMEM, VMEM)
            scratch += [pltpu.SMEM((8, 32), jnp.int32)]
        elif step == 3:
            ins += (here(early),)
            specs += [VMEM]
        outs = pl.pallas_call(
            functools.partial(ahead_kernel, step),
            out_shape=out_shape,
            in_specs=specs,
            out_specs=out_specs,
            scratch_shapes=scratch,
            name=f"ahead{step}",
        )(*ins)
        sums, plan = outs[:2]
        if step == 2:
            early = outs[3]
        ins = (here(got), here(state), here(sums), kept(plan))
        specs = [VMEM, VMEM, VMEM, SMEM]
        if step > 1:
            ins += (here(masses), kept(before))
            specs += [VMEM, SMEM]
        if step == 2:
            ins += (here(outs[2]),)
            specs += [VMEM]
        pay_shape = array(everyone * 3 // 8, 8, 128) if step < 3 else near(columns_, 1, 1152)
        out_shape = {
            1: (state_shape, pay_shape, near(8, 8, everyone)), 2: (state_shape, pay_shape), 3: (pay_shape,),
        }[step]
        outs = pl.pallas_call(
            functools.partial(after_kernel, step),
            out_shape=out_shape,
            in_specs=specs,
            out_specs=tuple(VMEM for _ in out_shape),
            scratch_shapes=[
                tiles(4),
                pltpu.VMEM((lanes // 8, 8, everyone), F32),
            ],
            name=f"after{step}",
        )(*ins)
        if step == 1:
            state, pay, masses = outs
            before = plan
        elif step == 2:
            state, pay = outs
        else:
            (pay,) = outs
    got = exchange(pay, "grp")
    shape = array(6, W)
    return tuple(
        pl.pallas_call(
            last_kernel,
            out_shape=(shape, shape, shape),
            in_specs=[VMEM, VMEM, VMEM, VMEM, SMEM],
            out_specs=(VMEM, VMEM, VMEM),
            name="last",
        )(here(got), here(phase_space), here(force_rates), here(irregular), kept(plan))
    )


def solution(mesh):
    in_specs = (
        P(None, "blk"), P(None, "blk"), P(None, "blk"), P("blk"), P("blk"), P(None, "blk"), P("blk"),
    )
    out_specs = (P(None, "blk"), P(None, "blk"), P(None, "blk"))
    return jax.shard_map(body, mesh=mesh, in_specs=in_specs, out_specs=out_specs, check_vma=False)
```
